32 devices in a mesh: dp: 8 (over z, x), shard: 4 (over y, core).
Axes of the slice: x: 2, y: 2, z: 4, core: 2. Of those that a mesh axis runs over, the one named last changes fastest.
Arguments:
- inputs: bfloat16 [2, 8, 512, 1024], P(None, 'dp', 'shard'), may hold values from -6 to 6
- segments: int32 [2, 8, 512], P(None, 'dp', 'shard'), may hold values from 0 to 7, never falling along the last dimension, each value on 1 to 256 neighbouring positions
- padding: int32 [2, 8, 512], P(None, 'dp', 'shard'), may hold values 0 or 1
- routes_value: int32 [2, 8, 512, 4, 2], P(None, 'dp', 'shard'), may hold values from 0 to 4, all different within a row
- routes_output: int32 [2, 8, 512, 4, 2], P(None, 'dp', 'shard'), may hold values from 0 to 4, all different within a row
- norm1_gain: bfloat16 [1024], P('shard'), may hold values from 0.5 to 1.5
- norm1_bias: bfloat16 [1024], P('shard'), may hold values from -1.25 to 1.25
- query_weight: bfloat16 [1024, 448], P('shard'), may hold values from -0.1875 to 0.1875
- key_weight: bfloat16 [1024, 448], P('shard'), may hold values from -0.1875 to 0.1875
- pos_weight: bfloat16 [1024, 448], P('shard'), may hold values from -0.1875 to 0.1875
- content_bias: bfloat16 [448], P('shard'), may hold values from -3 to 3
- pos_bias: bfloat16 [448], P('shard'), may hold values from -3 to 3
- value_router: bfloat16 [1024, 20], P('shard'), may hold values from -0.1875 to 0.1875
- output_router: bfloat16 [1024, 20], P('shard'), may hold values from -0.1875 to 0.1875
- value_experts: bfloat16 [1024, 2240], P('shard'), may hold values from -0.1875 to 0.1875
- output_experts: bfloat16 [2240, 1024], P('shard'), may hold values from -3 to 3
- norm2_gain: bfloat16 [1024], P('shard'), may hold values from 0.5 to 1.5
- norm2_bias: bfloat16 [1024], P('shard'), may hold values from -1.25 to 1.25
- ffn_in: bfloat16 [1024, 4096], P('shard'), may hold values from -0.1875 to 0.1875
- ffn_in_bias: bfloat16 [4096], P('shard'), may hold values from -1.75 to 1.75
- ffn_out: bfloat16 [4096, 1024], P('shard'), may hold values from -0.125 to 0.125
- ffn_out_bias: bfloat16 [1024], P('shard'), may hold values from -1.75 to 1.75
- cotangent: bfloat16 [2, 8, 512, 1024], P(None, 'dp', 'shard'), may hold values from -6 to 6
Outputs:
- output: bfloat16 [2, 8, 512, 1024], P(None, 'dp', 'shard')
- input_grad: float32 [2, 8, 512, 1024], P(None, 'dp', 'shard')
- norm1_gain_grad: float32 [1024], P('shard')
- norm1_bias_grad: float32 [1024], P('shard')
- query_weight_grad: float32 [1024, 448], P('shard')
- key_weight_grad: float32 [1024, 448], P('shard')
- pos_weight_grad: float32 [1024, 448], P('shard')
- content_bias_grad: float32 [448], P('shard')
- pos_bias_grad: float32 [448], P('shard')
- value_router_grad: float32 [1024, 20], P('shard')
- output_router_grad: float32 [1024, 20], P('shard')
- value_experts_grad: float32 [1024, 2240], P('shard')
- output_experts_grad: float32 [2240, 1024], P('shard')
- norm2_gain_grad: float32 [1024], P('shard')
- norm2_bias_grad: float32 [1024], P('shard')
- ffn_in_grad: float32 [1024, 4096], P('shard')
- ffn_in_bias_grad: float32 [4096], P('shard')
- ffn_out_grad: float32 [4096, 1024], P('shard')
- ffn_out_bias_grad: float32 [1024], P('shard')
The draws below stay inside these ranges and needn't reach their ends.
Inputs may be any that keep to these rules, and one draw needn't show every extreme that they name: `routes_value`: each token names 2 different value experts in each head. `routes_output`: each token names 2 different output experts in each head. `segments`: document numbers never fall along a sequence; a document has 1 to 256 tokens.
All inputs are finite; a program needn't handle non-finite values. No bound on the sum of `padding` on one device may be relied on, other than what follows from the above.
Results may differ from the reference program's by a relative error of at most 0.017.
Values may be sent and summed in bfloat16 or wider, within the bound.
No kernel may reach another device: no remote copies, remote signals or barrier semaphores. Data moves between devices by JAX's collectives and lax.ppermute only.
A program may use at most 192 MiB of HBM per device.

```python
import math
import jax
import jax.numpy as jnp
import numpy as np
from jax import lax

D = 1024
H = 4
DH = 112
E = 5
TOPK = 2
FF = 4096
Q_DEV = 128
MB = 2
SEQ = 512
BATCH = 8


def with_ends(values, own_key, low, top_value):
    shape = values.shape
    spot = [jax.random.randint(jax.random.fold_in(own_key, axis), (), 0, shape[axis]) for axis in range(len(shape))]
    values = values.at[tuple(spot)].set(low)
    longest = shape.index(max(shape))
    spot[longest] = (spot[longest] + 1) % shape[longest]
    return values.at[tuple(spot)].set(top_value)


def block_levels(key, dims, split, smallest, top_value):
    level = 1.0
    for axis_at, blocks in split:
        steps = jax.random.uniform(jax.random.fold_in(jax.random.fold_in(key, 6), axis_at), (blocks,), jnp.float32, smallest / len(split), top_value / len(split))
        level = level * jnp.repeat(jnp.exp(steps), dims[axis_at] // blocks).reshape((-1,) + (1,) * (len(dims) - 1 - axis_at))
    return level


def distinct(stream_key, rows, amount, top, lift):
    order = jax.random.permutation(jax.random.fold_in(stream_key, 1), amount)
    boost = order
    for power in range(3):
        boost = boost * boost // amount
    boost = boost * lift // amount
    chance = jax.random.randint(jax.random.fold_in(stream_key, 2), (rows, amount), 0, 4096) + boost
    holders = jax.random.permutation(jax.random.fold_in(stream_key, 3), rows)[jnp.arange(amount) % rows]
    chance = jnp.where(jnp.arange(rows)[:, None] == holders[None, :], 1 << 14, chance)
    score = chance * amount + jnp.arange(amount)
    return lax.top_k(score.astype(jnp.int32), top)[1].astype(jnp.int32)


def split_up(number_of, total, bound, slope):
    portions = [(1 << 20) // math.isqrt(rank ** slope) + 1 for rank in range(2, number_of + 1)]
    surplus, holding = total - bound - (number_of - 1), [1] * (number_of - 1)
    while surplus > 0:
        free = [i for i in range(number_of - 1) if holding[i] < bound]
        whole, left = sum([portions[i] for i in free]), surplus
        for i in free:
            extra = min(bound - holding[i], max(1, left * portions[i] // whole), surplus)
            holding[i] = holding[i] + extra
            surplus = surplus - extra
    return np.array([bound] + holding)


def ragged(rng, number_of, total, reach, skew):
    if number_of == 2:
        one = jax.random.randint(rng, (), max(1, total - reach), min(reach, total - 1) + 1)
        return jnp.stack([one, total - one])
    sizes = jnp.asarray(split_up(number_of, total, reach, skew), jnp.int32)
    twos = (number_of - 1) // 2
    source_of, sink = sizes[1:1 + 2 * twos:2], sizes[2:2 + 2 * twos:2]
    slack = jnp.minimum(source_of - 1, reach - sink)
    moved = jax.random.randint(jax.random.fold_in(rng, 1), (twos,), 0, 1 << 20) % (slack + 1)
    sizes = sizes.at[1:1 + 2 * twos:2].set(source_of - moved).at[2:2 + 2 * twos:2].set(sink + moved)
    return sizes[jax.random.permutation(jax.random.fold_in(rng, 2), number_of)]


def scatter_about(own_key, shape, scale, reach, split=(), kind=jnp.bfloat16):
    factor_of = block_levels(own_key, shape, split, -0.22, 0.18) if split else 1.0
    array = jax.random.normal(own_key, shape, jnp.float32) * scale * factor_of
    return jnp.minimum(jnp.maximum(array, -reach), reach).astype(kind)


def setup_inputs(seed: int = 0) -> dict:
    arg_keys = jax.random.split(jax.random.key(seed), 24)
    return {
        "inputs": scatter_about(arg_keys[0], (MB, BATCH, SEQ, D), 1.0, 6.0, ((1, 8), (2, 4))),
        "segments": jax.vmap(lambda own: jnp.searchsorted(jnp.cumsum(ragged(own, 8, SEQ, SEQ // 2, 2)), jnp.arange(SEQ), side="right"))(jax.random.split(arg_keys[1], MB * BATCH)).reshape((MB, BATCH, SEQ)).astype(jnp.int32),
        "padding": with_ends((jax.random.randint(arg_keys[2], (MB, BATCH, SEQ), 0, 8) < 7).astype(jnp.int32), jax.random.fold_in(arg_keys[2], 1), 0, 1),
        "routes_value": distinct(arg_keys[3], MB * BATCH * SEQ * H, E, TOPK, 3276).reshape((MB, BATCH, SEQ, H, TOPK)),
        "routes_output": distinct(arg_keys[4], MB * BATCH * SEQ * H, E, TOPK, 3276).reshape((MB, BATCH, SEQ, H, TOPK)),
        "norm1_gain": jnp.clip(1.0 + 0.1 * jax.random.normal(arg_keys[5], (D,), jnp.float32), 0.5, 1.5).astype(jnp.bfloat16),
        "norm1_bias": scatter_about(arg_keys[6], (D,), 0.2, 1.25, ((0, 4),)),
        "query_weight": scatter_about(arg_keys[7], (D, H * DH), D ** -0.5, 0.1875, ((0, 4),)),
        "key_weight": scatter_about(arg_keys[8], (D, H * DH), D ** -0.5, 0.1875, ((0, 4),)),
        "pos_weight": scatter_about(arg_keys[9], (D, H * DH), D ** -0.5, 0.1875, ((0, 4),)),
        "content_bias": scatter_about(arg_keys[10], (H * DH,), 0.5, 3.0, ((0, 4),)),
        "pos_bias": scatter_about(arg_keys[11], (H * DH,), 0.5, 3.0, ((0, 4),)),
        "value_router": scatter_about(arg_keys[12], (D, H * E), D ** -0.5, 0.1875, ((0, 4),)),
        "output_router": scatter_about(arg_keys[13], (D, H * E), D ** -0.5, 0.1875, ((0, 4),)),
        "value_experts": scatter_about(arg_keys[14], (D, H * E * DH), D ** -0.5, 0.1875, ((0, 4),)),
        "output_experts": scatter_about(arg_keys[15], (H * E * DH, D), 4 ** -0.5, 3.0, ((0, 4),)),
        "norm2_gain": jnp.clip(1.0 + 0.1 * jax.random.normal(arg_keys[16], (D,), jnp.float32), 0.5, 1.5).astype(jnp.bfloat16),
        "norm2_bias": scatter_about(arg_keys[17], (D,), 0.2, 1.25, ((0, 4),)),
        "ffn_in": scatter_about(arg_keys[18], (D, FF), D ** -0.5, 0.1875, ((0, 4),)),
        "ffn_in_bias": scatter_about(arg_keys[19], (FF,), 0.3, 1.75, ((0, 4),)),
        "ffn_out": scatter_about(arg_keys[20], (FF, D), (FF // 2) ** -0.5, 0.125, ((0, 4),)),
        "ffn_out_bias": scatter_about(arg_keys[21], (D,), 0.3, 1.75, ((0, 4),)),
        "cotangent": scatter_about(arg_keys[22], (MB, BATCH, SEQ, D), 1.0, 6.0, ((1, 8), (2, 4))),
    }


@jax.custom_vjp
def low(v):
    return lax.optimization_barrier(v.astype(jnp.bfloat16)).astype(jnp.float32)

@jax.custom_vjp
def low_back(v):
    return v

def low_keep(v):
    return (low(v), None)

def low_pass(kept, grad):
    return (grad,)

def back_keep(v):
    return (v, None)

def back_low(kept, grad):
    return (low(grad),)
low.defvjp(low_keep, low_pass)
low_back.defvjp(back_keep, back_low)
highest = lax.Precision.HIGHEST

def float_dot(left, right):
    return jnp.dot(left, right, precision=highest)

def layer_norm(values, gain_vec, shift_vec):
    row_mean = lax.optimization_barrier(jnp.mean(values, axis=-1, keepdims=True))
    centred = values - row_mean
    spread = lax.optimization_barrier(jnp.mean(centred * centred, axis=-1, keepdims=True))
    return centred * lax.rsqrt(spread + 1e-05) * gain_vec + shift_vec

def sinusoid(length, feature_count):
    distance = (length - 1 - jnp.arange(length, dtype=jnp.int32)).astype(jnp.float32)
    inv_freq = jnp.exp(jnp.arange(0, feature_count, 2, dtype=jnp.int32).astype(jnp.float32) * (-math.log(10000.0) / feature_count))
    angles = distance[:, None] * inv_freq[None, :]
    return jnp.concatenate([jnp.sin(angles), jnp.cos(angles)], axis=1)

def shift_rows(pos_table, row_count, key_count):
    head_count = pos_table.shape[0]
    flattened = pos_table.reshape(head_count, row_count * (row_count + key_count))
    kept_part = lax.slice_in_dim(flattened, row_count - 1, row_count - 1 + row_count * (row_count + key_count - 1), axis=1)
    return kept_part.reshape(head_count, row_count, row_count + key_count - 1)[:, :, :key_count]

def pick_experts(routes):
    return (routes[..., None] == jnp.arange(E, dtype=jnp.int32)).astype(jnp.float32).sum(axis=-2)

def allowed_mask(seg_query, seg_key, pad_key, row_start, key_count):
    query_pos = row_start + jnp.arange(seg_query.shape[0], dtype=jnp.int32)
    key_pos = jnp.arange(key_count, dtype=jnp.int32)
    same_doc = seg_query[:, None] == seg_key[None, :]
    causal = key_pos[None, :] <= query_pos[:, None]
    live_key = (pad_key[None, :] > 0) | (key_pos[None, :] == query_pos[:, None])
    return same_doc & causal & live_key

def attend_block(query_cont, query_posn, keys, values, pos_desc, seg_ids, pad_ids, block_idx):
    length = keys.shape[0]
    row_start = block_idx * Q_DEV
    window = lax.dynamic_slice_in_dim(pos_desc, length - row_start - Q_DEV, Q_DEV + length, 0)
    cont_block = lax.dynamic_slice_in_dim(query_cont, row_start, Q_DEV, 0)
    posn_block = lax.dynamic_slice_in_dim(query_posn, row_start, Q_DEV, 0)
    seg_query = lax.dynamic_slice_in_dim(seg_ids, row_start, Q_DEV, 0)
    allowed = allowed_mask(seg_query, seg_ids, pad_ids, row_start, length)
    content = jnp.einsum('qhd,khd->hqk', cont_block, keys, precision=highest)
    pos_table = jnp.einsum('qhd,khd->hqk', posn_block, window, precision=highest)
    scores = low_back(content + shift_rows(pos_table, Q_DEV, length))
    scores = jnp.where(allowed[None], scores, -1e+30)
    prob_low = low(jax.nn.softmax(scores, axis=-1))
    return jnp.einsum('hqk,khd->qhd', prob_low, values, precision=highest)

def forward(weights, tokens, seg_ids, pad_ids, pick_value, pick_output, sine_table):
    gain_one, bias_one, query_w, key_w, pos_w, content_b, pos_b, value_r, output_r, value_w, output_w, gain_two, bias_two, inner_w, inner_b, outer_w, outer_b = weights
    length = tokens.shape[0]
    query_scale = DH ** (-0.5)
    normed = low(layer_norm(tokens, gain_one, bias_one))
    query_raw = low_back(float_dot(normed, query_w)).reshape(length, H, DH)
    query_cont = low((query_raw + content_b.reshape(H, DH)) * query_scale)
    query_posn = low((query_raw + pos_b.reshape(H, DH)) * query_scale)
    keys = low(low_back(float_dot(normed, key_w))).reshape(length, H, DH)
    value_gate = jax.nn.sigmoid(float_dot(normed, value_r)).reshape(length, H, E) * pick_value
    value_all = low_back(float_dot(normed, value_w)).reshape(length, H, E, DH)
    values = low(low_back(lax.optimization_barrier(jnp.sum(value_all * value_gate[..., None], axis=2))))
    pos_top = low(float_dot(sine_table, pos_w))
    pos_desc = jnp.concatenate([pos_top, jnp.zeros_like(pos_top)], axis=0).reshape(2 * length, H, DH)
    checked = jax.checkpoint(attend_block)
    attended = lax.map(lambda block_idx: checked(query_cont, query_posn, keys, values, pos_desc, seg_ids, pad_ids, block_idx), jnp.arange(length // Q_DEV, dtype=jnp.int32))
    attended = low_back(attended.reshape(length, H, DH))
    output_gate = jax.nn.sigmoid(float_dot(normed, output_r)).reshape(length, H, E) * pick_output
    mixed_heads = low(attended[:, :, None, :] * output_gate[..., None]).reshape(length, H * E * DH)
    branch = low_back(float_dot(mixed_heads, output_w))
    residual = tokens + branch
    normed_two = low(layer_norm(residual, gain_two, bias_two))
    pre_act = low_back(float_dot(normed_two, inner_w) + inner_b)
    hidden = low(jax.nn.gelu(pre_act, approximate=False))
    return residual + float_dot(hidden, outer_w) + outer_b

def reference(inputs, segments, padding, routes_value, routes_output, norm1_gain, norm1_bias, query_weight, key_weight, pos_weight, content_bias, pos_bias, value_router, output_router, value_experts, output_experts, norm2_gain, norm2_bias, ffn_in, ffn_in_bias, ffn_out, ffn_out_bias, cotangent):
    weights = tuple((weight.astype(jnp.float32) for weight in (norm1_gain, norm1_bias, query_weight, key_weight, pos_weight, content_bias, pos_bias, value_router, output_router, value_experts, output_experts, norm2_gain, norm2_bias, ffn_in, ffn_in_bias, ffn_out, ffn_out_bias)))
    micro_count = inputs.shape[0]
    batch_count = inputs.shape[1]
    length = inputs.shape[2]
    seq_total = micro_count * batch_count
    sine_table = low(sinusoid(length, D))
    seq_items = (inputs.reshape(seq_total, length, D), cotangent.reshape(seq_total, length, D), segments.reshape(seq_total, length), padding.reshape(seq_total, length), routes_value.reshape(seq_total, length, H, TOPK), routes_output.reshape(seq_total, length, H, TOPK))

    def scan_step(totals, seq_item):
        tokens, grad_out, seg_ids, pad_ids, route_value, route_output = seq_item
        pick_value = pick_experts(route_value)
        pick_output = pick_experts(route_output)

        def run_forward(layer_weights, layer_input):
            return forward(layer_weights, layer_input, seg_ids, pad_ids, pick_value, pick_output, sine_table)
        result, pullback = jax.vjp(run_forward, weights, tokens.astype(jnp.float32))
        weight_grads, token_grad = pullback(grad_out.astype(jnp.float32))
        totals = tuple((old_sum + new_term for old_sum, new_term in zip(totals, weight_grads)))
        return (totals, (result.astype(jnp.bfloat16), token_grad))
    zero_grads = tuple((jnp.zeros_like(weight) for weight in weights))
    totals, (results, token_grads) = lax.scan(scan_step, zero_grads, seq_items)
    return (results.reshape(inputs.shape), token_grads.reshape(inputs.shape), totals[0], totals[1], totals[2], totals[3], totals[4], totals[5], totals[6], totals[7], totals[8], totals[9], totals[10], totals[11], totals[12], totals[13], totals[14], totals[15], totals[16])
```

```python
import functools
import math

import jax
import jax.numpy as jnp
from jax import lax
from jax.experimental import pallas as pl
from jax.experimental.pallas import tpu as pltpu
from jax.sharding import PartitionSpec as P

D = 1024
H = 4
DH = 112
E = 5
FF = 4096
LANE = 128
PACK = 1024
BLK = 128
MASKED = -1e30
SCALE = DH ** (-0.5)
bf16 = jnp.bfloat16
f32 = jnp.float32
NN = (((1,), (0,)), ((), ()))
NT = (((1,), (1,)), ((), ()))
TN = (((0,), (0,)), ((), ()))


def mm(a, b, dims=NN):
    return lax.dot_general(a, b, dims, preferred_element_type=f32)


def call(kernel, outs, args, scratch=(), flops=0, smem=0, vmem=48):
    in_specs = [pl.BlockSpec(memory_space=pltpu.SMEM)] * smem + [
        pl.BlockSpec(memory_space=pltpu.VMEM)
    ] * (len(args) - smem)
    moved = sum(math.prod(a.shape) * a.dtype.itemsize for a in args)
    moved += sum(math.prod(o.shape) * o.dtype.itemsize for o in outs)
    return pl.pallas_call(
        kernel,
        out_shape=outs,
        in_specs=in_specs,
        out_specs=[pl.BlockSpec(memory_space=pltpu.VMEM)] * len(outs),
        scratch_shapes=list(scratch),
        compiler_params=pltpu.CompilerParams(vmem_limit_bytes=vmem << 20),
        cost_estimate=pl.CostEstimate(flops=flops, bytes_accessed=moved, transcendentals=0),
    )(*args)


def out(shape, dtype):
    return jax.ShapeDtypeStruct(shape, dtype)


def selector(rows, first, count, place):
    row = lax.broadcasted_iota(jnp.int32, (rows, LANE), 0)
    col = lax.broadcasted_iota(jnp.int32, (rows, LANE), 1)
    hit = (row - first == col - place) & (col >= place) & (col < place + count)
    return jnp.where(hit, 1.0, 0.0).astype(bf16)


def pack_kernel(q_ref, k_ref, p_ref, rv_ref, ro_ref, v_ref, out_ref):
    for h in range(H):
        head = selector(H * DH, DH * h, DH, 0)
        block = mm(q_ref[...], head)
        block += mm(rv_ref[...], selector(H * E, E * h, E, DH))
        block += mm(ro_ref[...], selector(H * E, E * h, E, DH + E))
        out_ref[h, :, 0:LANE] = block.astype(bf16)
        out_ref[h, :, LANE : 2 * LANE] = mm(k_ref[...], head).astype(bf16)
        out_ref[h, :, 2 * LANE : 3 * LANE] = mm(p_ref[...], head).astype(bf16)
        for e in range(E):
            first = DH * (E * h + e)
            low = first // LANE * LANE
            wide = min(2 * LANE, H * E * DH - low)
            part = mm(v_ref[:, low : low + wide], selector(wide, first - low, DH, 0))
            out_ref[h, :, (3 + e) * LANE : (4 + e) * LANE] = part.astype(bf16)


def unpack_kernel(g_ref, q_ref, k_ref, p_ref, rv_ref, ro_ref, v_ref):
    def spread(value, rows, first, count, place):
        return mm(value, selector(rows, first, count, place), NT)

    def total(terms):
        return functools.reduce(lambda a, b: a + b, terms)

    first_block = [g_ref[h, :, 0:LANE] for h in range(H)]
    q_ref[...] = total(spread(first_block[h], H * DH, DH * h, DH, 0) for h in range(H))
    rv_ref[...] = total(spread(first_block[h], H * E, E * h, E, DH) for h in range(H))
    ro_ref[...] = total(spread(first_block[h], H * E, E * h, E, DH + E) for h in range(H))
    k_ref[...] = total(
        spread(g_ref[h, :, LANE : 2 * LANE], H * DH, DH * h, DH, 0) for h in range(H)
    )
    p_ref[...] = total(
        spread(g_ref[h, :, 2 * LANE : 3 * LANE], H * DH, DH * h, DH, 0) for h in range(H)
    )
    width = H * E * DH
    for low in range(0, width, LANE):
        wide = min(LANE, width - low)
        terms = []
        for head in range(H * E):
            first = DH * head
            if first < low + wide and first + DH > low:
                h, e = divmod(head, E)
                row = lax.broadcasted_iota(jnp.int32, (LANE, wide), 0)
                col = lax.broadcasted_iota(jnp.int32, (LANE, wide), 1)
                hit = (col + low - first == row) & (row < DH)
                pick = jnp.where(hit, 1.0, 0.0).astype(bf16)
                terms.append(mm(g_ref[h, :, (3 + e) * LANE : (4 + e) * LANE], pick))
        v_ref[:, low : low + wide] = total(terms)


def norm_stats(x):
    mean = jnp.mean(x, axis=-1, keepdims=True)
    centred = x - mean
    var = jnp.mean(centred * centred, axis=-1, keepdims=True)
    rstd = lax.rsqrt(var + 1e-05)
    return centred * rstd, rstd


def norm_back(grad, unit, rstd, gain):
    g = grad * gain
    return rstd * (
        g
        - jnp.mean(g, axis=-1, keepdims=True)
        - unit * jnp.mean(g * unit, axis=-1, keepdims=True)
    )


def attention_kernel(
    x_ref,
    vec_ref,
    head_ref,
    rows_ref,
    w_ref,
    pos_ref,
    wo_ref,
    n_ref,
    qc_ref,
    qp_ref,
    k_ref,
    v_ref,
    va_ref,
    gate_ref,
    p_ref,
    att_ref,
    mix_ref,
    part_ref,
):
    length = x_ref.shape[0]
    blocks = length // BLK

    @pl.loop(0, blocks)
    def _(b):
        rows = pl.ds(pl.multiple_of(b * BLK, BLK), BLK)
        unit, _ = norm_stats(x_ref[rows, :].astype(f32))
        n_ref[rows, :] = (unit * vec_ref[0:1, :] + vec_ref[1:2, :]).astype(bf16)

    lane = lax.broadcasted_iota(jnp.int32, (1, LANE), 1)
    first = mm(n_ref[...], w_ref[:, 0:LANE])
    columns = rows_ref[...].T
    code = columns[:, 0:1].astype(jnp.int32)
    slot = jnp.where((lane >= DH) & (lane < DH + 2 * E), lane - DH, 31)
    pick = (lax.shift_right_logical(jnp.broadcast_to(code, (length, LANE)), jnp.broadcast_to(slot, (length, LANE))) & 1) == 1
    gate = jnp.where(pick, 1.0 / (1.0 + jnp.exp(-first)), 0.0)
    gate_ref[...] = gate
    is_head = lane < DH
    qc_ref[...] = jnp.where(is_head, (first + head_ref[0:1, :]) * SCALE, 0.0).astype(bf16)
    qp_ref[...] = jnp.where(is_head, (first + head_ref[1:2, :]) * SCALE, 0.0).astype(bf16)
    k_ref[...] = mm(n_ref[...], w_ref[:, LANE : 2 * LANE]).astype(bf16)
    values = jnp.zeros((length, LANE), f32)
    for e in range(E):
        part = mm(n_ref[...], w_ref[:, (3 + e) * LANE : (4 + e) * LANE])
        va_ref[:, e * LANE : (e + 1) * LANE] = part
        values += part * gate[:, DH + e : DH + e + 1]
    v_ref[...] = values.astype(bf16)
    seg_col = columns[:, 1:2]
    for b in range(blocks):
        rows = slice(b * BLK, (b + 1) * BLK)
        wide = (b + 1) * BLK
        content = mm(qc_ref[rows, :], k_ref[0:wide, :], NT)
        table = mm(qp_ref[rows, :], pos_ref[length - wide : length, :], NT)
        table = pltpu.roll(table, (wide - BLK + 1) % wide, 1, stride=1, stride_axis=0)
        row = lax.broadcasted_iota(jnp.int32, (BLK, wide), 0) + b * BLK
        col = lax.broadcasted_iota(jnp.int32, (BLK, wide), 1)
        same = seg_col[rows, :] == rows_ref[1:2, 0:wide]
        live = ((rows_ref[2:3, 0:wide] > 0.0) & (col < row)) | (col == row)
        scores = jnp.where(same & live, content + table, MASKED)
        top = jnp.max(scores, axis=-1, keepdims=True)
        expo = jnp.exp(scores - top)
        prob = expo / jnp.sum(expo, axis=-1, keepdims=True)
        p_ref[rows, 0:wide] = prob
        att = mm(prob.astype(bf16), v_ref[0:wide, :])
        att_ref[rows, :] = att
        for e in range(E):
            share = gate_ref[rows, DH + E + e : DH + E + e + 1]
            mix_ref[rows, e * LANE : (e + 1) * LANE] = (att * share).astype(bf16)
    part_ref[...] = mm(mix_ref[...], wo_ref[...]).astype(bf16)


def normal_terms(v):
    bell = jnp.exp(-0.5 * v * v)
    phi = 0.5 * (1.0 + lax.erf(v * (1.0 / math.sqrt(2.0))))
    return phi, bell * (1.0 / math.sqrt(2.0 * math.pi))


def ffn_kernel(
    x_ref, tot_ref, vec_ref, win_ref, bin_ref, wout_ref, cot_ref, n_ref, hid_ref, gp_ref, gn_ref
):
    length = x_ref.shape[0]

    @pl.loop(0, length // BLK)
    def _(b):
        rows = pl.ds(pl.multiple_of(b * BLK, BLK), BLK)
        unit, _ = norm_stats(x_ref[rows, :].astype(f32) + tot_ref[rows, :].astype(f32))
        n_ref[rows, :] = (unit * vec_ref[2:3, :] + vec_ref[3:4, :]).astype(bf16)

    width = 256

    @pl.loop(0, win_ref.shape[1] // width)
    def _(c):
        cols = pl.ds(pl.multiple_of(c * width, width), width)
        pre = mm(n_ref[...], win_ref[:, cols]) + bin_ref[0:1, cols]
        back = mm(cot_ref[...], wout_ref[cols, :], NT)
        phi, density = normal_terms(pre)
        hid_ref[:, cols] = (pre * phi).astype(bf16)
        gp_ref[:, cols] = (back * (phi + pre * density)).astype(bf16)

    gn_ref[...] = mm(gp_ref[...], win_ref[...], NT).astype(bf16)


def back_kernel(
    x_ref,
    tot_ref,
    gn2_ref,
    cot_ref,
    vec_ref,
    w_ref,
    wo_ref,
    pos_ref,
    qc_ref,
    qp_ref,
    k_ref,
    v_ref,
    va_ref,
    gate_ref,
    p_ref,
    att_ref,
    gb_ref,
    sums_ref,
    dproj_ref,
    gpos_ref,
    bias_ref,
    part_ref,
    ga_ref,
    gk_ref,
    gv_ref,
    logit_ref,
):
    length = x_ref.shape[0]
    blocks = length // BLK
    sums_ref[...] = jnp.zeros(sums_ref.shape, f32)

    @pl.loop(0, blocks)
    def _(b):
        rows = pl.ds(pl.multiple_of(b * BLK, BLK), BLK)
        unit, rstd = norm_stats(x_ref[rows, :].astype(f32) + tot_ref[rows, :].astype(f32))
        grad = gn2_ref[rows, :].astype(f32)
        sums_ref[0:1, :] += jnp.sum(grad * unit, axis=0, keepdims=True)
        sums_ref[1:2, :] += jnp.sum(grad, axis=0, keepdims=True)
        cot = cot_ref[rows, :].astype(f32)
        sums_ref[2:3, :] += jnp.sum(cot, axis=0, keepdims=True)
        gb_ref[rows, :] = (cot + norm_back(grad, unit, rstd, vec_ref[2:3, :])).astype(bf16)

    lane = lax.broadcasted_iota(jnp.int32, (1, LANE), 1)
    acc = jnp.zeros((length, LANE), f32)
    logits = jnp.zeros((length, LANE), f32)
    for e in range(E):
        mixed = mm(gb_ref[...], wo_ref[e * LANE : (e + 1) * LANE, :], NT)
        acc += mixed * gate_ref[:, DH + E + e : DH + E + e + 1]
        dot = jnp.sum(mixed * att_ref[...], axis=-1, keepdims=True)
        logits = jnp.where(lane == DH + E + e, dot, logits)
    ga_ref[...] = acc.astype(bf16)
    logit_ref[...] = logits
    gk_ref[...] = jnp.zeros(gk_ref.shape, f32)
    gv_ref[...] = jnp.zeros(gv_ref.shape, f32)
    gpos_ref[...] = jnp.zeros(gpos_ref.shape, f32)
    row = lax.broadcasted_iota(jnp.int32, (BLK, BLK), 0)
    col = lax.broadcasted_iota(jnp.int32, (BLK, BLK), 1)
    mirror = jnp.where(row + col == BLK - 1, 1.0, 0.0).astype(bf16)
    cont_sum = jnp.zeros((1, LANE), f32)
    posn_sum = jnp.zeros((1, LANE), f32)
    for b in range(blocks):
        rows = slice(b * BLK, (b + 1) * BLK)
        wide = (b + 1) * BLK
        prob = p_ref[rows, 0:wide]
        ga = ga_ref[rows, :]
        grad_prob = mm(ga, v_ref[0:wide, :], NT)
        delta = jnp.sum(prob * grad_prob, axis=-1, keepdims=True)
        grad_score = (prob * (grad_prob - delta)).astype(bf16)
        gv_ref[0:wide, :] += mm(prob.astype(bf16), ga, TN)
        gk_ref[0:wide, :] += mm(grad_score, qc_ref[rows, :], TN)
        cont = mm(grad_score, k_ref[0:wide, :]) * SCALE
        table = pltpu.roll(mm(mirror, grad_score), 0, 1, stride=1, stride_axis=0)
        table = mm(mirror, table.astype(bf16)).astype(bf16)
        posn = mm(table, pos_ref[length - wide : length, :]) * SCALE
        gpos_ref[length - wide : length, :] += mm(table, qp_ref[rows, :], TN)
        cont_sum += jnp.sum(cont, axis=0, keepdims=True)
        posn_sum += jnp.sum(posn, axis=0, keepdims=True)
        dproj_ref[rows, 0:LANE] = (cont + posn).astype(bf16)
    bias_ref[0:1, :] = cont_sum
    bias_ref[1:2, :] = posn_sum
    dproj_ref[:, LANE : 2 * LANE] = gk_ref[...].astype(bf16)
    dproj_ref[:, 2 * LANE : 3 * LANE] = jnp.zeros((length, LANE), bf16)
    grad_values = gv_ref[...].astype(bf16).astype(f32)
    logits = logit_ref[...]
    for e in range(E):
        cols = slice((3 + e) * LANE, (4 + e) * LANE)
        dproj_ref[:, cols] = (grad_values * gate_ref[:, DH + e : DH + e + 1]).astype(bf16)
        dot = jnp.sum(
            grad_values * va_ref[:, e * LANE : (e + 1) * LANE], axis=-1, keepdims=True
        )
        logits = jnp.where(lane == DH + e, dot, logits)
    gate = gate_ref[...]
    logits = logits * gate * (1.0 - gate)
    dproj_ref[:, 0:LANE] = jnp.where(
        lane < DH, dproj_ref[:, 0:LANE].astype(f32), logits
    ).astype(bf16)
    part_ref[...] = mm(dproj_ref[...], w_ref[...], NT).astype(bf16)


def output_kernel(x_ref, tot_ref, mine_ref, other_ref, vec_ref, y_ref):
    residual = x_ref[...].astype(f32) + tot_ref[...].astype(f32)
    y_ref[...] = (
        residual + mine_ref[...].astype(f32) + other_ref[...].astype(f32) + vec_ref[4:5, :]
    ).astype(bf16)


def input_kernel(x_ref, tot_ref, gn2_ref, cot_ref, mine_ref, other_ref, vec_ref, y_ref, sums_ref):
    x = x_ref[...].astype(f32)
    unit, rstd = norm_stats(x + tot_ref[...].astype(f32))
    grad = cot_ref[...].astype(f32)
    grad = grad + norm_back(gn2_ref[...].astype(f32), unit, rstd, vec_ref[2:3, :])
    unit, rstd = norm_stats(x)
    back = mine_ref[...].astype(f32) + other_ref[...].astype(f32)
    y_ref[...] = grad + norm_back(back, unit, rstd, vec_ref[0:1, :])
    sums_ref[0:1, :] = jnp.sum(back * unit, axis=0, keepdims=True)
    sums_ref[1:2, :] = jnp.sum(back, axis=0, keepdims=True)


def flip_shard(value, bit):
    return lax.ppermute(value, "shard", [(s, s ^ bit) for s in range(H)])


def flip_dp(value, bit):
    count = lax.axis_size("dp")
    return lax.ppermute(value, "dp", [(d, d ^ bit) for d in range(count)])


def take(value, at, size, axis=0):
    return lax.dynamic_slice_in_dim(value, at, size, axis)


def gather_shard(own, rank):
    across = flip_shard(own, 2)
    beside = flip_shard(jnp.stack([own, across]), 1)
    full = jnp.zeros((H,) + own.shape, own.dtype)
    for relative, block in ((0, own), (2, across), (1, beside[0]), (3, beside[1])):
        full = lax.dynamic_update_slice_in_dim(full, block[None], rank ^ relative, 0)
    return full


def swap_shard(blocks, rank):
    full = jnp.zeros(blocks.shape, blocks.dtype)
    for relative in range(H):
        block = take(blocks, rank ^ relative, 1)
        if relative:
            block = flip_shard(block, relative)
        full = lax.dynamic_update_slice_in_dim(full, block, rank ^ relative, 0)
    return full


def sum_rows(part, core):
    half = part.shape[0] // 2
    got = flip_shard(take(part, (1 - core) * half, half), 1)
    chip = (take(part, core * half, half).astype(f32) + got.astype(f32)).astype(bf16)
    other = flip_shard(chip, 2)
    mine = (chip.astype(f32) + other.astype(f32)).astype(bf16)
    theirs = flip_shard(mine, 1)
    full = jnp.zeros(part.shape, bf16)
    full = lax.dynamic_update_slice_in_dim(full, mine, core * half, 0)
    return lax.dynamic_update_slice_in_dim(full, theirs, (1 - core) * half, 0)


def scatter_rows(part, rank):
    size = part.shape[0] // H
    blocks = part.reshape((H, size) + part.shape[1:])
    send = jnp.concatenate([take(blocks, rank ^ 1, 1), take(blocks, rank ^ 3, 1)])
    got = flip_shard(send, 1)
    mine = take(blocks, rank, 1)[0].astype(f32) + got[0].astype(f32)
    far = (take(blocks, rank ^ 2, 1)[0].astype(f32) + got[1].astype(f32)).astype(bf16)
    return mine.astype(bf16), flip_shard(far, 2)


def reduce_dp(grad, order, dp_rank):
    at = 0
    for bit in order:
        half = grad.shape[1] // 2
        side = (dp_rank >> bit) & 1
        send = take(grad, (1 - side) * half, half, 1).astype(bf16)
        got = flip_dp(send, 1 << bit)
        grad = take(grad, side * half, half, 1) + got.astype(f32)
        at = at + side * half
    return grad


def gather_dp(piece, order, dp_rank):
    for bit in reversed(order):
        side = (dp_rank >> bit) & 1
        got = flip_dp(piece, 1 << bit)
        half = piece.shape[1]
        full = jnp.zeros((piece.shape[0], 2 * half) + piece.shape[2:], piece.dtype)
        full = lax.dynamic_update_slice_in_dim(full, piece, side * half, 1)
        piece = lax.dynamic_update_slice_in_dim(full, got, (1 - side) * half, 1)
    return piece


def sum_dp_small(value, order):
    for bit in order:
        value = value + flip_dp(value, 1 << bit)
    return value


def sinusoid(length, feature_count):
    distance = (length - 1 - jnp.arange(length, dtype=jnp.int32)).astype(f32)
    inv_freq = jnp.exp(
        jnp.arange(0, feature_count, 2, dtype=jnp.int32).astype(f32)
        * (-math.log(10000.0) / feature_count)
    )
    angles = distance[:, None] * inv_freq[None, :]
    return jnp.concatenate([jnp.sin(angles), jnp.cos(angles)], axis=1)


def expert_codes(routes, weight):
    picked = (routes[..., None] == jnp.arange(E, dtype=jnp.int32)).astype(f32).sum(axis=-2)
    return (picked * (weight * 2.0 ** jnp.arange(E))).sum(axis=-1)


def local(
    inputs,
    segments,
    padding,
    routes_value,
    routes_output,
    norm1_gain,
    norm1_bias,
    query_weight,
    key_weight,
    pos_weight,
    content_bias,
    pos_bias,
    value_router,
    output_router,
    value_experts,
    output_experts,
    norm2_gain,
    norm2_bias,
    ffn_in,
    ffn_in_bias,
    ffn_out,
    ffn_out_bias,
    cotangent,
):
    micro = inputs.shape[0]
    own = inputs.shape[2]
    length = own * H
    rank = lax.axis_index("shard")
    core = rank & 1
    dp_rank = lax.axis_index("dp")
    dp_count = lax.axis_size("dp")
    order = list(range(dp_count.bit_length() - 1))
    quarter = D // H

    codes = [
        jnp.transpose(expert_codes(r[:, 0], 1.0), (2, 0, 1)).reshape(H, micro * own)
        for r in (routes_value, routes_output)
    ]
    marks = [segments[:, 0].reshape(1, -1), padding[:, 0].reshape(1, -1)]
    vectors = [norm1_gain, norm1_bias, norm2_gain, norm2_bias, ffn_out_bias]
    meta = jnp.concatenate(
        [c.astype(bf16) for c in codes]
        + [m.astype(bf16) for m in marks]
        + [v.reshape(1, quarter) for v in vectors]
        + [jnp.zeros((1, quarter), bf16)],
        axis=0,
    )
    meta_all = gather_shard(meta, rank).astype(f32)
    tokens = meta_all[:, :10].reshape(H, 10, micro, own).transpose(2, 1, 0, 3)
    tokens = tokens.reshape(micro, 10, length)
    vec = meta_all[:, 10:].transpose(1, 0, 2).reshape(6, D)
    vec = jnp.concatenate([vec, jnp.zeros((2, D), f32)])
    code = take(tokens, rank, 1, 1) + 2.0**E * take(tokens, rank + H, 1, 1)
    rows = jnp.concatenate([code, tokens[:, 8:10], jnp.zeros((micro, 5, length), f32)], axis=1)
    head = jnp.pad(jnp.stack([content_bias, pos_bias]).astype(f32), ((0, 6), (0, LANE - DH)))

    packed = call(
        pack_kernel,
        [out((H, quarter, PACK), bf16)],
        [query_weight, key_weight, pos_weight, value_router, output_router, value_experts],
    )[0]
    weight = swap_shard(packed, rank).reshape(D, PACK)
    x_own = inputs[:, 0]
    x_all = gather_shard(x_own, rank).transpose(1, 0, 2, 3).reshape(micro, length, D)
    w_out_heads = jnp.pad(output_experts.reshape(E, DH, D), ((0, 0), (0, LANE - DH), (0, 0)))
    w_out_heads = w_out_heads.reshape(E * LANE, D)
    w_in = swap_shard(ffn_in.reshape(quarter, H, D).transpose(1, 0, 2), rank).reshape(D, D)
    cot_own = cotangent[:, 0]
    cot_all = gather_shard(cot_own, rank).transpose(1, 0, 2, 3).reshape(micro, length, D)
    sine = sinusoid(length, D).astype(bf16)
    pos = mm(sine, weight[:, 2 * LANE : 3 * LANE]).astype(bf16)
    b_in = ffn_in_bias.astype(f32).reshape(1, -1)

    saved = []
    totals = []
    for m in range(micro):
        res = call(
            attention_kernel,
            [
                out((length, D), bf16),
                out((length, LANE), bf16),
                out((length, LANE), bf16),
                out((length, LANE), bf16),
                out((length, LANE), bf16),
                out((length, E * LANE), f32),
                out((length, LANE), f32),
                out((length, length), f32),
                out((length, LANE), f32),
                out((length, E * LANE), bf16),
                out((length, D), bf16),
            ],
            [x_all[m], vec, head, rows[m], weight, pos, w_out_heads],
            flops=2 * length * D * 1700,
        )
        saved.append(res)
        totals.append(sum_rows(res[-1], core))
    ffn = []
    for m in range(micro):
        ffn.append(
            call(
                ffn_kernel,
                [out((length, D), bf16)] * 4,
                [x_all[m], totals[m], vec, w_in, b_in, ffn_out, cot_all[m]],
                flops=2 * length * D * D * 3,
            )
        )
    gn2 = [sum_rows(f[3], core) for f in ffn]
    outs_m = []
    for m in range(micro):
        part = mm(ffn[m][1], ffn_out).astype(bf16)
        mine, other = scatter_rows(part, rank)
        tot_own = take(totals[m], rank * own, own)
        outs_m.append(
            call(output_kernel, [out((own, D), bf16)], [x_own[m], tot_own, mine, other, vec])[0]
        )
    grad_out_w = sum(mm(ffn[m][1], cot_all[m], TN) for m in range(micro))
    grad_in_w = sum(mm(ffn[m][0], ffn[m][2], TN) for m in range(micro))
    grad_in_b = sum(jnp.sum(ffn[m][2].astype(f32), axis=0) for m in range(micro))
    back = []
    for m in range(micro):
        n1, qc, qp, k, v, va, gate, prob, att, mix, _ = saved[m]
        back.append(
            call(
                back_kernel,
                [
                    out((length, D), bf16),
                    out((8, D), f32),
                    out((length, PACK), bf16),
                    out((length, LANE), f32),
                    out((8, LANE), f32),
                    out((length, D), bf16),
                ],
                [
                    x_all[m],
                    totals[m],
                    gn2[m],
                    cot_all[m],
                    vec,
                    weight,
                    w_out_heads,
                    pos,
                    qc,
                    qp,
                    k,
                    v,
                    va,
                    gate,
                    prob,
                    att,
                ],
                scratch=[
                    pltpu.VMEM((length, LANE), bf16),
                    pltpu.VMEM((length, LANE), f32),
                    pltpu.VMEM((length, LANE), f32),
                    pltpu.VMEM((length, LANE), f32),
                ],
                flops=2 * length * D * 2000,
            )
        )
    grads_x = []
    norm1_sums = 0.0
    for m in range(micro):
        mine, other = scatter_rows(back[m][5], rank)
        tot_own = take(totals[m], rank * own, own)
        gn2_own = take(gn2[m], rank * own, own)
        gx, sums = call(
            input_kernel,
            [out((own, D), f32), out((8, D), f32)],
            [x_own[m], tot_own, gn2_own, cot_own[m], mine, other, vec],
        )
        grads_x.append(gx)
        norm1_sums = norm1_sums + sums[0:2]
    grad_wo = sum(mm(saved[m][9], back[m][0], TN) for m in range(micro))
    grad_pack = sum(mm(saved[m][0], back[m][2], TN) for m in range(micro))
    grad_pos = mm(sine, sum(back[m][3] for m in range(micro)).astype(bf16), TN)
    grad_pack = lax.dynamic_update_slice(grad_pack, grad_pos, (0, 2 * LANE))

    def combine(grad, exchange):
        piece = reduce_dp(grad, order, dp_rank).astype(bf16)
        if exchange:
            piece = swap_shard(piece, rank)
        return gather_dp(piece, order, dp_rank)

    g_out = combine(grad_out_w.reshape(H, quarter, D), False).reshape(D, D).astype(f32)
    g_in = combine(grad_in_w.reshape(H, quarter, D), True)
    g_in = g_in.transpose(1, 0, 2).reshape(quarter, FF).astype(f32)
    g_wo = combine(grad_wo.reshape(1, E * LANE, D), False)
    g_wo = g_wo.reshape(E, LANE, D)[:, :DH].reshape(E * DH, D).astype(f32)
    g_pack = combine(grad_pack.reshape(H, quarter, PACK), True)
    g_q, g_k, g_p, g_rv, g_ro, g_v = call(
        unpack_kernel,
        [
            out((quarter, H * DH), f32),
            out((quarter, H * DH), f32),
            out((quarter, H * DH), f32),
            out((quarter, H * E), f32),
            out((quarter, H * E), f32),
            out((quarter, H * E * DH), f32),
        ],
        [g_pack],
    )

    norm1 = norm1_sums.reshape(2, H, quarter)
    norm1 = sum(
        flip_shard(take(norm1, rank ^ r, 1, 1), r) if r else take(norm1, rank, 1, 1)
        for r in range(H)
    )[:, 0]
    sums = sum(back[m][1] for m in range(micro))
    sums = take(sums[0:3], rank * quarter, quarter, 1)
    biases = sum(back[m][4] for m in range(micro))[0:2]
    small = jnp.concatenate(
        [norm1.reshape(-1), sums.reshape(-1), biases.reshape(-1), grad_in_b]
    ).reshape(-1, LANE)
    small = sum_dp_small(small, order).reshape(-1)
    n = quarter
    g1, b1, g2, b2, bo = (small[i * n : (i + 1) * n] for i in range(5))
    content = small[5 * n : 5 * n + DH]
    posb = small[5 * n + LANE : 5 * n + LANE + DH]
    bi = small[5 * n + 2 * LANE :]
    return (
        jnp.stack(outs_m)[:, None],
        jnp.stack(grads_x)[:, None],
        g1,
        b1,
        g_q,
        g_k,
        g_p,
        content,
        posb,
        g_rv,
        g_ro,
        g_v,
        g_wo,
        g2,
        b2,
        g_in,
        bi,
        g_out,
        bo,
    )


def solution(mesh):
    tokens = P(None, "dp", "shard")
    whole = P(None, "dp", "shard", None)
    routes = P(None, "dp", "shard", None, None)
    vector = P("shard")
    matrix = P("shard", None)
    weights = (
        vector,
        vector,
        matrix,
        matrix,
        matrix,
        vector,
        vector,
        matrix,
        matrix,
        matrix,
        matrix,
        vector,
        vector,
        matrix,
        vector,
        matrix,
        vector,
    )
    return jax.shard_map(
        local,
        mesh=mesh,
        in_specs=(whole, tokens, tokens, routes, routes) + weights + (whole,),
        out_specs=(whole, whole) + weights,
        check_vma=False,
    )
```

```python
import functools
import math

import jax
import jax.numpy as jnp
from jax import lax
from jax.experimental import pallas as pl
from jax.experimental.pallas import tpu as pltpu
from jax.sharding import PartitionSpec as P

D = 1024
H = 4
DH = 112
E = 5
FF = 4096
LANE = 128
PACK = 1024
BLK = 128
RING = 8
TAIL = 8
MASKED = -1e30
SCALE = DH ** (-0.5)
bf16 = jnp.bfloat16
f32 = jnp.float32
NN = (((1,), (0,)), ((), ()))
NT = (((1,), (1,)), ((), ()))
TN = (((0,), (0,)), ((), ()))


def mm(a, b, dims=NN):
    return lax.dot_general(a, b, dims, preferred_element_type=f32)


def call(kernel, outs, args, scratch=(), copies=0, flops=0, vmem=56, smem=2):
    in_specs, arrays = [], []
    for i, arg in enumerate(args):
        far = isinstance(arg, Far)
        space = pltpu.SMEM if i < smem else pl.ANY if far else pltpu.VMEM
        in_specs.append(pl.BlockSpec(memory_space=space))
        arrays.append(arg.value if far else arg)
    out_specs, out_shapes = [], []
    for o in outs:
        far = isinstance(o, Far)
        out_specs.append(pl.BlockSpec(memory_space=pl.ANY if far else pltpu.VMEM))
        out_shapes.append(o.value if far else o)
    moved = sum(math.prod(a.shape) * a.dtype.itemsize for a in arrays + out_shapes)
    scratch = list(scratch)
    if copies:
        scratch.append(pltpu.SemaphoreType.DMA((copies,)))
    return pl.pallas_call(
        kernel,
        out_shape=out_shapes,
        in_specs=in_specs,
        out_specs=out_specs,
        scratch_shapes=scratch,
        compiler_params=pltpu.CompilerParams(vmem_limit_bytes=vmem << 20),
        cost_estimate=pl.CostEstimate(flops=flops, bytes_accessed=moved, transcendentals=0),
    )(*arrays)


class Far:
    def __init__(self, value):
        self.value = value


class Copies:
    def __init__(self, sems):
        self.sems, self.count, self.left = sems, 0, []

    def start(self, src, dst):
        copy = pltpu.make_async_copy(src, dst, self.sems.at[self.count])
        self.count += 1
        copy.start()
        self.left.append(copy)
        return copy

    def wait(self, *copies):
        for copy in copies:
            copy.wait()
            self.left.remove(copy)

    def finish(self):
        self.wait(*list(self.left))


def out(shape, dtype):
    return jax.ShapeDtypeStruct(shape, dtype)


def prep_kernel(rank_ref, side_ref, *refs):
    count = 18
    ins, outs, scratch = refs[:count], refs[count : count + 6], refs[count + 6 :]
    held, marks_ref, sems = scratch[:count], scratch[count], scratch[count + 1]
    copies = Copies(sems)
    for src, dst in zip(ins, held):
        copies.start(src, dst)
    copies.finish()
    q_ref, k_ref, p_ref, rv_ref, ro_ref, v_ref, routes_v_ref, routes_o_ref = held[:8]
    seg_ref, pad_ref, g1_ref, b1_ref, g2_ref, b2_ref, bo_ref, cb_ref, pb_ref, bi_ref = held[8:]
    head_ref, bin_ref = outs[4:]
    head_ref[...] = jnp.zeros(head_ref.shape, f32)
    head_ref[0:1, 0:DH] = cb_ref[...].astype(f32).reshape(1, -1)
    head_ref[1:2, 0:DH] = pb_ref[...].astype(f32).reshape(1, -1)
    bin_ref[...] = bi_ref[...].astype(f32).reshape(1, -1)
    micro, own = seg_ref.shape[0], seg_ref.shape[2]
    marks_ref[...] = jnp.zeros(marks_ref.shape, f32)
    for m in range(micro):
        cols = slice(m * own, (m + 1) * own)
        marks_ref[2:3, cols] = seg_ref[m].astype(f32)
        marks_ref[3:4, cols] = pad_ref[m].astype(f32)
    for i, ref in enumerate((g1_ref, b1_ref, g2_ref, b2_ref, bo_ref)):
        marks_ref[4 + i : 5 + i, :] = ref[...].astype(f32).reshape(1, -1)
    row = lax.broadcasted_iota(jnp.int32, (16, H * E), 0)
    col = lax.broadcasted_iota(jnp.int32, (16, H * E), 1)
    for r, out_ref in enumerate(outs[:4]):
        h = rank_ref[0] ^ r
        rows = pl.ds(pl.multiple_of(h * DH, 16), DH)
        for m in range(micro):
            cols = slice(m * own, (m + 1) * own)
            for i, ref in enumerate((routes_v_ref, routes_o_ref)):
                ones = lax.shift_left(jnp.ones((2, own), jnp.int32), ref[m, h])
                marks_ref[i : i + 1, cols] = jnp.sum(ones.astype(f32), axis=0, keepdims=True)
        pick_v = jnp.where((row < E) & (col == h * E + row), 1.0, 0.0).astype(bf16)
        pick_o = jnp.where((row >= E) & (row < 2 * E) & (col == h * E + row - E), 1.0, 0.0)
        routers = mm(pick_v, rv_ref[...]) + mm(pick_o.astype(bf16), ro_ref[...])
        out_ref[0:DH, :] = q_ref[rows, :]
        out_ref[DH:LANE, :] = routers.astype(bf16)
        out_ref[LANE : LANE + DH, :] = k_ref[rows, :]
        out_ref[LANE + DH : 2 * LANE, :] = marks_ref[...].astype(bf16)
        out_ref[2 * LANE : 2 * LANE + DH, :] = p_ref[rows, :]
        out_ref[2 * LANE + DH : 3 * LANE, :] = jnp.zeros((LANE - DH, out_ref.shape[1]), bf16)
        for e in range(E):
            at = (3 + e) * LANE
            expert = pl.ds(pl.multiple_of((h * E + e) * DH, 16), DH)
            out_ref[at : at + DH, :] = v_ref[expert, :]
            out_ref[at + DH : at + LANE, :] = jnp.zeros((LANE - DH, out_ref.shape[1]), bf16)


def norm_stats(x):
    mean = jnp.mean(x, axis=-1, keepdims=True)
    centred = x - mean
    var = jnp.mean(centred * centred, axis=-1, keepdims=True)
    rstd = lax.rsqrt(var + 1e-05)
    return centred * rstd, rstd


def norm_back(grad, unit, rstd, gain):
    g = grad * gain
    return rstd * (
        g
        - jnp.mean(g, axis=-1, keepdims=True)
        - unit * jnp.mean(g * unit, axis=-1, keepdims=True)
    )


def attention_kernel(m, rank_ref, side_ref, *refs):
    first = m == 0
    (x0, x1, x2, x3), refs = refs[:4], refs[4:]
    head_ref, refs = refs[0], refs[1:]
    if first:
        (w0, w1, w2, w3, sine_hbm, wo_hbm), refs = refs[:6], refs[6:]
    else:
        (wt_hbm, wo_hbm, pos_ref, vec_ref, rows_ref), refs = refs[:5], refs[5:]
    (x_ref, n_hbm, qc_hbm, qp_hbm, k_hbm, v_hbm, va_hbm, gate_hbm, p_hbm, att_hbm), refs = (
        refs[:10],
        refs[10:],
    )
    (mix_hbm, stat_ref), refs = refs[:2], refs[2:]
    (send_ref, keep_ref), refs = refs[:2], refs[2:]
    if first:
        (wt_hbm, wop_hbm, pos_ref, vec_ref, rows_ref), refs = refs[:5], refs[5:]
    n_ref, qc_ref, qp_ref, k_ref, v_ref, va_ref, gate_ref, p_ref, att_ref, mix_ref = refs[:10]
    wt_ref, wo_ref = refs[10:12]
    sine_ref = refs[12] if first else None
    copies = Copies(refs[-1])
    length = x_ref.shape[0]
    blocks = length // BLK
    rank = rank_ref[0]
    quarter = D // H

    def at(r, size):
        return pl.ds(pl.multiple_of((rank ^ r) * size, size), size)

    loads = [copies.start(ref.at[m], x_ref.at[at(r, BLK), :]) for r, ref in enumerate((x0, x1, x2, x3))]
    if first:
        for r, ref in enumerate((w0, w1, w2, w3)):
            loads.append(copies.start(ref, wt_ref.at[:, at(r, quarter)]))
        sine_load = copies.start(sine_hbm, sine_ref)
        wo_loads = []
        for e in range(E):
            rows = slice(e * LANE, e * LANE + DH)
            wo_loads.append(copies.start(wo_hbm.at[e * DH : (e + 1) * DH, :], wo_ref.at[rows, :]))
            wo_ref[e * LANE + DH : (e + 1) * LANE, :] = jnp.zeros((LANE - DH, D), bf16)
        copies.wait(*loads)
        vec_ref[...] = jnp.zeros(vec_ref.shape, f32)
        rows_ref[...] = jnp.zeros(rows_ref.shape, f32)
        for r in range(H):
            marks = wt_ref[LANE + DH : 2 * LANE, at(r, quarter)].astype(f32)
            vec_ref[0:5, at(r, quarter)] = marks[4:9, :]
            for i in range(rows_ref.shape[0]):
                part = marks[:, i * BLK : (i + 1) * BLK]
                rows_ref[i, 0:1, at(r, BLK)] = part[0:1, :] + 2.0**E * part[1:2, :]
                rows_ref[i, 1:3, at(r, BLK)] = part[2:4, :]
        copies.start(wt_ref, wt_hbm)
    else:
        wt_load = copies.start(wt_hbm, wt_ref)
        wo_loads = [copies.start(wo_hbm, wo_ref)]
        copies.wait(*loads)

    @pl.loop(0, blocks)
    def _(b):
        rows = pl.ds(pl.multiple_of(b * BLK, BLK), BLK)
        x = x_ref[rows, :].astype(f32)
        unit, rstd = norm_stats(x)
        n_ref[rows, :] = (unit * vec_ref[0:1, :] + vec_ref[1:2, :]).astype(bf16)
        first_lane = lax.broadcasted_iota(jnp.int32, (BLK, LANE), 1) == 0
        stat_ref[rows, :] = jnp.where(first_lane, jnp.mean(x, axis=-1, keepdims=True), rstd)

    copies.start(n_ref, n_hbm)
    if first:
        copies.wait(sine_load)
        pos_ref[...] = mm(sine_ref[...], wt_ref[2 * LANE : 3 * LANE, :], NT).astype(bf16)
    else:
        copies.wait(wt_load)
    lane = lax.broadcasted_iota(jnp.int32, (1, LANE), 1)
    is_head = lane < DH
    raw = mm(n_ref[...], wt_ref[0:LANE, :], NT)
    columns = rows_ref[m].T
    code = jnp.broadcast_to(columns[:, 0:1].astype(jnp.int32), (length, LANE))
    slot = jnp.where((lane >= DH) & (lane < DH + 2 * E), lane - DH, 31)
    pick = (lax.shift_right_logical(code, jnp.broadcast_to(slot, (length, LANE))) & 1) == 1
    gate = jnp.where(pick, 1.0 / (1.0 + jnp.exp(-raw)), 0.0)
    gate_ref[...] = gate
    copies.start(gate_ref, gate_hbm)
    qc_ref[...] = jnp.where(is_head, (raw + head_ref[0:1, :]) * SCALE, 0.0).astype(bf16)
    qp_ref[...] = jnp.where(is_head, (raw + head_ref[1:2, :]) * SCALE, 0.0).astype(bf16)
    keys = mm(n_ref[...], wt_ref[LANE : 2 * LANE, :], NT)
    k_ref[...] = jnp.where(is_head, keys, 0.0).astype(bf16)
    values = jnp.zeros((length, LANE), f32)
    for e in range(E):
        part = mm(n_ref[...], wt_ref[(3 + e) * LANE : (4 + e) * LANE, :], NT)
        va_ref[:, e * LANE : (e + 1) * LANE] = part
        values += part * gate[:, DH + e : DH + e + 1]
    v_ref[...] = values.astype(bf16)
    for src, dst in ((qc_ref, qc_hbm), (qp_ref, qp_hbm), (k_ref, k_hbm), (v_ref, v_hbm), (va_ref, va_hbm)):
        copies.start(src, dst)
    seg_col = columns[:, 1:2]
    for b in range(blocks):
        rows = slice(b * BLK, (b + 1) * BLK)
        wide = (b + 1) * BLK
        content = mm(qc_ref[rows, :], k_ref[0:wide, :], NT)
        table = mm(qp_ref[rows, :], pos_ref[length - wide : length, :], NT)
        table = pltpu.roll(table, (wide - BLK + 1) % wide, 1, stride=1, stride_axis=0)
        row = lax.broadcasted_iota(jnp.int32, (BLK, wide), 0) + b * BLK
        col = lax.broadcasted_iota(jnp.int32, (BLK, wide), 1)
        same = seg_col[rows, :] == rows_ref[m, 1:2, 0:wide]
        live = ((rows_ref[m, 2:3, 0:wide] > 0.0) & (col < row)) | (col == row)
        scores = jnp.where(same & live, content + table, MASKED)
        top = jnp.max(scores, axis=-1, keepdims=True)
        expo = jnp.exp(scores - top)
        prob = expo / jnp.sum(expo, axis=-1, keepdims=True)
        p_ref[rows, 0:wide] = prob
        att = mm(prob.astype(bf16), v_ref[0:wide, :])
        att_ref[rows, :] = att
        for e in range(E):
            share = gate_ref[rows, DH + E + e : DH + E + e + 1]
            mix_ref[rows, e * LANE : (e + 1) * LANE] = (att * share).astype(bf16)
        copies.start(p_ref.at[rows, 0:wide], p_hbm.at[rows, 0:wide])
    copies.start(att_ref, att_hbm)
    copies.start(mix_ref, mix_hbm)
    half = length // 2
    core = rank & 1
    copies.wait(*wo_loads)
    if first:
        copies.start(wo_ref, wop_hbm)
    for place, ref in ((core, keep_ref), (1 - core, send_ref)):
        rows = pl.ds(pl.multiple_of(place * half, half), half)
        ref[...] = mm(mix_ref[rows, :], wo_ref[...]).astype(bf16)
    copies.finish()


def normal_terms(v):
    bell = jnp.exp(-0.5 * v * v)
    phi = 0.5 * (1.0 + lax.erf(v * (1.0 / math.sqrt(2.0))))
    return phi, bell * (1.0 / math.sqrt(2.0 * math.pi))


def pair_rows(core, b, refs):
    mine, far, mine2, far2 = refs
    own_half = (b // 2) == core
    rows = pl.ds(pl.multiple_of((b % 2) * BLK, BLK), BLK)
    near = mine[rows, :].astype(f32) + far[rows, :].astype(f32)
    away = mine2[rows, :].astype(f32) + far2[rows, :].astype(f32)
    return jnp.where(own_half, near, away)


def ffn_kernel(
    m,
    rank_ref,
    side_ref,
    x_ref,
    a0,
    a1,
    a2,
    a3,
    vec_ref,
    bin_ref,
    win_hbm,
    win_core,
    *refs,
):
    win_shares, refs = refs[:RING], refs[RING:]
    (wout_hbm, c0, c1, c2, c3), refs = refs[:5], refs[5:]
    (n_ref, hid_ref, gp_ref, cot_ref, unit_hbm, rstd_ref, resid_ref, sum_ref), refs = (
        refs[:8],
        refs[8:],
    )
    send_ref, keep_ref, unit_ref, win_ref, wout_ref, sems = refs
    length = x_ref.shape[0]
    rank, place = rank_ref[0], side_ref[0]
    core = rank & 1
    copies = Copies(sems)
    size = D // H
    sum_ref[...] = jnp.zeros(sum_ref.shape, f32)

    def at(r, size):
        return pl.ds(pl.multiple_of((rank ^ r) * size, size), size)

    loads = []
    width = win_ref.shape[1]
    own_cols = pl.ds(pl.multiple_of(rank * width, width), width)
    loads.append(copies.start(win_hbm.at[:, own_cols], win_ref.at[at(0, size), :]))
    loads.append(copies.start(win_core, win_ref.at[at(1, size), :]))
    share = size // RING
    for o, ref in enumerate(win_shares):
        for r in (2, 3):
            start = (rank ^ r) * size + (place ^ o) * share
            rows = pl.ds(pl.multiple_of(start, share), share)
            loads.append(copies.start(ref.at[r - 2], win_ref.at[rows, :]))
    loads.append(copies.start(wout_hbm, wout_ref))
    for r, ref in enumerate((c0, c1, c2, c3)):
        loads.append(copies.start(ref.at[m], cot_ref.at[at(r, BLK), :]))

    @pl.loop(0, length // BLK)
    def _(b):
        rows = pl.ds(pl.multiple_of(b * BLK, BLK), BLK)
        resid = x_ref[rows, :].astype(f32) + pair_rows(core, b, (a0, a1, a2, a3))
        unit, rstd = norm_stats(resid)
        unit_ref[rows, :] = unit
        rstd_ref[rows, :] = jnp.broadcast_to(rstd, (BLK, LANE))
        n_ref[rows, :] = (unit * vec_ref[2:3, :] + vec_ref[3:4, :]).astype(bf16)

        @pl.when(b == rank)
        def _():
            resid_ref[...] = resid

    copies.wait(*loads)
    copies.start(unit_ref, unit_hbm)
    chunk = 256

    @pl.loop(0, width // chunk)
    def _(c):
        cols = pl.ds(pl.multiple_of(c * chunk, chunk), chunk)
        pre = mm(n_ref[...], win_ref[:, cols]) + bin_ref[0:1, cols]
        back = mm(cot_ref[...], wout_ref[cols, :], NT)
        phi, density = normal_terms(pre)
        hid_ref[:, cols] = (pre * phi).astype(bf16)
        grad = (back * (phi + pre * density)).astype(bf16)
        gp_ref[:, cols] = grad
        sum_ref[0:1, cols] = jnp.sum(grad.astype(f32), axis=0, keepdims=True)

    half = length // 2
    for place, ref in ((core, keep_ref), (1 - core, send_ref)):
        rows = pl.ds(pl.multiple_of(place * half, half), half)
        ref[...] = mm(gp_ref[rows, :], win_ref[...], NT).astype(bf16)
    copies.finish()


def split_blocks(rank, value_ref, keep_ref, send_ref):
    for r in range(H):
        rows = pl.ds(pl.multiple_of((rank ^ r) * BLK, BLK), BLK)
        (send_ref if r % 2 else keep_ref)[r // 2] = value_ref[rows, :]


def project_kernel(rank_ref, side_ref, hid_ref, wout_ref, keep_ref, send_ref, full_ref):
    full_ref[...] = mm(hid_ref[...], wout_ref[...]).astype(bf16)
    split_blocks(rank_ref[0], full_ref, keep_ref, send_ref)


def back_kernel(
    rank_ref,
    side_ref,
    rstd_ref,
    a0,
    a1,
    a2,
    a3,
    cot_ref,
    vec_ref,
    pos_ref,
    *refs,
):
    hbm, refs = refs[:13], refs[13:]
    (gb_ref, sums_ref, dproj_ref, gpos_ref, bias_ref, grad_ref, keep_ref, send_ref), refs = (
        refs[:8],
        refs[8:],
    )
    held, refs = refs[:13], refs[13:]
    ga_ref, gk_ref, gv_ref, logit_ref, full_ref, sems = refs
    copies = Copies(sems)
    unit_load, *loads = [copies.start(src, dst) for src, dst in zip(hbm, held)]
    unit_ref, wo_ref, gate_ref, att_ref, p_ref, v_ref, k_ref, qc_ref, qp_ref, va_ref = held[:10]
    wt_ref, x_ref, stat_ref = held[10:]
    length = unit_ref.shape[0]
    blocks = length // BLK
    rank = rank_ref[0]
    core = rank & 1
    copies.wait(unit_load)
    sums_ref[...] = jnp.zeros(sums_ref.shape, f32)

    @pl.loop(0, blocks)
    def _(b):
        rows = pl.ds(pl.multiple_of(b * BLK, BLK), BLK)
        unit = unit_ref[rows, :]
        grad = pair_rows(core, b, (a0, a1, a2, a3))
        sums_ref[0:1, :] += jnp.sum(grad * unit, axis=0, keepdims=True)
        sums_ref[1:2, :] += jnp.sum(grad, axis=0, keepdims=True)
        cot = cot_ref[rows, :].astype(f32)
        sums_ref[2:3, :] += jnp.sum(cot, axis=0, keepdims=True)
        total = cot + norm_back(grad, unit, rstd_ref[rows, 0:1], vec_ref[2:3, :])
        gb_ref[rows, :] = total.astype(bf16)

        @pl.when(b == rank)
        def _():
            grad_ref[...] = total

    copies.wait(*loads)
    lane = lax.broadcasted_iota(jnp.int32, (1, LANE), 1)
    acc = jnp.zeros((length, LANE), f32)
    logits = jnp.zeros((length, LANE), f32)
    for e in range(E):
        mixed = mm(gb_ref[...], wo_ref[e * LANE : (e + 1) * LANE, :], NT)
        acc += mixed * gate_ref[:, DH + E + e : DH + E + e + 1]
        dot = jnp.sum(mixed * att_ref[...], axis=-1, keepdims=True)
        logits = jnp.where(lane == DH + E + e, dot, logits)
    ga_ref[...] = acc.astype(bf16)
    logit_ref[...] = logits
    gk_ref[...] = jnp.zeros(gk_ref.shape, f32)
    gv_ref[...] = jnp.zeros(gv_ref.shape, f32)
    gpos_ref[...] = jnp.zeros(gpos_ref.shape, f32)
    row = lax.broadcasted_iota(jnp.int32, (BLK, BLK), 0)
    col = lax.broadcasted_iota(jnp.int32, (BLK, BLK), 1)
    mirror = jnp.where(row + col == BLK - 1, 1.0, 0.0).astype(bf16)
    cont_sum = jnp.zeros((1, LANE), f32)
    posn_sum = jnp.zeros((1, LANE), f32)
    for b in range(blocks):
        rows = slice(b * BLK, (b + 1) * BLK)
        wide = (b + 1) * BLK
        prob = p_ref[rows, 0:wide]
        ga = ga_ref[rows, :]
        grad_prob = mm(ga, v_ref[0:wide, :], NT)
        delta = jnp.sum(prob * grad_prob, axis=-1, keepdims=True)
        grad_score = (prob * (grad_prob - delta)).astype(bf16)
        gv_ref[0:wide, :] += mm(prob.astype(bf16), ga, TN)
        gk_ref[0:wide, :] += mm(grad_score, qc_ref[rows, :], TN)
        cont = mm(grad_score, k_ref[0:wide, :]) * SCALE
        table = pltpu.roll(mm(mirror, grad_score), 0, 1, stride=1, stride_axis=0)
        table = mm(mirror, table.astype(bf16)).astype(bf16)
        posn = mm(table, pos_ref[length - wide : length, :]) * SCALE
        gpos_ref[length - wide : length, :] += mm(table, qp_ref[rows, :], TN)
        cont_sum += jnp.sum(cont, axis=0, keepdims=True)
        posn_sum += jnp.sum(posn, axis=0, keepdims=True)
        dproj_ref[rows, 0:LANE] = (cont + posn).astype(bf16)
    bias_ref[...] = jnp.zeros(bias_ref.shape, f32)
    bias_ref[0:1, :] = cont_sum
    bias_ref[1:2, :] = posn_sum
    dproj_ref[:, LANE : 2 * LANE] = gk_ref[...].astype(bf16)
    dproj_ref[:, 2 * LANE : 3 * LANE] = jnp.zeros((length, LANE), bf16)
    grad_values = gv_ref[...].astype(bf16).astype(f32)
    logits = logit_ref[...]
    for e in range(E):
        cols = slice((3 + e) * LANE, (4 + e) * LANE)
        dproj_ref[:, cols] = (grad_values * gate_ref[:, DH + e : DH + e + 1]).astype(bf16)
        dot = jnp.sum(grad_values * va_ref[:, e * LANE : (e + 1) * LANE], axis=-1, keepdims=True)
        logits = jnp.where(lane == DH + e, dot, logits)
    gate = gate_ref[...]
    logits = logits * gate * (1.0 - gate)
    dproj_ref[:, 0:LANE] = jnp.where(
        lane < DH, dproj_ref[:, 0:LANE].astype(f32), logits
    ).astype(bf16)
    chunk = 256
    mean, rstd = stat_ref[:, 0:1], stat_ref[:, 1:2]

    @pl.loop(0, D // chunk)
    def _(c):
        cols = pl.ds(pl.multiple_of(c * chunk, chunk), chunk)
        part = mm(dproj_ref[...], wt_ref[:, cols])
        full_ref[:, cols] = part.astype(bf16)
        unit = (x_ref[:, cols].astype(f32) - mean) * rstd
        sums_ref[3:4, cols] = jnp.sum(part * unit, axis=0, keepdims=True)
        sums_ref[4:5, cols] = jnp.sum(part, axis=0, keepdims=True)

    split_blocks(rank, full_ref, keep_ref, send_ref)


def output_kernel(m, rank_ref, side_ref, resid_ref, keep_ref, got_ref, far_ref, vec_ref, y_ref):
    total = resid_ref[...] + keep_ref[0].astype(f32) + got_ref[0].astype(f32)
    y_ref[...] = (total + far_ref[...].astype(f32) + vec_ref[4:5, :]).astype(bf16)


def input_kernel(m, rank_ref, side_ref, x_ref, grad_ref, keep_ref, got_ref, far_ref, vec_ref, y_ref):
    unit, rstd = norm_stats(x_ref[m].astype(f32))
    back = keep_ref[0].astype(f32) + got_ref[0].astype(f32) + far_ref[...].astype(f32)
    y_ref[...] = grad_ref[...] + norm_back(back, unit, rstd, vec_ref[0:1, :])


def vectors_kernel(rank_ref, side_ref, sums0, sums1, bias0, bias1, hid0, hid1, y_ref):
    y_ref[...] = jnp.zeros(y_ref.shape, f32)
    width = D // H
    own = pl.ds(pl.multiple_of(rank_ref[0] * width, width), width)
    y_ref[0, 6:7, :] = sums0[3:4, :] + sums1[3:4, :]
    y_ref[1, 6:7, :] = sums0[4:5, :] + sums1[4:5, :]
    for i in range(3):
        y_ref[i, 7:8, own] = sums0[i : i + 1, own] + sums1[i : i + 1, own]
    for i in range(2):
        cols = pl.ds(pl.multiple_of(rank_ref[0] * width + i * LANE, LANE), LANE)
        y_ref[3, 7:8, cols] = bias0[i : i + 1, :] + bias1[i : i + 1, :]
    for i in range(4):
        cols = slice(i * width, (i + 1) * width)
        y_ref[4 + i, 7:8, own] = hid0[0:1, cols] + hid1[0:1, cols]


def load_ffn_chunk(copies, c, sources, dst):
    grad_o, grad_i = sources
    rows = D // RING
    part = rows // H
    copies.start(grad_o.at[pl.ds(pl.multiple_of(c * rows, rows), rows), :], dst.at[0:rows, :])
    for s in range(H):
        src = pl.ds(pl.multiple_of(s * (D // H) + c * part, part), part)
        copies.start(grad_i.at[src, :], dst.at[rows + s * part : rows + (s + 1) * part, :])


def load_pack_chunk(copies, c, sources, dst):
    grad_p, grad_w = sources
    rows = D // RING
    part = E * LANE // RING
    copies.start(grad_p.at[pl.ds(pl.multiple_of(c * rows, rows), rows), :], dst.at[0:rows, :])
    copies.start(
        grad_w.at[pl.ds(pl.multiple_of(c * part, part), part), :], dst.at[rows : rows + part, :]
    )


def ring_kernel(load, split, t, rank_ref, pos_ref, src0, src1, *refs):
    tail_ref, refs = (refs[0], refs[1:]) if load is load_pack_chunk else (None, refs)
    got, refs = (refs[:2], refs[2:]) if t else ((None, None), refs)
    outs, refs = (refs[:2], refs[2:]) if t < 4 else (refs[:1], refs[1:])
    held, sems = refs
    copies = Copies(sems)
    pos = pos_ref[0]
    total = held.shape[1]
    chunks = [(pos + 4 - t) % RING, (pos + 4 + t) % RING][: len(outs)]
    for i, c in enumerate(chunks):
        load(copies, c, (src0, src1), held.at[i])
    copies.finish()
    if tail_ref is not None:
        for i, c in enumerate(chunks):
            rows = slice(D // RING - TAIL, D // RING)
            held[i, rows, :] = held[i, rows, :] + tail_ref[c]
    if t == 0:
        outs[0][...] = held[0, 0:split, :].astype(bf16)
        outs[1][...] = held[1, split:total, :].astype(bf16)
    elif t == 1:
        outs[0][0:split, :] = (held[0, 0:split, :] + got[0][...].astype(f32)).astype(bf16)
        outs[0][split:total, :] = held[0, split:total, :].astype(bf16)
        outs[1][0:split, :] = held[1, 0:split, :].astype(bf16)
        outs[1][split:total, :] = (held[1, split:total, :] + got[1][...].astype(f32)).astype(bf16)
    elif t < 4:
        for i in range(2):
            outs[i][...] = (held[i] + got[i][...].astype(f32)).astype(bf16)
    else:
        outs[0][...] = (held[0] + got[0][...].astype(f32) + got[1][...].astype(f32)).astype(bf16)


def load_ring(copies, pos, split, refs, dst):
    own, fwd, bwd, half_fwd, half_bwd = refs[0], refs[1:4], refs[4:7], refs[7], refs[8]
    copies.start(own, dst.at[pos])
    for i in range(3):
        copies.start(fwd[i], dst.at[(pos + RING - 1 - i) % RING])
        copies.start(bwd[i], dst.at[(pos + 1 + i) % RING])
    last = (pos + 4) % RING
    copies.start(half_fwd, dst.at[last, 0:split, :])
    copies.start(half_bwd, dst.at[last, split : dst.shape[1], :])
    copies.finish()


def ffn_grads_kernel(split, rank_ref, pos_ref, *refs):
    parts, (o_hbm, i_hbm, held, o_ref, i_ref, sems) = refs[:9], refs[9:]
    copies = Copies(sems)
    load_ring(copies, pos_ref[0], split, parts, held)
    rows = D // RING
    part = rows // H
    for c in range(RING):
        o_rows = slice(c * rows, (c + 1) * rows)
        o_ref[o_rows, :] = held[c, 0:rows, :].astype(f32)
        copies.start(o_ref.at[o_rows, :], o_hbm.at[o_rows, :])
        i_rows = slice(c * part, (c + 1) * part)
        for r in range(H):
            cols = pl.ds(pl.multiple_of((rank_ref[0] ^ r) * D, D), D)
            at = rows + r * part
            i_ref[i_rows, cols] = held[c, at : at + part, :].astype(f32)
        copies.start(i_ref.at[i_rows, :], i_hbm.at[i_rows, :])
    copies.finish()


def pack_grads_kernel(split, rank_ref, pos_ref, *refs):
    parts, refs = refs[:9], refs[9:]
    (q_ref, rv_ref, ro_ref, k_ref, p_ref, v_ref, w_ref), refs = refs[:7], refs[7:]
    (g1, b1, g2, b2, bo, content, posn, bin_ref), refs = refs[:8], refs[8:]
    held, heads, sems = refs
    copies = Copies(sems)
    load_ring(copies, pos_ref[0], split, parts, held)
    width = D // H
    rank = rank_ref[0]
    for r in range(H):
        heads[rank ^ r] = held[:, 0:LANE, r * width : (r + 1) * width].astype(f32)
    for h in range(H):
        rows = slice(h * DH, (h + 1) * DH)
        q_ref[rows, :] = heads[h, 0, 0:DH, :]
        rv_ref[h * E : (h + 1) * E, :] = heads[h, 0, DH : DH + E, :]
        ro_ref[h * E : (h + 1) * E, :] = heads[h, 0, DH + E : DH + 2 * E, :]
        k_ref[rows, :] = heads[h, 1, 0:DH, :]
        p_ref[rows, :] = heads[h, 2, 0:DH, :]
        for e in range(E):
            at = (h * E + e) * DH
            v_ref[at : at + DH, :] = heads[h, 3 + e, 0:DH, :]
    part = E * LANE // RING
    for c in range(RING):
        for e in range(E):
            low, high = max(c * part, e * LANE), min((c + 1) * part, e * LANE + DH)
            if low < high:
                at = low - e * LANE + e * DH
                w_ref[at : at + high - low, :] = held[
                    c, LANE + low - c * part : LANE + high - c * part, :
                ].astype(f32)
    last = slice(LANE - 1, LANE)
    before = slice(LANE - 2, LANE - 1)
    for ref, c in ((g1, 0), (b1, 1)):
        ref[...] = sum(heads[h, c, before, :] for h in range(H)).reshape(ref.shape)
    for c, ref in enumerate((g2, b2, bo)):
        ref[...] = heads[rank, c, last, :].reshape(ref.shape)
    row = heads[rank, 3, last, :]
    content[...] = row[:, 0:DH].reshape(content.shape)
    posn[...] = row[:, LANE : LANE + DH].reshape(posn.shape)
    for i in range(4):
        bin_ref[i * width : (i + 1) * width] = heads[rank, 4 + i, last, :].reshape((width,))


def flip_shard(value, bit):
    return lax.ppermute(value, "shard", [(s, s ^ bit) for s in range(H)])


def flip_dp(value, bit):
    count = lax.axis_size("dp")
    return lax.ppermute(value, "dp", [(d, d ^ bit) for d in range(count)])


def take(value, at, size, axis=0):
    return lax.dynamic_slice_in_dim(value, at, size, axis)


def put(value, part, at, axis=0):
    return lax.dynamic_update_slice_in_dim(value, part, at, axis)


def spread(own):
    across = flip_shard(own, 2)
    return own, flip_shard(own, 1), across, flip_shard(across, 1)


def ring_order():
    return list(range(0, RING, 2)) + list(range(RING - 1, 0, -2))


def pass_on(value, way):
    order, count = ring_order(), lax.axis_size("dp")
    pairs = [
        (base + order[i], base + order[(i + way) % RING])
        for base in range(0, count, RING)
        for i in range(RING)
    ]
    return lax.ppermute(value, "dp", pairs)


def swap_shard(value, rank, size, axis):
    parts = [take(value, (rank ^ r) * size, size, axis) for r in range(H)]
    return [flip_shard(p, r) if r else p for r, p in enumerate(parts)]


def sinusoid(length, feature_count):
    distance = (length - 1 - jnp.arange(length, dtype=jnp.int32)).astype(f32)
    inv_freq = jnp.exp(
        jnp.arange(0, feature_count, 2, dtype=jnp.int32).astype(f32)
        * (-math.log(10000.0) / feature_count)
    )
    angles = distance[:, None] * inv_freq[None, :]
    return jnp.concatenate([jnp.sin(angles), jnp.cos(angles)], axis=1)


def local(
    inputs,
    segments,
    padding,
    routes_value,
    routes_output,
    norm1_gain,
    norm1_bias,
    query_weight,
    key_weight,
    pos_weight,
    content_bias,
    pos_bias,
    value_router,
    output_router,
    value_experts,
    output_experts,
    norm2_gain,
    norm2_bias,
    ffn_in,
    ffn_in_bias,
    ffn_out,
    ffn_out_bias,
    cotangent,
):
    micro = inputs.shape[0]
    own = inputs.shape[2]
    length = own * H
    dp_count = lax.axis_size("dp")
    rank = lax.axis_index("shard")
    me = rank.astype(jnp.int32).reshape(1)
    dp_rank = lax.axis_index("dp")
    side = (dp_rank % RING).astype(jnp.int32).reshape(1)
    place = dp_rank % RING
    place = jnp.where(place % 2 == 0, place // 2, RING - 1 - place // 2)
    place = place.astype(jnp.int32).reshape(1)
    quarter = D // H

    token = [me]

    def after(value, *deps):
        return lax.optimization_barrier((value, *deps))[0]

    def step(fn, first, *rest):
        res = fn(after(first, token[0]), *rest)
        token[0] = jax.tree.leaves(res)[0]
        return res

    def kernel(fn, outs, args, second=side, **kwargs):
        return step(lambda first: call(fn, outs, [first, second, *args], **kwargs), me)

    packs = kernel(
        prep_kernel,
        [out((PACK, quarter), bf16)] * H + [out((8, LANE), f32), out((1, FF // H), f32)],
        [
            Far(a)
            for a in (
                query_weight.T,
                key_weight.T,
                pos_weight.T,
                value_router.T,
                output_router.T,
                value_experts.T,
                routes_value[:, 0].transpose(0, 2, 3, 1),
                routes_output[:, 0].transpose(0, 2, 3, 1),
                segments,
                padding,
                norm1_gain,
                norm1_bias,
                norm2_gain,
                norm2_bias,
                ffn_out_bias,
                content_bias,
                pos_bias,
                ffn_in_bias,
            )
        ],
        scratch=[
            pltpu.VMEM(shape, dtype)
            for shape, dtype in [((H * DH, quarter), bf16)] * 3
            + [((H * E, quarter), bf16)] * 2
            + [((H * E * DH, quarter), bf16)]
            + [((micro, H, 2, own), jnp.int32)] * 2
            + [((micro, 1, own), jnp.int32)] * 2
            + [((quarter,), bf16)] * 5
            + [((DH,), bf16)] * 2
            + [((FF // H,), bf16)]
            + [((LANE - DH, quarter), f32)]
        ],
        copies=18,
    )
    head, b_in = packs[H:]
    weights = [packs[0]] + [flip_shard(packs[r], r) for r in range(1, H)]
    x_own = inputs[:, 0]
    x_parts = spread(x_own)
    share = quarter // RING
    cut = lambda r: lax.dynamic_slice(
        ffn_in, ((dp_rank % RING) * share, (rank ^ r) * (FF // H)), (share, FF // H)
    )
    shares = step(lambda w: (cut(2), cut(3), take(w, (rank ^ 1) * (FF // H), FF // H, 1)), ffn_in)
    w_in_core = flip_shard(shares[2], 1)
    w_in_share = step(
        lambda a, b: jnp.stack([a, b]), flip_shard(shares[0], 2), flip_shard(shares[1], 3)
    )
    w_in_shares = [w_in_share] + [flip_dp(w_in_share, o) for o in range(1, RING)]
    cot_parts = spread(after(cotangent[:, 0], x_parts[2]))
    sine = sinusoid(length, D).astype(bf16)

    def add_chip(keep, send):
        got = flip_shard(send, 1)
        add = lambda k, g: (k.astype(f32) + g.astype(f32)).astype(bf16)
        return step(add, keep, got)

    def finish_halves(chip):
        across = flip_shard(chip, 2)
        return chip, across, flip_shard(chip, 1), flip_shard(across, 1)

    half = out((length // 2, D), bf16)
    wide = out((length, D), bf16)
    saved_shapes = (
        [wide]
        + [out((length, LANE), bf16)] * 4
        + [
            out((length, E * LANE), f32),
            out((length, LANE), f32),
            out((length, length), f32),
            out((length, LANE), f32),
            out((length, E * LANE), bf16),
        ]
    )
    vmem_of = lambda shapes: [pltpu.VMEM(o.shape, o.dtype) for o in shapes]
    weight_shapes = [out((PACK, D), bf16), out((E * LANE, D), bf16)]
    saved = []
    residuals = []
    token[0] = after(token[0], *w_in_shares, w_in_core)
    for m in range(micro):
        if m == 0:
            more = [Far(w) for w in weights] + [Far(sine), Far(output_experts)]
            extra = [Far(o) for o in weight_shapes]
            extra += [out((length, LANE), bf16), out((8, D), f32), out((micro, 8, length), f32)]
        else:
            more = [Far(wt), Far(w_out_heads), pos, vec, rows]
            extra = []
        res = kernel(
            functools.partial(attention_kernel, m),
            [wide]
            + [Far(o) for o in saved_shapes]
            + [out((length, LANE), f32), half, half]
            + extra,
            [Far(x) for x in x_parts] + [head] + more,
            scratch=vmem_of(saved_shapes + weight_shapes + ([wide] if m == 0 else [])),
            copies=40,
            flops=2 * length * D * 1700,
        )
        saved.append(res[:12])
        if m == 0:
            wt, w_out_heads, pos, vec, rows = res[14:]
        residuals.append(finish_halves(add_chip(res[13], res[12])))
    ffn = []
    gn2 = []
    for m in range(micro):
        res = kernel(
            functools.partial(ffn_kernel, m),
            [wide] * 4
            + [
                Far(out((length, D), f32)),
                out((length, LANE), f32),
                out((own, D), f32),
                out((8, FF // H), f32),
                half,
                half,
            ],
            [saved[m][0], *residuals[m], vec, b_in]
            + [Far(w) for w in (ffn_in, w_in_core, *w_in_shares, ffn_out, *cot_parts)],
            scratch=vmem_of([out((length, D), f32), out((D, FF // H), bf16), out((FF // H, D), bf16)]),
            copies=24,
            flops=2 * length * D * D * 3,
        )
        ffn.append(res)
        gn2.append(finish_halves(add_chip(res[-1], res[-2])))

    def two(a, b):
        return lambda first: sum(
            mm(first if m == 0 else a[m], b[m], TN) for m in range(micro)
        )

    class Ring:
        def __init__(self, load, split, total, sources):
            self.load, self.split, self.total = load, split, total
            self.sources, self.got, self.t = sources, (), 0

        def step(self):
            sizes = {0: [self.split, self.total - self.split], 4: [self.total]}
            sizes = sizes.get(self.t, [self.total] * 2)
            res = kernel(
                functools.partial(ring_kernel, self.load, self.split, self.t),
                [out((n, D), bf16) for n in sizes],
                [Far(g) for g in self.sources[:2]] + list(self.sources[2:]) + list(self.got),
                second=place,
                scratch=[pltpu.VMEM((2, self.total, D), f32)],
                copies=10,
            )
            self.t += 1
            if len(res) == 1:
                return self.across(res[0])
            self.got = (pass_on(res[0], 1), pass_on(res[1], -1))

        def across(self, piece):
            bit = RING
            while bit < dp_count:
                piece = (piece.astype(f32) + flip_dp(piece, bit).astype(f32)).astype(bf16)
                bit *= 2
            return piece

        def gather(self, piece):
            self.parts = [[piece], [piece]]
            self.pass_parts()

        def pass_parts(self):
            for way, parts in zip((1, -1), self.parts):
                value = parts[-1]
                if len(parts) == 4:
                    cut = (lambda v: v[: self.split]) if way == 1 else (lambda v: v[self.split :])
                    value = step(cut, value)
                parts.append(pass_on(value, way))

        def result(self):
            fwd, bwd = self.parts
            return [fwd[0], *fwd[1:4], *bwd[1:4], fwd[4], bwd[4]]

    hid = [f[1] for f in ffn]
    cots = [f[3] for f in ffn]
    n2 = [f[0] for f in ffn]
    gp = [f[2] for f in ffn]
    grad_o = step(two(hid, cots), hid[0])
    grad_i = step(two(n2, gp), n2[0])
    ffn_ring = Ring(load_ffn_chunk, D // RING, 2 * D // RING, [grad_o, grad_i])
    ffn_ring.step()
    back = []

    def run_back(m):
        x, n1, qc, qp, k, v, va, gate, prob, att, mix, stat = saved[m]
        from_far = [ffn[m][4], w_out_heads, gate, att, prob, v, k, qc, qp, va, wt, x, stat]
        back.append(
            kernel(
                back_kernel,
                [
                    out((length, D), bf16),
                    out((8, D), f32),
                    out((length, PACK), bf16),
                    out((length, LANE), f32),
                    out((8, LANE), f32),
                    out((own, D), f32),
                    out((2, own, D), bf16),
                    out((2, own, D), bf16),
                ],
                [ffn[m][5], *gn2[m], ffn[m][3], vec, pos] + [Far(a) for a in from_far],
                copies=13,
                scratch=vmem_of(from_far)
                + [
                    pltpu.VMEM((length, LANE), bf16),
                    pltpu.VMEM((length, LANE), f32),
                    pltpu.VMEM((length, LANE), f32),
                    pltpu.VMEM((length, LANE), f32),
                    pltpu.VMEM((length, D), bf16),
                ],
                flops=2 * length * D * 2000,
            )
        )

    def own_rows(keep, send):
        got = flip_shard(send, 1)
        far_part = step(lambda k, g: (k[1].astype(f32) + g[1].astype(f32)).astype(bf16), keep, got)
        return keep, got, flip_shard(far_part, 2)

    def project(m):
        keep, send = kernel(
            project_kernel,
            [out((2, own, D), bf16)] * 2,
            [ffn[m][1], ffn_out],
            scratch=[pltpu.VMEM((length, D), bf16)],
            flops=2 * length * D * D,
        )
        return own_rows(keep, send)

    run_back(0)
    ffn_ring.step()
    run_back(1)
    ffn_ring.step()
    dproj = [b[2] for b in back]
    gb = [b[0] for b in back]
    n1 = [r[1] for r in saved]
    mix = [r[10] for r in saved]
    grad_p = step(two(dproj, n1), dproj[0])
    gpos = step(lambda a, b: (a + b).astype(bf16), back[0][3], back[1][3])
    grad_p = step(
        lambda g: lax.dynamic_update_slice(g, mm(gpos, sine, TN), (2 * LANE, 0)), grad_p
    )
    grad_w = step(two(mix, gb), mix[0])
    tails = kernel(
        vectors_kernel,
        [out((RING, TAIL, D), f32)],
        [back[0][1], back[1][1], back[0][4], back[1][4], ffn[0][7], ffn[1][7]],
    )[0]
    pack_ring = Ring(
        load_pack_chunk, DH, D // RING + E * LANE // RING, [grad_p, grad_w, tails]
    )
    pack_ring.step()
    ffn_ring.step()
    gx = [own_rows(back[m][6], back[m][7]) for m in range(micro)]
    pack_ring.step()
    piece = ffn_ring.step()
    rows8 = D // RING
    parts = swap_shard(piece[rows8:], rank, rows8 // H, 0)
    ffn_piece = step(lambda p, *more: jnp.concatenate([p[:rows8], *more]), piece, *parts)
    ffn_ring.gather(ffn_piece)
    pack_ring.step()
    outputs = [project(m) for m in range(micro)]
    ffn_ring.pass_parts()
    pack_ring.step()
    grads_x = [
        kernel(
            functools.partial(input_kernel, m),
            [out((own, D), f32)],
            [x_own, back[m][5], *gx[m], vec],
        )[0]
        for m in range(micro)
    ]
    ffn_ring.pass_parts()
    piece = pack_ring.step()
    parts = swap_shard(piece[:rows8], rank, quarter, 1)
    pack_piece = step(
        lambda p, *more: jnp.concatenate([jnp.concatenate(more, axis=1), p[rows8:]]), piece, *parts
    )
    pack_ring.gather(pack_piece)
    outputs = [
        kernel(
            functools.partial(output_kernel, m),
            [out((own, D), bf16)],
            [ffn[m][6], *outputs[m], vec],
        )[0]
        for m in range(micro)
    ]
    ffn_ring.pass_parts()
    pack_ring.pass_parts()
    pack_ring.pass_parts()
    g_out, g_in = kernel(
        functools.partial(ffn_grads_kernel, ffn_ring.split),
        [Far(out((FF // H, D), f32)), Far(out((quarter, FF), f32))],
        [Far(p) for p in ffn_ring.result()],
        second=place,
        scratch=[
            pltpu.VMEM((RING, ffn_ring.total, D), bf16),
            pltpu.VMEM((FF // H, D), f32),
            pltpu.VMEM((quarter, FF), f32),
        ],
        copies=25,
    )
    pack_ring.pass_parts()
    res = kernel(
        functools.partial(pack_grads_kernel, pack_ring.split),
        [
            out((H * DH, quarter), f32),
            out((H * E, quarter), f32),
            out((H * E, quarter), f32),
            out((H * DH, quarter), f32),
            out((H * DH, quarter), f32),
            out((H * E * DH, quarter), f32),
            out((E * DH, D), f32),
        ]
        + [out((quarter,), f32)] * 5
        + [out((DH,), f32)] * 2
        + [out((FF // H,), f32)],
        [Far(p) for p in pack_ring.result()],
        second=place,
        scratch=[
            pltpu.VMEM((RING, pack_ring.total, D), bf16),
            pltpu.VMEM((H, RING, LANE, quarter), f32),
        ],
        copies=9,
    )
    g_q, g_rv, g_ro, g_k, g_p, g_v, g_wo, g1, b1, g2, b2, bo, content, posb, bi = res
    return (
        jnp.stack(outputs)[:, None],
        jnp.stack(grads_x)[:, None],
        g1,
        b1,
        g_q.T,
        g_k.T,
        g_p.T,
        content,
        posb,
        g_rv.T,
        g_ro.T,
        g_v.T,
        g_wo,
        g2,
        b2,
        g_in,
        bi,
        g_out,
        bo,
    )


def solution(mesh):
    tokens = P(None, "dp", "shard")
    whole = P(None, "dp", "shard", None)
    routes = P(None, "dp", "shard", None, None)
    vector = P("shard")
    matrix = P("shard", None)
    weights = (
        vector,
        vector,
        matrix,
        matrix,
        matrix,
        vector,
        vector,
        matrix,
        matrix,
        matrix,
        matrix,
        vector,
        vector,
        matrix,
        vector,
        matrix,
        vector,
    )
    return jax.shard_map(
        local,
        mesh=mesh,
        in_specs=(whole, tokens, tokens, routes, routes) + weights + (whole,),
        out_specs=(whole, whole) + weights,
        check_vma=False,
    )
```

```python
import functools
import math

import jax
import jax.numpy as jnp
from jax import lax
from jax.experimental import pallas as pl
from jax.experimental.pallas import tpu as pltpu
from jax.sharding import PartitionSpec as P

D = 1024
H = 4
DH = 112
E = 5
FF = 4096
LANE = 128
PACK = 1024
BLK = 128
RING = 8
TAIL = 8
MASKED = -1e30
SCALE = DH ** (-0.5)
bf16 = jnp.bfloat16
f32 = jnp.float32
NN = (((1,), (0,)), ((), ()))
NT = (((1,), (1,)), ((), ()))
TN = (((0,), (0,)), ((), ()))


def mm(a, b, dims=NN):
    return lax.dot_general(a, b, dims, preferred_element_type=f32)


def call(kernel, outs, args, scratch=(), copies=0, flops=0, vmem=12, smem=2, deps=(), into=None):
    in_specs, arrays = [], []
    args = list(args)
    count = len(args)
    into = into or {}
    deps = [*deps, *into.values()]
    aliases = {count + len(deps) - len(into) + n: i for n, i in enumerate(into)}
    args += [Far(d, pl.ANY) for d in deps]
    body = lambda *refs: kernel(*refs[:count], *refs[count + len(deps) :])
    for i, arg in enumerate(args):
        far = isinstance(arg, Far)
        space = pltpu.SMEM if i < smem else arg.space if far else pltpu.VMEM
        in_specs.append(pl.BlockSpec(memory_space=space))
        arrays.append(arg.value if far else arg)
    out_specs, out_shapes = [], []
    for o in outs:
        far = isinstance(o, Far)
        out_specs.append(pl.BlockSpec(memory_space=o.space if far else pltpu.VMEM))
        out_shapes.append(o.value if far else o)
    moved = sum(math.prod(a.shape) * a.dtype.itemsize for a in arrays + out_shapes)
    scratch = list(scratch)
    if copies:
        scratch.append(pltpu.SemaphoreType.DMA((copies,)))
    return pl.pallas_call(
        body if deps else kernel,
        out_shape=out_shapes,
        in_specs=in_specs,
        out_specs=out_specs,
        scratch_shapes=scratch,
        compiler_params=pltpu.CompilerParams(vmem_limit_bytes=vmem << 20),
        input_output_aliases=aliases,
        cost_estimate=pl.CostEstimate(flops=0, bytes_accessed=0, transcendentals=0),
    )(*arrays)


class Far:
    def __init__(self, value, space=pltpu.HBM):
        self.value, self.space = value, space


class Copies:
    def __init__(self, sems):
        self.sems, self.count, self.left = sems, 0, []

    def start(self, src, dst):
        copy = pltpu.make_async_copy(src, dst, self.sems.at[self.count])
        self.count += 1
        copy.start()
        self.left.append(copy)
        return copy

    def wait(self, *copies):
        for copy in copies:
            copy.wait()
            self.left.remove(copy)

    def finish(self):
        self.wait(*list(self.left))


def gate(value, deps):
    return pl.pallas_call(
        lambda *refs: None,
        out_shape=jax.ShapeDtypeStruct(value.shape, value.dtype),
        in_specs=[pl.BlockSpec(memory_space=pl.ANY)] * (1 + len(deps)),
        out_specs=pl.BlockSpec(memory_space=pl.ANY),
        input_output_aliases={0: 0},
        cost_estimate=pl.CostEstimate(flops=0, bytes_accessed=0, transcendentals=0),
    )(value, *deps)


def out(shape, dtype):
    return jax.ShapeDtypeStruct(shape, dtype)


def prep_kernel(rank_ref, side_ref, *refs):
    count = 18
    (x_hbm, win_hbm), refs = refs[:2], refs[2:]
    ins, outs, scratch = refs[:count], refs[count : count + 6], refs[count + 6 :]
    (core_hbm, near2_hbm, near3_hbm, *x_outs), scratch = scratch[:5], scratch[5:]
    held, (marks_ref, pack_ref, sems) = scratch[:count], scratch[count:]
    copies = Copies(sems)
    loads = [copies.start(src, dst) for src, dst in zip(ins, held)]
    for m, ref in enumerate(x_outs):
        copies.start(x_hbm.at[m, 0], ref)
    width = win_hbm.shape[1] // H
    size = win_hbm.shape[0] // 2
    for r, ref in ((1, core_hbm), (2, near2_hbm), (3, near3_hbm)):
        cols = pl.ds(pl.multiple_of((rank_ref[0] ^ r) * width, width), width)
        rows = pl.ds(pl.multiple_of((side_ref[0] % 2) * size, size), size) if r > 1 else slice(0, 2 * size)
        copies.start(win_hbm.at[rows, cols], ref)
    copies.wait(*loads)
    q_ref, k_ref, p_ref, rv_ref, ro_ref, v_ref, routes_v_ref, routes_o_ref = held[:8]
    seg_ref, pad_ref, g1_ref, b1_ref, g2_ref, b2_ref, bo_ref, cb_ref, pb_ref, bi_ref = held[8:]
    head_ref, bin_ref = outs[4:]
    head_ref[...] = jnp.zeros(head_ref.shape, f32)
    head_ref[0:1, 0:DH] = cb_ref[...].astype(f32).reshape(1, -1)
    head_ref[1:2, 0:DH] = pb_ref[...].astype(f32).reshape(1, -1)
    bin_ref[...] = bi_ref[...].astype(f32).reshape(1, -1)
    micro, own = seg_ref.shape[0], seg_ref.shape[2]
    marks_ref[...] = jnp.zeros(marks_ref.shape, f32)
    copied = [slice(0, own), slice(own, 2 * own)]
    for m in range(micro):
        for cols in copied:
            marks_ref[4 * m + 2 : 4 * m + 3, cols] = seg_ref[m].astype(f32)
            marks_ref[4 * m + 3 : 4 * m + 4, cols] = pad_ref[m].astype(f32)
    for i, ref in enumerate((g1_ref, b1_ref, g2_ref, b2_ref, bo_ref)):
        marks_ref[4 * micro + i : 4 * micro + i + 1, :] = ref[...].astype(f32).reshape(1, -1)
    row = lax.broadcasted_iota(jnp.int32, (16, H * E), 0)
    col = lax.broadcasted_iota(jnp.int32, (16, H * E), 1)
    for r in range(H):
        out_ref = outs[r] if r < 2 else pack_ref
        h = rank_ref[0] ^ r
        rows = pl.ds(pl.multiple_of(h * DH, 16), DH)
        for m in range(micro):
            for i, ref in enumerate((routes_v_ref, routes_o_ref)):
                ones = lax.shift_left(jnp.ones((2, own), jnp.int32), ref[m, h])
                code = jnp.sum(ones.astype(f32), axis=0, keepdims=True)
                for cols in copied:
                    marks_ref[4 * m + i : 4 * m + i + 1, cols] = code
        pick_v = jnp.where((row < E) & (col == h * E + row), 1.0, 0.0).astype(bf16)
        pick_o = jnp.where((row >= E) & (row < 2 * E) & (col == h * E + row - E), 1.0, 0.0)
        routers = mm(pick_v, rv_ref[...]) + mm(pick_o.astype(bf16), ro_ref[...])
        out_ref[0:DH, :] = q_ref[rows, :]
        out_ref[DH:LANE, :] = routers.astype(bf16)
        out_ref[LANE : LANE + DH, :] = k_ref[rows, :]
        out_ref[LANE + DH : 2 * LANE, :] = marks_ref[...].astype(bf16)
        out_ref[2 * LANE : 2 * LANE + DH, :] = p_ref[rows, :]
        out_ref[2 * LANE + DH : 3 * LANE, :] = jnp.zeros((LANE - DH, out_ref.shape[1]), bf16)
        for e in range(E):
            at = (3 + e) * LANE
            expert = pl.ds(pl.multiple_of((h * E + e) * DH, 16), DH)
            out_ref[at : at + DH, :] = v_ref[expert, :]
            out_ref[at + DH : at + LANE, :] = jnp.zeros((LANE - DH, out_ref.shape[1]), bf16)
        if r >= 2:
            half = pl.ds(pl.multiple_of((side_ref[0] % 2) * LANE, LANE), LANE)
            outs[r][...] = pack_ref[:, half]
    copies.finish()


def norm_stats(x):
    mean = jnp.mean(x, axis=-1, keepdims=True)
    centred = x - mean
    var = jnp.mean(centred * centred, axis=-1, keepdims=True)
    rstd = lax.rsqrt(var + 1e-05)
    return centred * rstd, rstd


def norm_back(grad, unit, rstd, gain):
    g = grad * gain
    return rstd * (
        g
        - jnp.mean(g, axis=-1, keepdims=True)
        - unit * jnp.mean(g * unit, axis=-1, keepdims=True)
    )


def x_send_keep(held, x_hbm, send_hbm, keep_hbm):
    return held[0], held[1], x_hbm, send_hbm, keep_hbm


def attention_kernel(m, rank_ref, side_ref, *refs):
    first = m == 0
    (x0, x1, x2, x3), refs = refs[:4], refs[4:]
    head_ref, refs = refs[0], refs[1:]
    if first:
        (w0, w1, near2, near3, far2, far3, sine_hbm, wo_hbm), refs = refs[:8], refs[8:]
    else:
        (wt_hbm, wo_hbm, pos_ref, vec_ref, rows_ref), refs = refs[:5], refs[5:]
    (x_ref, n_hbm, qc_hbm, qp_hbm, k_hbm, v_hbm, va_hbm, gate_hbm, p_hbm, att_hbm), refs = (
        refs[:10],
        refs[10:],
    )
    (mix_hbm, stat_ref), refs = refs[:2], refs[2:]
    (send_ref, keep_ref), refs = refs[:2], refs[2:]
    if first:
        (wt_hbm, wop_hbm, pos_ref, vec_ref, rows_ref), refs = refs[:5], refs[5:]
    n_ref, qc_ref, qp_ref, k_ref, v_ref, va_ref, gate_ref, p_ref, att_ref, mix_ref = refs[:10]
    wt_ref, wo_ref, x_out, send_out, keep_out = x_send_keep(refs[10:15], x_ref, send_ref, keep_ref)
    x_ref, send_ref, keep_ref = refs[12:15]
    sine_ref = refs[15] if first else None
    copies = Copies(refs[-1])
    length = x_ref.shape[0]
    both = slice(m * length, (m + 1) * length)
    blocks = length // BLK
    rank = rank_ref[0]
    quarter = D // H

    def at(r, size):
        return pl.ds(pl.multiple_of((rank ^ r) * size, size), size)

    loads = [copies.start(x0.at[m], x_ref.at[at(0, BLK), :])]
    loads += [copies.start(ref, x_ref.at[at(r, BLK), :]) for r, ref in enumerate((x1, x2, x3), 1)]
    if first:
        side = side_ref[0] % 2
        for r, ref in enumerate((w0, w1)):
            loads.append(copies.start(ref, wt_ref.at[:, at(r, quarter)]))
        for r, place, ref in (
            (2, side, near2),
            (3, side, near3),
            (2, 1 - side, far2),
            (3, 1 - side, far3),
        ):
            cols = pl.ds(pl.multiple_of((rank ^ r) * quarter + place * LANE, LANE), LANE)
            loads.append(copies.start(ref, wt_ref.at[:, cols]))
        sine_load = copies.start(sine_hbm, sine_ref)
        wo_loads = []
        for e in range(E):
            rows = slice(e * LANE, e * LANE + DH)
            wo_loads.append(copies.start(wo_hbm.at[e * DH : (e + 1) * DH, :], wo_ref.at[rows, :]))
            wo_ref[e * LANE + DH : (e + 1) * LANE, :] = jnp.zeros((LANE - DH, D), bf16)
        copies.wait(*loads)
        vec_ref[...] = jnp.zeros(vec_ref.shape, f32)
        rows_ref[...] = jnp.zeros(rows_ref.shape, f32)
        for r in range(H):
            micro = rows_ref.shape[0]
            marks = wt_ref[LANE + DH : 2 * LANE, at(r, quarter)].astype(f32)
            vec_ref[0:5, at(r, quarter)] = marks[4 * micro : 4 * micro + 5, :]
            fresh = pl.ds(pl.multiple_of((rank ^ r) * quarter + side * LANE, LANE), LANE)
            marks = wt_ref[LANE + DH : 2 * LANE, fresh].astype(f32)
            for i in range(micro):
                part = marks[4 * i : 4 * i + 4, :]
                rows_ref[i, 0:1, at(r, BLK)] = part[0:1, :] + 2.0**E * part[1:2, :]
                rows_ref[i, 1:3, at(r, BLK)] = part[2:4, :]
        copies.start(wt_ref, wt_hbm)
    else:
        wt_load = copies.start(wt_hbm, wt_ref)
        wo_loads = [copies.start(wo_hbm, wo_ref)]
        copies.wait(*loads)

    @pl.loop(0, blocks)
    def _(b):
        rows = pl.ds(pl.multiple_of(b * BLK, BLK), BLK)
        x = x_ref[rows, :].astype(f32)
        unit, rstd = norm_stats(x)
        n_ref[rows, :] = (unit * vec_ref[0:1, :] + vec_ref[1:2, :]).astype(bf16)
        first_lane = lax.broadcasted_iota(jnp.int32, (BLK, LANE), 1) == 0
        stat_ref[rows, :] = jnp.where(first_lane, jnp.mean(x, axis=-1, keepdims=True), rstd)

    copies.start(x_ref, x_out)
    copies.start(n_ref, n_hbm.at[both, :])
    if first:
        copies.wait(sine_load)
        pos_ref[...] = mm(sine_ref[...], wt_ref[2 * LANE : 3 * LANE, :], NT).astype(bf16)
    else:
        copies.wait(wt_load)
    lane = lax.broadcasted_iota(jnp.int32, (1, LANE), 1)
    is_head = lane < DH
    raw = mm(n_ref[...], wt_ref[0:LANE, :], NT)
    columns = rows_ref[m].T
    code = jnp.broadcast_to(columns[:, 0:1].astype(jnp.int32), (length, LANE))
    slot = jnp.where((lane >= DH) & (lane < DH + 2 * E), lane - DH, 31)
    pick = (lax.shift_right_logical(code, jnp.broadcast_to(slot, (length, LANE))) & 1) == 1
    gate = jnp.where(pick, 1.0 / (1.0 + jnp.exp(-raw)), 0.0)
    gate_ref[...] = gate
    copies.start(gate_ref, gate_hbm)
    qc_ref[...] = jnp.where(is_head, (raw + head_ref[0:1, :]) * SCALE, 0.0).astype(bf16)
    qp_ref[...] = jnp.where(is_head, (raw + head_ref[1:2, :]) * SCALE, 0.0).astype(bf16)
    keys = mm(n_ref[...], wt_ref[LANE : 2 * LANE, :], NT)
    k_ref[...] = jnp.where(is_head, keys, 0.0).astype(bf16)
    values = jnp.zeros((length, LANE), f32)
    for e in range(E):
        part = mm(n_ref[...], wt_ref[(3 + e) * LANE : (4 + e) * LANE, :], NT)
        va_ref[:, e * LANE : (e + 1) * LANE] = part.astype(bf16)
        values += part * gate[:, DH + e : DH + e + 1]
    v_ref[...] = values.astype(bf16)
    for src, dst in ((qc_ref, qc_hbm), (qp_ref, qp_hbm), (k_ref, k_hbm), (v_ref, v_hbm), (va_ref, va_hbm)):
        copies.start(src, dst)
    seg_col = columns[:, 1:2]
    for b in range(blocks):
        rows = slice(b * BLK, (b + 1) * BLK)
        wide = (b + 1) * BLK
        content = mm(qc_ref[rows, :], k_ref[0:wide, :], NT)
        table = mm(qp_ref[rows, :], pos_ref[length - wide : length, :], NT)
        table = pltpu.roll(table, (wide - BLK + 1) % wide, 1, stride=1, stride_axis=0)
        row = lax.broadcasted_iota(jnp.int32, (BLK, wide), 0) + b * BLK
        col = lax.broadcasted_iota(jnp.int32, (BLK, wide), 1)
        same = seg_col[rows, :] == rows_ref[m, 1:2, 0:wide]
        live = ((rows_ref[m, 2:3, 0:wide] > 0.0) & (col < row)) | (col == row)
        scores = jnp.where(same & live, content + table, MASKED)
        top = jnp.max(scores, axis=-1, keepdims=True)
        expo = jnp.exp(scores - top)
        prob = (expo / jnp.sum(expo, axis=-1, keepdims=True)).astype(bf16)
        p_ref[rows, 0:wide] = prob
        att = mm(prob, v_ref[0:wide, :])
        att_ref[rows, :] = att
        for e in range(E):
            share = gate_ref[rows, DH + E + e : DH + E + e + 1]
            mix_ref[rows, e * LANE : (e + 1) * LANE] = (att * share).astype(bf16)
        copies.start(p_ref.at[rows, 0:wide], p_hbm.at[rows, 0:wide])
    copies.start(att_ref, att_hbm)
    copies.start(mix_ref, mix_hbm.at[both, :])
    half = length // 2
    core = rank & 1
    copies.wait(*wo_loads)
    if first:
        copies.start(wo_ref, wop_hbm)
    for place, ref, dst in ((1 - core, send_ref, send_out), (core, keep_ref, keep_out)):
        rows = pl.ds(pl.multiple_of(place * half, half), half)
        ref[...] = mm(mix_ref[rows, :], wo_ref[...]).astype(bf16)
        copies.start(ref, dst)
    copies.finish()


def normal_terms(v):
    bell = jnp.exp(-0.5 * v * v)
    phi = 0.5 * (1.0 + lax.erf(v * (1.0 / math.sqrt(2.0))))
    return phi, bell * (1.0 / math.sqrt(2.0 * math.pi))


def pair_rows(core, b, refs):
    mine, far, mine2, far2 = refs
    own_half = (b // 2) == core
    rows = pl.ds(pl.multiple_of((b % 2) * BLK, BLK), BLK)
    near = mine[rows, :].astype(f32) + far[rows, :].astype(f32)
    away = mine2[rows, :].astype(f32) + far2[rows, :].astype(f32)
    return jnp.where(own_half, near, away)


def ffn_kernel(
    m,
    rank_ref,
    side_ref,
    x_hbm,
    a0,
    a1,
    a2,
    a3,
    vec_ref,
    bin_ref,
    win_hbm,
    win_core,
    *refs,
):
    (near2, near3, far2, far3), refs = refs[:4], refs[4:]
    (wout_hbm, c0, c1, c2, c3), refs = refs[:5], refs[5:]
    (n_hbm, hid_hbm, gp_hbm, cot_hbm, unit_hbm, rstd_ref, resid_ref, sum_ref), refs = (
        refs[:8],
        refs[8:],
    )
    (send_hbm, keep_hbm), refs = refs[:2], refs[2:]
    (unit_ref, win_ref, wout_ref, x_ref, n_ref, hid_ref, gp_ref, cot_ref), refs = refs[:8], refs[8:]
    halves, (send_ref, keep_ref, sems) = refs[:4], refs[4:]
    length = x_ref.shape[0]
    both = slice(m * length, (m + 1) * length)
    rank, place = rank_ref[0], side_ref[0]
    core = rank & 1
    copies = Copies(sems)
    size = D // H
    sum_ref[...] = jnp.zeros(sum_ref.shape, f32)

    def at(r, size):
        return pl.ds(pl.multiple_of((rank ^ r) * size, size), size)

    early = [copies.start(x_hbm, x_ref)]
    early += [copies.start(src, dst) for src, dst in zip((a0, a1, a2, a3), halves)]
    loads = []
    width = win_ref.shape[1]
    own_cols = pl.ds(pl.multiple_of(rank * width, width), width)
    loads.append(copies.start(win_hbm.at[:, own_cols], win_ref.at[at(0, size), :]))
    loads.append(copies.start(win_core, win_ref.at[at(1, size), :]))
    side = place % 2
    for r, half, ref in ((2, side, near2), (3, side, near3), (2, 1 - side, far2), (3, 1 - side, far3)):
        rows = pl.ds(pl.multiple_of((rank ^ r) * size + half * (size // 2), size // 2), size // 2)
        loads.append(copies.start(ref, win_ref.at[rows, :]))
    loads.append(copies.start(wout_hbm, wout_ref))
    for r, ref in enumerate((c0, c1, c2, c3)):
        loads.append(copies.start(ref.at[m], cot_ref.at[at(r, BLK), :]))

    copies.wait(*early)

    @pl.loop(0, length // BLK)
    def _(b):
        rows = pl.ds(pl.multiple_of(b * BLK, BLK), BLK)
        resid = x_ref[rows, :].astype(f32) + pair_rows(core, b, halves)
        unit, rstd = norm_stats(resid)
        unit_ref[rows, :] = unit.astype(bf16)
        rstd_ref[rows, :] = jnp.broadcast_to(rstd, (BLK, LANE))
        n_ref[rows, :] = (unit * vec_ref[2:3, :] + vec_ref[3:4, :]).astype(bf16)

        @pl.when(b == rank)
        def _():
            resid_ref[...] = resid

    copies.wait(*loads)
    for src, dst in (
        (unit_ref, unit_hbm),
        (n_ref, n_hbm.at[both, :]),
        (cot_ref, cot_hbm.at[both, :]),
    ):
        copies.start(src, dst)
    chunk = 256

    @pl.loop(0, width // chunk)
    def _(c):
        cols = pl.ds(pl.multiple_of(c * chunk, chunk), chunk)
        pre = mm(n_ref[...], win_ref[:, cols]) + bin_ref[0:1, cols]
        back = mm(cot_ref[...], wout_ref[cols, :], NT)
        phi, density = normal_terms(pre)
        hid_ref[:, cols] = (pre * phi).astype(bf16)
        grad = (back * (phi + pre * density)).astype(bf16)
        gp_ref[:, cols] = grad
        sum_ref[0:1, cols] = jnp.sum(grad.astype(f32), axis=0, keepdims=True)

    copies.start(hid_ref, hid_hbm.at[both, :])
    copies.start(gp_ref, gp_hbm.at[both, :])
    half = length // 2
    for place, ref, dst in ((1 - core, send_ref, send_hbm), (core, keep_ref, keep_hbm)):
        rows = pl.ds(pl.multiple_of(place * half, half), half)
        ref[...] = mm(gp_ref[rows, :], win_ref[...], NT).astype(bf16)
        copies.start(ref, dst)
    copies.finish()


def split_blocks(rank, value_ref, keep_ref, send_ref):
    for r in range(H):
        rows = pl.ds(pl.multiple_of((rank ^ r) * BLK, BLK), BLK)
        (send_ref if r % 2 else keep_ref)[r // 2] = value_ref[rows, :]


def project_kernel(rank_ref, side_ref, hid_hbm, wout_hbm, keep_hbm, send_hbm, *refs):
    hid_ref, wout_ref, full_ref, keep_ref, send_ref, sems = refs
    copies = Copies(sems)
    loads = [copies.start(wout_hbm, wout_ref), copies.start(hid_hbm, hid_ref)]
    copies.wait(*loads)
    full_ref[...] = mm(hid_ref[...], wout_ref[...]).astype(bf16)
    micro = keep_ref.shape[1]
    length = full_ref.shape[0] // micro
    for m in range(micro):
        for r in range(H):
            at = pl.multiple_of((rank_ref[0] ^ r) * BLK + m * length, BLK)
            ref = send_ref if r % 2 else keep_ref
            ref[r // 2, m] = full_ref[pl.ds(at, BLK), :]
    copies.start(keep_ref, keep_hbm)
    copies.start(send_ref, send_hbm)
    copies.finish()


def branch_kernel(m, rank_ref, side_ref, vec_ref, rstd_ref, gate_ref, att_ref, *refs):
    hbm, refs = refs[:7], refs[7:]
    (gb_hbm, sums_ref, grad_ref, ga_ref, logit_ref), refs = refs[:5], refs[5:]
    held, (gb_ref, sems) = refs[:7], refs[7:]
    copies = Copies(sems)
    *halves, cot_ref, unit_ref, wo_ref = held
    length = unit_ref.shape[0]
    both = slice(m * length, (m + 1) * length)
    hbm = [*hbm[:4], hbm[4].at[both, :], *hbm[5:]]
    *loads, wo_load = [copies.start(src, dst) for src, dst in zip(hbm, held)]
    rank = rank_ref[0]
    core = rank & 1
    sums_ref[...] = jnp.zeros(sums_ref.shape, f32)
    copies.wait(*loads)

    @pl.loop(0, length // BLK)
    def _(b):
        rows = pl.ds(pl.multiple_of(b * BLK, BLK), BLK)
        unit = unit_ref[rows, :].astype(f32)
        grad = pair_rows(core, b, halves)
        sums_ref[0:1, :] += jnp.sum(grad * unit, axis=0, keepdims=True)
        sums_ref[1:2, :] += jnp.sum(grad, axis=0, keepdims=True)
        cot = cot_ref[rows, :].astype(f32)
        sums_ref[2:3, :] += jnp.sum(cot, axis=0, keepdims=True)
        total = cot + norm_back(grad, unit, rstd_ref[rows, 0:1], vec_ref[2:3, :])
        gb_ref[rows, :] = total.astype(bf16)

        @pl.when(b == rank)
        def _():
            grad_ref[...] = total

    copies.start(gb_ref, gb_hbm.at[both, :])
    copies.wait(wo_load)
    lane = lax.broadcasted_iota(jnp.int32, (1, LANE), 1)
    acc = jnp.zeros((length, LANE), f32)
    logits = jnp.zeros((length, LANE), f32)
    for e in range(E):
        mixed = mm(gb_ref[...], wo_ref[e * LANE : (e + 1) * LANE, :], NT)
        acc += mixed * gate_ref[:, DH + E + e : DH + E + e + 1]
        dot = jnp.sum(mixed * att_ref[...], axis=-1, keepdims=True)
        logits = jnp.where(lane == DH + E + e, dot, logits)
    ga_ref[...] = acc.astype(bf16)
    logit_ref[...] = logits
    copies.finish()


def back_kernel(m, rank_ref, side_ref, ga_ref, logit_ref, pos_ref, gate_ref, stat_ref, *refs):
    hbm, refs = refs[:8], refs[8:]
    (sums_ref, dproj_hbm, gpos_ref, bias_ref, keep_hbm, send_hbm), refs = refs[:6], refs[6:]
    held, refs = refs[:8], refs[8:]
    dproj_ref, gk_ref, gv_ref, full_ref, keep_ref, send_ref, sems = refs
    copies = Copies(sems)
    *loads, va_load, wt_load, x_load = [copies.start(src, dst) for src, dst in zip(hbm, held)]
    p_ref, v_ref, k_ref, qc_ref, qp_ref, va_ref, wt_ref, x_ref = held
    length = x_ref.shape[0]
    blocks = length // BLK
    rank = rank_ref[0]
    lane = lax.broadcasted_iota(jnp.int32, (1, LANE), 1)
    sums_ref[...] = jnp.zeros(sums_ref.shape, f32)
    gk_ref[...] = jnp.zeros(gk_ref.shape, f32)
    gv_ref[...] = jnp.zeros(gv_ref.shape, f32)
    gpos_ref[...] = jnp.zeros(gpos_ref.shape, f32)
    row = lax.broadcasted_iota(jnp.int32, (BLK, BLK), 0)
    col = lax.broadcasted_iota(jnp.int32, (BLK, BLK), 1)
    mirror = jnp.where(row + col == BLK - 1, 1.0, 0.0).astype(bf16)
    cont_sum = jnp.zeros((1, LANE), f32)
    posn_sum = jnp.zeros((1, LANE), f32)
    copies.wait(*loads)
    for b in range(blocks):
        rows = slice(b * BLK, (b + 1) * BLK)
        wide = (b + 1) * BLK
        prob = p_ref[rows, 0:wide].astype(f32)
        ga = ga_ref[rows, :]
        grad_prob = mm(ga, v_ref[0:wide, :], NT)
        delta = jnp.sum(prob * grad_prob, axis=-1, keepdims=True)
        grad_score = (prob * (grad_prob - delta)).astype(bf16)
        gv_ref[0:wide, :] += mm(p_ref[rows, 0:wide], ga, TN)
        gk_ref[0:wide, :] += mm(grad_score, qc_ref[rows, :], TN)
        cont = mm(grad_score, k_ref[0:wide, :]) * SCALE
        table = pltpu.roll(mm(mirror, grad_score), 0, 1, stride=1, stride_axis=0)
        table = mm(mirror, table.astype(bf16)).astype(bf16)
        posn = mm(table, pos_ref[length - wide : length, :]) * SCALE
        gpos_ref[length - wide : length, :] += mm(table, qp_ref[rows, :], TN)
        cont_sum += jnp.sum(cont, axis=0, keepdims=True)
        posn_sum += jnp.sum(posn, axis=0, keepdims=True)
        dproj_ref[rows, 0:LANE] = (cont + posn).astype(bf16)
    bias_ref[...] = jnp.zeros(bias_ref.shape, f32)
    bias_ref[0:1, :] = cont_sum
    bias_ref[1:2, :] = posn_sum
    dproj_ref[:, LANE : 2 * LANE] = gk_ref[...].astype(bf16)
    dproj_ref[:, 2 * LANE : 3 * LANE] = jnp.zeros((length, LANE), bf16)
    copies.wait(va_load, wt_load, x_load)
    grad_values = gv_ref[...].astype(bf16).astype(f32)
    logits = logit_ref[...]
    for e in range(E):
        cols = slice((3 + e) * LANE, (4 + e) * LANE)
        dproj_ref[:, cols] = (grad_values * gate_ref[:, DH + e : DH + e + 1]).astype(bf16)
        dot = jnp.sum(grad_values * va_ref[:, e * LANE : (e + 1) * LANE].astype(f32), axis=-1, keepdims=True)
        logits = jnp.where(lane == DH + e, dot, logits)
    gate = gate_ref[...]
    logits = logits * gate * (1.0 - gate)
    dproj_ref[:, 0:LANE] = jnp.where(
        lane < DH, dproj_ref[:, 0:LANE].astype(f32), logits
    ).astype(bf16)
    copies.start(dproj_ref, dproj_hbm.at[m * length : (m + 1) * length, :])
    chunk = 256
    mean, rstd = stat_ref[:, 0:1], stat_ref[:, 1:2]

    @pl.loop(0, D // chunk)
    def _(c):
        cols = pl.ds(pl.multiple_of(c * chunk, chunk), chunk)
        part = mm(dproj_ref[...], wt_ref[:, cols])
        full_ref[:, cols] = part.astype(bf16)
        unit = (x_ref[:, cols].astype(f32) - mean) * rstd
        sums_ref[3:4, cols] = jnp.sum(part * unit, axis=0, keepdims=True)
        sums_ref[4:5, cols] = jnp.sum(part, axis=0, keepdims=True)

    split_blocks(rank, full_ref, keep_ref, send_ref)
    copies.start(send_ref, send_hbm)
    copies.start(keep_ref, keep_hbm)
    copies.finish()


def output_kernel(rank_ref, side_ref, vec_ref, keep_ref, got_ref, far_ref, *refs):
    y_ref = refs[-1]
    for m in range(y_ref.shape[0]):
        total = refs[m][...] + keep_ref[0, m].astype(f32) + got_ref[0, m].astype(f32)
        y_ref[m, 0] = (total + far_ref[m].astype(f32) + vec_ref[4:5, :]).astype(bf16)


def input_kernel(rank_ref, side_ref, x_ref, vec_ref, far_ref, *refs):
    y_ref = refs[-1]
    for m in range(y_ref.shape[0]):
        grad_ref, keep_ref, got_ref = refs[3 * m : 3 * m + 3]
        unit, rstd = norm_stats(x_ref[m].astype(f32))
        back = keep_ref[0].astype(f32) + got_ref[0].astype(f32) + far_ref[m].astype(f32)
        y_ref[m, 0] = grad_ref[...] + norm_back(back, unit, rstd, vec_ref[0:1, :])


def vectors_kernel(
    rank_ref, side_ref, sums0, sums1, norm0, norm1, bias0, bias1, hid0, hid1, y_ref
):
    y_ref[...] = jnp.zeros(y_ref.shape, f32)
    width = D // H
    own = pl.ds(pl.multiple_of(rank_ref[0] * width, width), width)
    y_ref[0, 6:7, :] = norm0[3:4, :] + norm1[3:4, :]
    y_ref[1, 6:7, :] = norm0[4:5, :] + norm1[4:5, :]
    for i in range(3):
        y_ref[i, 7:8, own] = sums0[i : i + 1, own] + sums1[i : i + 1, own]
    for i in range(2):
        cols = pl.ds(pl.multiple_of(rank_ref[0] * width + i * LANE, LANE), LANE)
        y_ref[3, 7:8, cols] = bias0[i : i + 1, :] + bias1[i : i + 1, :]
    for i in range(4):
        cols = slice(i * width, (i + 1) * width)
        y_ref[4 + i, 7:8, own] = hid0[0:1, cols] + hid1[0:1, cols]


def load_ffn_chunk(copies, c, sources, dst):
    grad_o, grad_i = sources
    rows = D // RING
    part = rows // H
    copies.start(grad_o.at[pl.ds(pl.multiple_of(c * rows, rows), rows), :], dst.at[0:rows, :])
    for s in range(H):
        src = pl.ds(pl.multiple_of(s * (D // H) + c * part, part), part)
        copies.start(grad_i.at[src, :], dst.at[rows + s * part : rows + (s + 1) * part, :])


def load_pack_chunk(copies, c, sources, dst):
    grad_p, grad_w = sources
    rows = D // RING
    part = E * LANE // RING
    copies.start(grad_p.at[pl.ds(pl.multiple_of(c * rows, rows), rows), :], dst.at[0:rows, :])
    copies.start(
        grad_w.at[pl.ds(pl.multiple_of(c * part, part), part), :], dst.at[rows : rows + part, :]
    )


def ring_kernel(load, split, t, rank_ref, pos_ref, src0, src1, *refs):
    tail_ref, refs = (refs[0], refs[1:]) if load is load_pack_chunk else (None, refs)
    got_hbm, refs = (refs[:2], refs[2:]) if t else ((), refs)
    outs_hbm, refs = (refs[:2], refs[2:]) if t < 4 else (refs[: 1 + H], refs[1 + H :])
    loaded, held, *more, sems = refs
    got, outs = more[: len(got_hbm)], more[len(got_hbm) :]
    copies = Copies(sems)
    for src, dst in zip(got_hbm, got):
        copies.start(src, dst)
    pos = pos_ref[0]
    total = held.shape[1]
    chunks = [(pos + 4 - t) % RING, (pos + 4 + t) % RING][: 2 if t < 4 else 1]
    for i, c in enumerate(chunks[: 2 if t < 4 else 1]):
        load(copies, c, (src0, src1), loaded.at[i])
    copies.finish()
    held[...] = loaded[...].astype(f32)
    if tail_ref is not None:
        for i, c in enumerate(chunks):
            rows = slice(D // RING - TAIL, D // RING)
            held[i, rows, :] = held[i, rows, :] + tail_ref[c]
    if t == 4:
        held[0] = held[0] + got[0][...].astype(f32) + got[1][...].astype(f32)
        rows = D // RING
        rank = rank_ref[0]
        for r, ref in enumerate(outs[1:]):
            if tail_ref is None:
                size = rows // H
                at = pl.multiple_of(rows + (rank ^ r) * size, size)
                ref[...] = held[0, pl.ds(at, size), :].astype(bf16)
            else:
                size = D // H
                at = pl.multiple_of((rank ^ r) * size, size)
                ref[...] = held[0, 0:rows, pl.ds(at, size)].astype(bf16)
        outs[0][...] = (held[0, 0:rows, :] if tail_ref is None else held[0, rows:total, :]).astype(bf16)
        for ref, dst in zip(outs, outs_hbm):
            copies.start(ref, dst)
        copies.finish()
        return
    for i, ref in enumerate(outs):
        part = slice(0, split) if i == 0 else slice(split, total)
        if t == 0:
            ref[...] = held[i, part, :].astype(bf16)
        elif t == 1:
            ref[...] = held[i].astype(bf16)
            ref[part, :] = (held[i, part, :] + got[i][...].astype(f32)).astype(bf16)
        else:
            ref[...] = (held[i] + got[i][...].astype(f32)).astype(bf16)
        copies.start(ref, outs_hbm[i])
    copies.finish()


def load_ring(copies, pos, split, refs, dst):
    own, fwd, bwd, half_fwd, half_bwd = refs[0], refs[1:4], refs[4:7], refs[7], refs[8]
    copies.start(own, dst.at[pos])
    for i in range(3):
        copies.start(fwd[i], dst.at[(pos + RING - 1 - i) % RING])
        copies.start(bwd[i], dst.at[(pos + 1 + i) % RING])
    last = (pos + 4) % RING
    copies.start(half_fwd, dst.at[last, 0:split, :])
    copies.start(half_bwd, dst.at[last, split : dst.shape[1], :])
    copies.finish()


def ffn_grads_kernel(split, rank_ref, pos_ref, *refs):
    parts, (o_hbm, i_hbm, held, o_ref, i_ref, sems) = refs[:9], refs[9:]
    copies = Copies(sems)
    load_ring(copies, pos_ref[0], split, parts, held)
    rows = D // RING
    part = rows // H
    for c in range(RING):
        o_rows = slice(c * rows, (c + 1) * rows)
        o_ref[o_rows, :] = held[c, 0:rows, :].astype(f32)
        copies.start(o_ref.at[o_rows, :], o_hbm.at[o_rows, :])
        i_rows = slice(c * part, (c + 1) * part)
        for r in range(H):
            cols = pl.ds(pl.multiple_of((rank_ref[0] ^ r) * D, D), D)
            at = rows + r * part
            i_ref[i_rows, cols] = held[c, at : at + part, :].astype(f32)
        copies.start(i_ref.at[i_rows, :], i_hbm.at[i_rows, :])
    copies.finish()


def pack_grads_kernel(split, rank_ref, pos_ref, *refs):
    parts, refs = refs[:9], refs[9:]
    (q_ref, rv_ref, ro_ref, k_ref, p_ref, v_ref, w_ref), refs = refs[:7], refs[7:]
    (g1, b1, g2, b2, bo, content, posn, bin_ref), refs = refs[:8], refs[8:]
    held, heads, sems = refs
    copies = Copies(sems)
    load_ring(copies, pos_ref[0], split, parts, held)
    width = D // H
    rank = rank_ref[0]
    for r in range(H):
        heads[rank ^ r] = held[:, 0:LANE, r * width : (r + 1) * width].astype(f32)
    for h in range(H):
        rows = slice(h * DH, (h + 1) * DH)
        q_ref[rows, :] = heads[h, 0, 0:DH, :]
        rv_ref[h * E : (h + 1) * E, :] = heads[h, 0, DH : DH + E, :]
        ro_ref[h * E : (h + 1) * E, :] = heads[h, 0, DH + E : DH + 2 * E, :]
        k_ref[rows, :] = heads[h, 1, 0:DH, :]
        p_ref[rows, :] = heads[h, 2, 0:DH, :]
        for e in range(E):
            at = (h * E + e) * DH
            v_ref[at : at + DH, :] = heads[h, 3 + e, 0:DH, :]
    part = E * LANE // RING
    for c in range(RING):
        for e in range(E):
            low, high = max(c * part, e * LANE), min((c + 1) * part, e * LANE + DH)
            if low < high:
                at = low - e * LANE + e * DH
                w_ref[at : at + high - low, :] = held[
                    c, LANE + low - c * part : LANE + high - c * part, :
                ].astype(f32)
    last = slice(LANE - 1, LANE)
    before = slice(LANE - 2, LANE - 1)
    for ref, c in ((g1, 0), (b1, 1)):
        ref[...] = sum(heads[h, c, before, :] for h in range(H)).reshape(ref.shape)
    for c, ref in enumerate((g2, b2, bo)):
        ref[...] = heads[rank, c, last, :].reshape(ref.shape)
    row = heads[rank, 3, last, :]
    content[...] = row[:, 0:DH].reshape(content.shape)
    posn[...] = row[:, LANE : LANE + DH].reshape(posn.shape)
    for i in range(4):
        bin_ref[i * width : (i + 1) * width] = heads[rank, 4 + i, last, :].reshape((width,))


def flip_shard(value, bit):
    return lax.ppermute(value, "shard", [(s, s ^ bit) for s in range(H)])


def flip_dp(value, bit):
    count = lax.axis_size("dp")
    return lax.ppermute(value, "dp", [(d, d ^ bit) for d in range(count)])


def take(value, at, size, axis=0):
    return lax.dynamic_slice_in_dim(value, at, size, axis)


def put(value, part, at, axis=0):
    return lax.dynamic_update_slice_in_dim(value, part, at, axis)


def spread(own):
    across = flip_shard(own, 2)
    return own, flip_shard(own, 1), across, flip_shard(across, 1)


def ring_order():
    return list(range(0, RING, 2)) + list(range(RING - 1, 0, -2))


def pass_on(value, way):
    order, count = ring_order(), lax.axis_size("dp")
    pairs = [
        (base + order[i], base + order[(i + way) % RING])
        for base in range(0, count, RING)
        for i in range(RING)
    ]
    return lax.ppermute(value, "dp", pairs)


def swap_shard(value, rank, size, axis):
    parts = [take(value, (rank ^ r) * size, size, axis) for r in range(H)]
    return [flip_shard(p, r) if r else p for r, p in enumerate(parts)]


def sinusoid(length, feature_count):
    distance = (length - 1 - jnp.arange(length, dtype=jnp.int32)).astype(f32)
    inv_freq = jnp.exp(
        jnp.arange(0, feature_count, 2, dtype=jnp.int32).astype(f32)
        * (-math.log(10000.0) / feature_count)
    )
    angles = distance[:, None] * inv_freq[None, :]
    return jnp.concatenate([jnp.sin(angles), jnp.cos(angles)], axis=1)


def local(
    inputs,
    segments,
    padding,
    routes_value,
    routes_output,
    norm1_gain,
    norm1_bias,
    query_weight,
    key_weight,
    pos_weight,
    content_bias,
    pos_bias,
    value_router,
    output_router,
    value_experts,
    output_experts,
    norm2_gain,
    norm2_bias,
    ffn_in,
    ffn_in_bias,
    ffn_out,
    ffn_out_bias,
    cotangent,
):
    micro = inputs.shape[0]
    own = inputs.shape[2]
    length = own * H
    dp_count = lax.axis_size("dp")
    rank = lax.axis_index("shard")
    me = rank.astype(jnp.int32).reshape(1)
    dp_rank = lax.axis_index("dp")
    side = (dp_rank % RING).astype(jnp.int32).reshape(1)
    place = dp_rank % RING
    place = jnp.where(place % 2 == 0, place // 2, RING - 1 - place // 2)
    place = place.astype(jnp.int32).reshape(1)
    quarter = D // H

    token = [me]

    def after(value, *deps):
        return lax.optimization_barrier((value, *deps))[0]

    def step(fn, first, *rest):
        res = fn(after(first, token[0]), *rest)
        token[0] = jax.tree.leaves(res)[0]
        return res

    def kernel(fn, outs, args, second=side, **kwargs):
        deps = [*kwargs.pop("deps", ()), *([] if token[0] is me else [token[0]])]
        res = call(fn, outs, [me, second, *args], deps=deps, **kwargs)
        token[0] = res[0]
        return res

    packs = kernel(
        prep_kernel,
        [out((PACK, quarter), bf16)] * 2
        + [out((PACK, LANE), bf16)] * 2
        + [out((8, LANE), f32), out((1, FF // H), f32)]
        + [out((quarter, FF // H), bf16)]
        + [out((quarter // 2, FF // H), bf16)] * 2
        + [out((own, D), bf16)] * micro,
        [
            Far(a)
            for a in (
                inputs,
                ffn_in,
                query_weight.T,
                key_weight.T,
                pos_weight.T,
                value_router.T,
                output_router.T,
                value_experts.T,
                routes_value[:, 0].transpose(0, 2, 3, 1),
                routes_output[:, 0].transpose(0, 2, 3, 1),
                segments,
                padding,
                norm1_gain,
                norm1_bias,
                norm2_gain,
                norm2_bias,
                ffn_out_bias,
                content_bias,
                pos_bias,
                ffn_in_bias,
            )
        ],
        scratch=[
            pltpu.VMEM(shape, dtype)
            for shape, dtype in [((H * DH, quarter), bf16)] * 3
            + [((H * E, quarter), bf16)] * 2
            + [((H * E * DH, quarter), bf16)]
            + [((micro, H, 2, own), jnp.int32)] * 2
            + [((micro, 1, own), jnp.int32)] * 2
            + [((quarter,), bf16)] * 5
            + [((DH,), bf16)] * 2
            + [((FF // H,), bf16)]
            + [((LANE - DH, quarter), f32), ((PACK, quarter), bf16)]
        ],
        copies=18 + 3 + micro,
        vmem=56,
    )
    sine = sinusoid(length, D).astype(bf16)
    head, b_in, core_in, *sent = packs[H:]
    sent_in, sent_x = sent[:2], sent[2:]
    near = [flip_shard(packs[r], r) for r in (2, 3)]
    w_core = flip_shard(packs[1], 1)
    far = [flip_dp(w, 1) for w in near]
    weights = [packs[0], w_core, *near, *far]
    x_own = inputs[:, 0]
    sent_x[0] = gate(sent_x[0], [*near, sine])
    x_parts = [spread(x) for x in sent_x]
    near_in = [flip_shard(w, r) for w, r in zip(sent_in, (2, 3))]
    w_in_core = flip_shard(core_in, 1)
    cot_parts = spread(cotangent[:, 0])

    def add_chip(keep, send):
        got = flip_shard(send, 1)
        add = lambda k, g: (k.astype(f32) + g.astype(f32)).astype(bf16)
        return step(add, keep, got)

    def finish_halves(chip):
        across = flip_shard(chip, 2)
        return chip, across, flip_shard(chip, 1), flip_shard(across, 1)

    half = out((length // 2, D), bf16)
    wide = out((length, D), bf16)
    saved_shapes = (
        [wide]
        + [out((length, LANE), bf16)] * 4
        + [
            out((length, E * LANE), bf16),
            out((length, LANE), f32),
            out((length, length), bf16),
            out((length, LANE), f32),
            out((length, E * LANE), bf16),
        ]
    )
    vmem_of = lambda shapes: [pltpu.VMEM(o.shape, o.dtype) for o in shapes]
    weight_shapes = [out((PACK, D), bf16), out((E * LANE, D), bf16)]
    joined = out((micro * length, D), bf16)
    saved = []
    residuals = []
    for m in range(micro):
        if m == 0:
            more = [Far(w) for w in weights] + [Far(sine), Far(output_experts)]
            extra = [Far(o) for o in weight_shapes]
            extra += [out((length, LANE), bf16), out((8, D), f32), out((micro, 8, length), f32)]
        else:
            more = [Far(wt), Far(w_out_heads), pos, vec, rows]
            extra = []
        res = kernel(
            functools.partial(attention_kernel, m),
            [Far(wide)]
            + [Far(joined)]
            + [Far(o) for o in saved_shapes[1:-1]]
            + [Far(out((micro * length, E * LANE), bf16))]
            + [out((length, LANE), f32), Far(half), Far(half)]
            + extra,
            [Far(x) for x in (x_own, *x_parts[m][1:])] + [head] + more,
            scratch=vmem_of(
                saved_shapes + weight_shapes + [wide, half, half] + ([wide] if m == 0 else [])
            ),
            copies=40,
            into={1: saved[0][1], 10: saved[0][10]} if m else None,
            deps=[*near_in, residuals[0][0]] if m else [],
            vmem=60,
            flops=2 * length * D * 1700,
        )
        saved.append(res[:12])
        if m == 0:
            near_in = [gate(w, [res[12]]) for w in near_in]
            far_in = [flip_dp(w, 1) for w in near_in]
        send, keep = res[12:14]
        if m == 0:
            wt, w_out_heads, pos, vec, rows = res[14:]
            send = gate(send, [*near_in, *x_parts[1][1:3]][: 4])
        else:
            send = gate(send, [*far_in, cot_parts[2], residuals[0][1]])
        residuals.append(finish_halves(add_chip(keep, send)))
    ffn = []
    gn2 = []
    for m in range(micro):
        res = kernel(
            functools.partial(ffn_kernel, m),
            [Far(joined)] * 4
            + [Far(wide)]
            + [
                out((length, LANE), f32),
                out((own, D), f32),
                out((8, FF // H), f32),
                Far(half),
                Far(half),
            ],
            [Far(a) for a in (saved[m][0], *residuals[m])]
            + [vec, b_in]
            + [Far(w) for w in (ffn_in, w_in_core, *near_in, *far_in, ffn_out, *cot_parts)],
            scratch=vmem_of(
                [wide, out((D, FF // H), bf16), out((FF // H, D), bf16)] + [wide] * 5 + [half] * 6
            ),
            copies=30,
            into={i: ffn[0][i] for i in range(4)} if m else None,
            vmem=60,
            deps=[residuals[1][0] if m == 0 else gn2[0][0]],
            flops=2 * length * D * D * 3,
        )
        ffn.append(res)
        gn2.append(finish_halves(add_chip(res[-1], res[-2])))

    def tn(a, b):
        return mm(a, b, TN).astype(bf16)

    class Ring:
        def __init__(self, load, split, total, sources):
            self.load, self.split, self.total = load, split, total
            self.sources, self.got, self.t = sources, (), 0

        def step(self, deps=()):
            rows = D // RING
            if self.t == 0:
                shapes = [(self.split, D), (self.total - self.split, D)]
            elif self.t < 4:
                shapes = [(self.total, D)] * 2
            elif len(self.sources) == 2:
                shapes = [(rows, D)] + [(rows // H, D)] * H
            else:
                shapes = [(self.total - rows, D)] + [(rows, D // H)] * H
            shapes = [out(shape, bf16) for shape in shapes]
            res = kernel(
                functools.partial(ring_kernel, self.load, self.split, self.t),
                [Far(o) for o in shapes],
                [Far(g) for g in self.sources[:2]]
                + list(self.sources[2:])
                + [Far(g) for g in self.got],
                second=place,
                scratch=[pltpu.VMEM((2, self.total, D), bf16), pltpu.VMEM((2, self.total, D), f32)]
                + vmem_of(self.got)
                + vmem_of(shapes),
                copies=20,
                deps=deps,
                vmem=56,
            )
            self.t += 1
            self.sent = res[0]
            if self.t == 5:
                return [self.across(p) for p in res]
            self.got = (pass_on(res[0], 1), pass_on(res[1], -1))

        def across(self, piece):
            bit = RING
            while bit < dp_count:
                piece = (piece.astype(f32) + flip_dp(piece, bit).astype(f32)).astype(bf16)
                bit *= 2
            return piece

        def gather(self, piece):
            self.parts = [[piece], [piece]]
            self.pass_parts()

        def pass_parts(self):
            for way, parts in zip((1, -1), self.parts):
                value = parts[-1]
                if len(parts) == 4:
                    cut = (lambda v: v[: self.split]) if way == 1 else (lambda v: v[self.split :])
                    value = step(cut, value)
                parts.append(pass_on(value, way))

        def result(self):
            fwd, bwd = self.parts
            return [fwd[0], *fwd[1:4], *bwd[1:4], fwd[4], bwd[4]]

    n2, hid, gp, cots = ffn[1][:4]
    grad_o = tn(hid, cots)
    grad_i = tn(n2, gp)
    ffn_ring = Ring(load_ffn_chunk, D // RING, 2 * D // RING, [grad_o, grad_i])
    ffn_ring.step()
    back = []

    branch = []

    def run_branch(m, deps=()):
        gate_m, att, rstd = saved[m][7], saved[m][9], ffn[m][5]
        from_far = [*gn2[m], ffn[1][3], ffn[m][4], w_out_heads]
        branch.append(
            kernel(
                functools.partial(branch_kernel, m),
                [
                    Far(joined),
                    out((8, D), f32),
                    out((own, D), f32),
                    out((length, LANE), bf16),
                    out((length, LANE), f32),
                ],
                [vec, rstd, gate_m, att] + [Far(a) for a in from_far],
                copies=10,
                vmem=56,
                deps=deps,
                scratch=vmem_of([*from_far[:4], wide, *from_far[5:], wide]),
                into={0: branch[0][0]} if m else None,
            )
        )

    def run_back(m, deps=()):
        x, n1, qc, qp, k, v, va, gate_m, prob, att, mix, stat = saved[m]
        from_far = [prob, v, k, qc, qp, va, wt, x]
        back.append(
            kernel(
                functools.partial(back_kernel, m),
                [
                    out((8, D), f32),
                    Far(out((micro * length, PACK), bf16)),
                    out((length, LANE), f32),
                    out((8, LANE), f32),
                    Far(out((2, own, D), bf16)),
                    Far(out((2, own, D), bf16)),
                ],
                [branch[m][3], branch[m][4], pos, gate_m, stat] + [Far(a) for a in from_far],
                copies=12,
                into={1: back[0][1]} if m else None,
                vmem=56,
                deps=deps,
                scratch=vmem_of(from_far)
                + [
                    pltpu.VMEM((length, PACK), bf16),
                    pltpu.VMEM((length, LANE), f32),
                    pltpu.VMEM((length, LANE), f32),
                    pltpu.VMEM((length, D), bf16),
                    pltpu.VMEM((2, own, D), bf16),
                    pltpu.VMEM((2, own, D), bf16),
                ],
            )
        )

    run_branch(0)
    ffn_ring.step()
    run_back(0)
    ffn_ring.step()
    run_branch(1)
    ffn_ring.step()
    grad_w = tn(saved[1][10], branch[1][0])
    run_back(1, deps=[grad_w])
    turned = lambda parts: [flip_shard(p, r) if r else p for r, p in enumerate(parts)]
    piece, *parts = ffn_ring.step()
    ffn_piece = jnp.concatenate([piece, *turned(parts)])
    gpos = (back[0][2] + back[1][2]).astype(bf16)
    grad_p = tn(gate(back[1][1], [piece]), saved[1][1])
    grad_p = lax.dynamic_update_slice(grad_p, tn(gpos, sine), (2 * LANE, 0))
    tails = kernel(
        vectors_kernel,
        [out((RING, TAIL, D), f32)],
        [branch[0][1], branch[1][1], back[0][0], back[1][0], back[0][3], back[1][3]]
        + [ffn[0][7], ffn[1][7]],
    )[0]
    pack_ring = Ring(
        load_pack_chunk, DH, D // RING + E * LANE // RING, [grad_p, grad_w, tails]
    )
    ffn_ring.gather(ffn_piece)
    pack_ring.step()
    add = lambda a, b: (a.astype(f32) + b.astype(f32)).astype(bf16)
    gx_got = [flip_shard(back[m][5], 1) for m in range(micro)]
    gx_far = jnp.stack([add(back[m][4][1], gx_got[m][1]) for m in range(micro)])
    gx_far = flip_shard(gx_far, 2)
    came = lambda i: [p[i] for p in ffn_ring.parts]
    both_ways = ffn_ring.parts
    both_ways[0][1] = gate(both_ways[0][1], [pack_ring.sent, both_ways[1][1]])
    for i in range(1, 4):
        ffn_ring.pass_parts()
        pack_ring.step(deps=came(i + 1))
    gx_all = kernel(
        input_kernel,
        [out((micro, 1, own, D), f32)],
        [x_own, vec, gx_far]
        + [a for m in range(micro) for a in (branch[m][2], back[m][4], gx_got[m])],
    )[0]
    piece, *parts = pack_ring.step()
    pack_piece = jnp.concatenate([jnp.concatenate(turned(parts), axis=1), piece])
    pack_ring.gather(pack_piece)
    g_out, g_in = kernel(
        functools.partial(ffn_grads_kernel, ffn_ring.split),
        [Far(out((FF // H, D), f32)), Far(out((quarter, FF), f32))],
        [Far(p) for p in ffn_ring.result()],
        second=place,
        scratch=[
            pltpu.VMEM((RING, ffn_ring.total, D), bf16),
            pltpu.VMEM((FF // H, D), f32),
            pltpu.VMEM((quarter, FF), f32),
        ],
        copies=25,
        vmem=40,
        deps=[pack_piece],
    )
    ways = pack_ring.parts
    sides = out((2, micro, own, D), bf16)
    keep, send = kernel(
        project_kernel,
        [Far(sides)] * 2,
        [Far(hid), Far(ffn_out)],
        scratch=vmem_of([joined, out((FF // H, D), bf16), joined, sides, sides]),
        copies=4,
        vmem=56,
        deps=[pack_piece],
    )
    ways[0][1] = gate(ways[0][1], [g_out, keep, ways[1][1]])
    got = flip_shard(gate(send, [ways[0][1]]), 1)
    far = flip_shard(add(keep[1], got[1]), 2)
    pack_ring.pass_parts()
    pack_ring.pass_parts()
    pack_ring.pass_parts()
    y_all = kernel(
        output_kernel,
        [out((micro, 1, own, D), bf16)],
        [vec, keep, got, far] + [ffn[m][6] for m in range(micro)],
    )[0]
    res = kernel(
        functools.partial(pack_grads_kernel, pack_ring.split),
        [
            out((H * DH, quarter), f32),
            out((H * E, quarter), f32),
            out((H * E, quarter), f32),
            out((H * DH, quarter), f32),
            out((H * DH, quarter), f32),
            out((H * E * DH, quarter), f32),
            out((E * DH, D), f32),
        ]
        + [out((quarter,), f32)] * 5
        + [out((DH,), f32)] * 2
        + [out((FF // H,), f32)],
        [Far(p) for p in pack_ring.result()],
        second=place,
        scratch=[
            pltpu.VMEM((RING, pack_ring.total, D), bf16),
            pltpu.VMEM((H, RING, LANE, quarter), f32),
        ],
        copies=9,
        vmem=40,
    )
    g_q, g_rv, g_ro, g_k, g_p, g_v, g_wo, g1, b1, g2, b2, bo, content, posb, bi = res
    return (
        y_all,
        gx_all,
        g1,
        b1,
        g_q.T,
        g_k.T,
        g_p.T,
        content,
        posb,
        g_rv.T,
        g_ro.T,
        g_v.T,
        g_wo,
        g2,
        b2,
        g_in,
        bi,
        g_out,
        bo,
    )


def solution(mesh):
    tokens = P(None, "dp", "shard")
    whole = P(None, "dp", "shard", None)
    routes = P(None, "dp", "shard", None, None)
    vector = P("shard")
    matrix = P("shard", None)
    weights = (
        vector,
        vector,
        matrix,
        matrix,
        matrix,
        vector,
        vector,
        matrix,
        matrix,
        matrix,
        matrix,
        vector,
        vector,
        matrix,
        vector,
        matrix,
        vector,
    )
    return jax.shard_map(
        local,
        mesh=mesh,
        in_specs=(whole, tokens, tokens, routes, routes) + weights + (whole,),
        out_specs=(whole, whole) + weights,
        check_vma=False,
    )
```

```python
import functools
import math

import jax
import jax.numpy as jnp
from jax import lax
from jax.experimental import pallas as pl
from jax.experimental.pallas import tpu as pltpu
from jax.sharding import PartitionSpec as P

D = 1024
H = 4
DH = 112
E = 5
FF = 4096
LANE = 128
PACK = 1024
BLK = 128
RING = 8
TAIL = 8
MASKED = -1e30
SCALE = DH ** (-0.5)
bf16 = jnp.bfloat16
f32 = jnp.float32
NN = (((1,), (0,)), ((), ()))
NT = (((1,), (1,)), ((), ()))
TN = (((0,), (0,)), ((), ()))


def mm(a, b, dims=NN):
    return lax.dot_general(a, b, dims, preferred_element_type=f32)


def call(kernel, outs, args, scratch=(), copies=0, flops=0, vmem=12, smem=2, deps=(), into=None):
    in_specs, arrays = [], []
    args = list(args)
    count = len(args)
    into = into or {}
    deps = [*deps, *into.values()]
    aliases = {count + len(deps) - len(into) + n: i for n, i in enumerate(into)}
    args += [Far(d, pl.ANY) for d in deps]
    body = lambda *refs: kernel(*refs[:count], *refs[count + len(deps) :])
    for i, arg in enumerate(args):
        far = isinstance(arg, Far)
        space = pltpu.SMEM if i < smem else arg.space if far else pltpu.VMEM
        in_specs.append(pl.BlockSpec(memory_space=space))
        arrays.append(arg.value if far else arg)
    out_specs, out_shapes = [], []
    for o in outs:
        far = isinstance(o, Far)
        out_specs.append(pl.BlockSpec(memory_space=o.space if far else pltpu.VMEM))
        out_shapes.append(o.value if far else o)
    moved = sum(math.prod(a.shape) * a.dtype.itemsize for a in arrays + out_shapes)
    scratch = list(scratch)
    if copies:
        scratch.append(pltpu.SemaphoreType.DMA((copies,)))
    return pl.pallas_call(
        body if deps else kernel,
        out_shape=out_shapes,
        in_specs=in_specs,
        out_specs=out_specs,
        scratch_shapes=scratch,
        compiler_params=pltpu.CompilerParams(vmem_limit_bytes=vmem << 20),
        input_output_aliases=aliases,
        cost_estimate=pl.CostEstimate(flops=0, bytes_accessed=0, transcendentals=0),
    )(*arrays)


class Far:
    def __init__(self, value, space=pltpu.HBM):
        self.value, self.space = value, space


class Copies:
    def __init__(self, sems):
        self.sems, self.count, self.left = sems, 0, []

    def start(self, src, dst):
        copy = pltpu.make_async_copy(src, dst, self.sems.at[self.count])
        self.count += 1
        copy.start()
        self.left.append(copy)
        return copy

    def wait(self, *copies):
        for copy in copies:
            copy.wait()
            self.left.remove(copy)

    def finish(self):
        self.wait(*list(self.left))


def gate(value, deps):
    return pl.pallas_call(
        lambda *refs: None,
        out_shape=jax.ShapeDtypeStruct(value.shape, value.dtype),
        in_specs=[pl.BlockSpec(memory_space=pl.ANY)] * (1 + len(deps)),
        out_specs=pl.BlockSpec(memory_space=pl.ANY),
        input_output_aliases={0: 0},
        cost_estimate=pl.CostEstimate(flops=0, bytes_accessed=0, transcendentals=0),
    )(value, *deps)


def out(shape, dtype):
    return jax.ShapeDtypeStruct(shape, dtype)


def prep_kernel(rank_ref, side_ref, *refs):
    count = 18
    (x_hbm, win_hbm), refs = refs[:2], refs[2:]
    ins, outs, scratch = refs[:count], refs[count : count + 6], refs[count + 6 :]
    (core_hbm, near2_hbm, near3_hbm, *x_outs), scratch = scratch[:5], scratch[5:]
    held, (marks_ref, pack_ref, sems) = scratch[:count], scratch[count:]
    copies = Copies(sems)
    loads = [copies.start(src, dst) for src, dst in zip(ins, held)]
    for m, ref in enumerate(x_outs):
        copies.start(x_hbm.at[m, 0], ref)
    width = win_hbm.shape[1] // H
    size = win_hbm.shape[0] // 2
    for r, ref in ((1, core_hbm), (2, near2_hbm), (3, near3_hbm)):
        cols = pl.ds(pl.multiple_of((rank_ref[0] ^ r) * width, width), width)
        rows = pl.ds(pl.multiple_of((side_ref[0] % 2) * size, size), size) if r > 1 else slice(0, 2 * size)
        copies.start(win_hbm.at[rows, cols], ref)
    copies.wait(*loads)
    q_ref, k_ref, p_ref, rv_ref, ro_ref, v_ref, routes_v_ref, routes_o_ref = held[:8]
    seg_ref, pad_ref, g1_ref, b1_ref, g2_ref, b2_ref, bo_ref, cb_ref, pb_ref, bi_ref = held[8:]
    head_ref, bin_ref = outs[4:]
    head_ref[...] = jnp.zeros(head_ref.shape, f32)
    head_ref[0:1, 0:DH] = cb_ref[...].astype(f32).reshape(1, -1)
    head_ref[1:2, 0:DH] = pb_ref[...].astype(f32).reshape(1, -1)
    bin_ref[...] = bi_ref[...].astype(f32).reshape(1, -1)
    micro, own = seg_ref.shape[0], seg_ref.shape[2]
    marks_ref[...] = jnp.zeros(marks_ref.shape, f32)
    copied = [slice(0, own), slice(own, 2 * own)]
    for m in range(micro):
        for cols in copied:
            marks_ref[4 * m + 2 : 4 * m + 3, cols] = seg_ref[m].astype(f32)
            marks_ref[4 * m + 3 : 4 * m + 4, cols] = pad_ref[m].astype(f32)
    for i, ref in enumerate((g1_ref, b1_ref, g2_ref, b2_ref, bo_ref)):
        marks_ref[4 * micro + i : 4 * micro + i + 1, :] = ref[...].astype(f32).reshape(1, -1)
    row = lax.broadcasted_iota(jnp.int32, (16, H * E), 0)
    col = lax.broadcasted_iota(jnp.int32, (16, H * E), 1)
    for r in range(H):
        out_ref = outs[r] if r < 2 else pack_ref
        h = rank_ref[0] ^ r
        rows = pl.ds(pl.multiple_of(h * DH, 16), DH)
        for m in range(micro):
            for i, ref in enumerate((routes_v_ref, routes_o_ref)):
                ones = lax.shift_left(jnp.ones((2, own), jnp.int32), ref[m, h])
                code = jnp.sum(ones.astype(f32), axis=0, keepdims=True)
                for cols in copied:
                    marks_ref[4 * m + i : 4 * m + i + 1, cols] = code
        pick_v = jnp.where((row < E) & (col == h * E + row), 1.0, 0.0).astype(bf16)
        pick_o = jnp.where((row >= E) & (row < 2 * E) & (col == h * E + row - E), 1.0, 0.0)
        routers = mm(pick_v, rv_ref[...]) + mm(pick_o.astype(bf16), ro_ref[...])
        out_ref[0:DH, :] = q_ref[rows, :]
        out_ref[DH:LANE, :] = routers.astype(bf16)
        out_ref[LANE : LANE + DH, :] = k_ref[rows, :]
        out_ref[LANE + DH : 2 * LANE, :] = marks_ref[...].astype(bf16)
        out_ref[2 * LANE : 2 * LANE + DH, :] = p_ref[rows, :]
        out_ref[2 * LANE + DH : 3 * LANE, :] = jnp.zeros((LANE - DH, out_ref.shape[1]), bf16)
        for e in range(E):
            at = (3 + e) * LANE
            expert = pl.ds(pl.multiple_of((h * E + e) * DH, 16), DH)
            out_ref[at : at + DH, :] = v_ref[expert, :]
            out_ref[at + DH : at + LANE, :] = jnp.zeros((LANE - DH, out_ref.shape[1]), bf16)
        if r >= 2:
            half = pl.ds(pl.multiple_of((side_ref[0] % 2) * LANE, LANE), LANE)
            outs[r][...] = pack_ref[:, half]
    copies.finish()


def norm_stats(x):
    mean = jnp.mean(x, axis=-1, keepdims=True)
    centred = x - mean
    var = jnp.mean(centred * centred, axis=-1, keepdims=True)
    rstd = lax.rsqrt(var + 1e-05)
    return centred * rstd, rstd


def norm_back(grad, unit, rstd, gain):
    g = grad * gain
    return rstd * (
        g
        - jnp.mean(g, axis=-1, keepdims=True)
        - unit * jnp.mean(g * unit, axis=-1, keepdims=True)
    )


def x_send_keep(held, x_hbm, send_hbm, keep_hbm):
    return held[0], held[1], x_hbm, send_hbm, keep_hbm


def attention_kernel(m, rank_ref, side_ref, *refs):
    first = m == 0
    (x0, x1, x2, x3), refs = refs[:4], refs[4:]
    head_ref, refs = refs[0], refs[1:]
    if first:
        (w0, w1, near2, near3, far2, far3, sine_hbm, wo_hbm), refs = refs[:8], refs[8:]
    else:
        (wt_hbm, wo_hbm, pos_ref, vec_ref, rows_ref), refs = refs[:5], refs[5:]
    (x_ref, n_hbm, qc_hbm, qp_hbm, k_hbm, v_hbm, va_hbm, gate_hbm, p_hbm, att_hbm), refs = (
        refs[:10],
        refs[10:],
    )
    (mix_hbm, stat_ref), refs = refs[:2], refs[2:]
    (send_ref, keep_ref), refs = refs[:2], refs[2:]
    if first:
        (wt_hbm, wop_hbm, pos_ref, vec_ref, rows_ref), refs = refs[:5], refs[5:]
    n_ref, qc_ref, qp_ref, k_ref, v_ref, va_ref, gate_ref, p_ref, att_ref, mix_ref = refs[:10]
    wt_ref, wo_ref, x_out, send_out, keep_out = x_send_keep(refs[10:15], x_ref, send_ref, keep_ref)
    x_ref, send_ref, keep_ref = refs[12:15]
    sine_ref = refs[15] if first else None
    copies = Copies(refs[-1])
    length = x_ref.shape[0]
    both = slice(m * length, (m + 1) * length)
    blocks = length // BLK
    rank = rank_ref[0]
    quarter = D // H

    def at(r, size):
        return pl.ds(pl.multiple_of((rank ^ r) * size, size), size)

    loads = [copies.start(x0.at[m], x_ref.at[at(0, BLK), :])]
    loads += [copies.start(ref, x_ref.at[at(r, BLK), :]) for r, ref in enumerate((x1, x2, x3), 1)]
    if first:
        side = side_ref[0] % 2
        for r, ref in enumerate((w0, w1)):
            loads.append(copies.start(ref, wt_ref.at[:, at(r, quarter)]))
        for r, place, ref in (
            (2, side, near2),
            (3, side, near3),
            (2, 1 - side, far2),
            (3, 1 - side, far3),
        ):
            cols = pl.ds(pl.multiple_of((rank ^ r) * quarter + place * LANE, LANE), LANE)
            loads.append(copies.start(ref, wt_ref.at[:, cols]))
        sine_load = copies.start(sine_hbm, sine_ref)
        wo_loads = []
        for e in range(E):
            rows = slice(e * LANE, e * LANE + DH)
            wo_loads.append(copies.start(wo_hbm.at[e * DH : (e + 1) * DH, :], wo_ref.at[rows, :]))
            wo_ref[e * LANE + DH : (e + 1) * LANE, :] = jnp.zeros((LANE - DH, D), bf16)
        copies.wait(*loads)
        vec_ref[...] = jnp.zeros(vec_ref.shape, f32)
        rows_ref[...] = jnp.zeros(rows_ref.shape, f32)
        for r in range(H):
            micro = rows_ref.shape[0]
            marks = wt_ref[LANE + DH : 2 * LANE, at(r, quarter)].astype(f32)
            vec_ref[0:5, at(r, quarter)] = marks[4 * micro : 4 * micro + 5, :]
            fresh = pl.ds(pl.multiple_of((rank ^ r) * quarter + side * LANE, LANE), LANE)
            marks = wt_ref[LANE + DH : 2 * LANE, fresh].astype(f32)
            for i in range(micro):
                part = marks[4 * i : 4 * i + 4, :]
                rows_ref[i, 0:1, at(r, BLK)] = part[0:1, :] + 2.0**E * part[1:2, :]
                rows_ref[i, 1:3, at(r, BLK)] = part[2:4, :]
        copies.start(wt_ref, wt_hbm)
    else:
        wt_load = copies.start(wt_hbm, wt_ref)
        wo_loads = [copies.start(wo_hbm, wo_ref)]
        copies.wait(*loads)

    @pl.loop(0, blocks)
    def _(b):
        rows = pl.ds(pl.multiple_of(b * BLK, BLK), BLK)
        x = x_ref[rows, :].astype(f32)
        unit, rstd = norm_stats(x)
        n_ref[rows, :] = (unit * vec_ref[0:1, :] + vec_ref[1:2, :]).astype(bf16)
        first_lane = lax.broadcasted_iota(jnp.int32, (BLK, LANE), 1) == 0
        stat_ref[rows, :] = jnp.where(first_lane, jnp.mean(x, axis=-1, keepdims=True), rstd)

    copies.start(x_ref, x_out)
    copies.start(n_ref, n_hbm.at[both, :])
    if first:
        copies.wait(sine_load)
        pos_ref[...] = mm(sine_ref[...], wt_ref[2 * LANE : 3 * LANE, :], NT).astype(bf16)
    else:
        copies.wait(wt_load)
    lane = lax.broadcasted_iota(jnp.int32, (1, LANE), 1)
    is_head = lane < DH
    raw = mm(n_ref[...], wt_ref[0:LANE, :], NT)
    columns = rows_ref[m].T
    code = jnp.broadcast_to(columns[:, 0:1].astype(jnp.int32), (length, LANE))
    slot = jnp.where((lane >= DH) & (lane < DH + 2 * E), lane - DH, 31)
    pick = (lax.shift_right_logical(code, jnp.broadcast_to(slot, (length, LANE))) & 1) == 1
    gate = jnp.where(pick, 1.0 / (1.0 + jnp.exp(-raw)), 0.0)
    gate_ref[...] = gate
    copies.start(gate_ref, gate_hbm)
    qc_ref[...] = jnp.where(is_head, (raw + head_ref[0:1, :]) * SCALE, 0.0).astype(bf16)
    qp_ref[...] = jnp.where(is_head, (raw + head_ref[1:2, :]) * SCALE, 0.0).astype(bf16)
    keys = mm(n_ref[...], wt_ref[LANE : 2 * LANE, :], NT)
    k_ref[...] = jnp.where(is_head, keys, 0.0).astype(bf16)
    values = jnp.zeros((length, LANE), f32)
    for e in range(E):
        part = mm(n_ref[...], wt_ref[(3 + e) * LANE : (4 + e) * LANE, :], NT)
        va_ref[:, e * LANE : (e + 1) * LANE] = part.astype(bf16)
        values += part * gate[:, DH + e : DH + e + 1]
    v_ref[...] = values.astype(bf16)
    for src, dst in ((qc_ref, qc_hbm), (qp_ref, qp_hbm), (k_ref, k_hbm), (v_ref, v_hbm), (va_ref, va_hbm)):
        copies.start(src, dst)
    seg_col = columns[:, 1:2]
    for b in range(blocks):
        rows = slice(b * BLK, (b + 1) * BLK)
        wide = (b + 1) * BLK
        content = mm(qc_ref[rows, :], k_ref[0:wide, :], NT)
        table = mm(qp_ref[rows, :], pos_ref[length - wide : length, :], NT)
        table = pltpu.roll(table, (wide - BLK + 1) % wide, 1, stride=1, stride_axis=0)
        row = lax.broadcasted_iota(jnp.int32, (BLK, wide), 0) + b * BLK
        col = lax.broadcasted_iota(jnp.int32, (BLK, wide), 1)
        same = seg_col[rows, :] == rows_ref[m, 1:2, 0:wide]
        live = ((rows_ref[m, 2:3, 0:wide] > 0.0) & (col < row)) | (col == row)
        scores = jnp.where(same & live, content + table, MASKED)
        top = jnp.max(scores, axis=-1, keepdims=True)
        expo = jnp.exp(scores - top)
        prob = (expo / jnp.sum(expo, axis=-1, keepdims=True)).astype(bf16)
        p_ref[rows, 0:wide] = prob
        att = mm(prob, v_ref[0:wide, :])
        att_ref[rows, :] = att
        for e in range(E):
            share = gate_ref[rows, DH + E + e : DH + E + e + 1]
            mix_ref[rows, e * LANE : (e + 1) * LANE] = (att * share).astype(bf16)
        copies.start(p_ref.at[rows, 0:wide], p_hbm.at[rows, 0:wide])
    copies.start(att_ref, att_hbm)
    copies.start(mix_ref, mix_hbm.at[both, :])
    half = length // 2
    core = rank & 1
    copies.wait(*wo_loads)
    if first:
        copies.start(wo_ref, wop_hbm)
    for place, ref, dst in ((1 - core, send_ref, send_out), (core, keep_ref, keep_out)):
        rows = pl.ds(pl.multiple_of(place * half, half), half)
        ref[...] = mm(mix_ref[rows, :], wo_ref[...]).astype(bf16)
        copies.start(ref, dst)
    copies.finish()


def normal_terms(v):
    bell = jnp.exp(-0.5 * v * v)
    phi = 0.5 * (1.0 + lax.erf(v * (1.0 / math.sqrt(2.0))))
    return phi, bell * (1.0 / math.sqrt(2.0 * math.pi))


def pair_rows(core, b, refs):
    mine, far, mine2, far2 = refs
    own_half = (b // 2) == core
    rows = pl.ds(pl.multiple_of((b % 2) * BLK, BLK), BLK)
    near = mine[rows, :].astype(f32) + far[rows, :].astype(f32)
    away = mine2[rows, :].astype(f32) + far2[rows, :].astype(f32)
    return jnp.where(own_half, near, away)


def ffn_kernel(
    m,
    rank_ref,
    side_ref,
    x_hbm,
    a0,
    a1,
    a2,
    a3,
    vec_ref,
    bin_ref,
    win_hbm,
    win_core,
    *refs,
):
    (near2, near3, far2, far3), refs = refs[:4], refs[4:]
    (wout_hbm, c0, c1, c2, c3), refs = refs[:5], refs[5:]
    (n_hbm, hid_hbm, gp_hbm, cot_hbm, unit_hbm, rstd_ref, resid_ref, sum_ref), refs = (
        refs[:8],
        refs[8:],
    )
    (send_hbm, keep_hbm), refs = refs[:2], refs[2:]
    (unit_ref, win_ref, wout_ref, x_ref, n_ref, hid_ref, gp_ref, cot_ref), refs = refs[:8], refs[8:]
    halves, (send_ref, keep_ref, sems) = refs[:4], refs[4:]
    length = x_ref.shape[0]
    both = slice(m * length, (m + 1) * length)
    rank, place = rank_ref[0], side_ref[0]
    core = rank & 1
    copies = Copies(sems)
    size = D // H
    sum_ref[...] = jnp.zeros(sum_ref.shape, f32)

    def at(r, size):
        return pl.ds(pl.multiple_of((rank ^ r) * size, size), size)

    early = [copies.start(x_hbm, x_ref)]
    early += [copies.start(src, dst) for src, dst in zip((a0, a1, a2, a3), halves)]
    loads = []
    width = win_ref.shape[1]
    own_cols = pl.ds(pl.multiple_of(rank * width, width), width)
    loads.append(copies.start(win_hbm.at[:, own_cols], win_ref.at[at(0, size), :]))
    loads.append(copies.start(win_core, win_ref.at[at(1, size), :]))
    side = place % 2
    for r, half, ref in ((2, side, near2), (3, side, near3), (2, 1 - side, far2), (3, 1 - side, far3)):
        rows = pl.ds(pl.multiple_of((rank ^ r) * size + half * (size // 2), size // 2), size // 2)
        loads.append(copies.start(ref, win_ref.at[rows, :]))
    loads.append(copies.start(wout_hbm, wout_ref))
    for r, ref in enumerate((c0, c1, c2, c3)):
        loads.append(copies.start(ref.at[m], cot_ref.at[at(r, BLK), :]))

    copies.wait(*early)

    @pl.loop(0, length // BLK)
    def _(b):
        rows = pl.ds(pl.multiple_of(b * BLK, BLK), BLK)
        resid = x_ref[rows, :].astype(f32) + pair_rows(core, b, halves)
        unit, rstd = norm_stats(resid)
        unit_ref[rows, :] = unit.astype(bf16)
        rstd_ref[rows, :] = jnp.broadcast_to(rstd, (BLK, LANE))
        n_ref[rows, :] = (unit * vec_ref[2:3, :] + vec_ref[3:4, :]).astype(bf16)

        @pl.when(b == rank)
        def _():
            resid_ref[...] = resid

    copies.wait(*loads)
    for src, dst in (
        (unit_ref, unit_hbm),
        (n_ref, n_hbm.at[both, :]),
        (cot_ref, cot_hbm.at[both, :]),
    ):
        copies.start(src, dst)
    chunk = 256

    @pl.loop(0, width // chunk)
    def _(c):
        cols = pl.ds(pl.multiple_of(c * chunk, chunk), chunk)
        pre = mm(n_ref[...], win_ref[:, cols]) + bin_ref[0:1, cols]
        back = mm(cot_ref[...], wout_ref[cols, :], NT)
        phi, density = normal_terms(pre)
        hid_ref[:, cols] = (pre * phi).astype(bf16)
        grad = (back * (phi + pre * density)).astype(bf16)
        gp_ref[:, cols] = grad
        sum_ref[0:1, cols] = jnp.sum(grad.astype(f32), axis=0, keepdims=True)

    copies.start(hid_ref, hid_hbm.at[both, :])
    copies.start(gp_ref, gp_hbm.at[both, :])
    half = length // 2
    for place, ref, dst in ((1 - core, send_ref, send_hbm), (core, keep_ref, keep_hbm)):
        rows = pl.ds(pl.multiple_of(place * half, half), half)
        ref[...] = mm(gp_ref[rows, :], win_ref[...], NT).astype(bf16)
        copies.start(ref, dst)
    copies.finish()


def split_blocks(rank, value_ref, keep_ref, send_ref):
    for r in range(H):
        rows = pl.ds(pl.multiple_of((rank ^ r) * BLK, BLK), BLK)
        (send_ref if r % 2 else keep_ref)[r // 2] = value_ref[rows, :]


def project_kernel(rank_ref, side_ref, hid_hbm, wout_hbm, keep_hbm, send_hbm, *refs):
    hid_ref, wout_ref, full_ref, keep_ref, send_ref, sems = refs
    copies = Copies(sems)
    loads = [copies.start(wout_hbm, wout_ref), copies.start(hid_hbm, hid_ref)]
    copies.wait(*loads)
    full_ref[...] = mm(hid_ref[...], wout_ref[...]).astype(bf16)
    micro = keep_ref.shape[1]
    length = full_ref.shape[0] // micro
    for m in range(micro):
        for r in range(H):
            at = pl.multiple_of((rank_ref[0] ^ r) * BLK + m * length, BLK)
            ref = send_ref if r % 2 else keep_ref
            ref[r // 2, m] = full_ref[pl.ds(at, BLK), :]
    copies.start(keep_ref, keep_hbm)
    copies.start(send_ref, send_hbm)
    copies.finish()


def branch_kernel(m, rank_ref, side_ref, vec_ref, rstd_ref, gate_ref, att_ref, *refs):
    hbm, refs = refs[:7], refs[7:]
    (gb_hbm, sums_ref, grad_ref, ga_ref, logit_ref), refs = refs[:5], refs[5:]
    held, (gb_ref, sems) = refs[:7], refs[7:]
    copies = Copies(sems)
    *halves, cot_ref, unit_ref, wo_ref = held
    length = unit_ref.shape[0]
    both = slice(m * length, (m + 1) * length)
    hbm = [*hbm[:4], hbm[4].at[both, :], *hbm[5:]]
    *loads, wo_load = [copies.start(src, dst) for src, dst in zip(hbm, held)]
    rank = rank_ref[0]
    core = rank & 1
    sums_ref[...] = jnp.zeros(sums_ref.shape, f32)
    copies.wait(*loads)

    @pl.loop(0, length // BLK)
    def _(b):
        rows = pl.ds(pl.multiple_of(b * BLK, BLK), BLK)
        unit = unit_ref[rows, :].astype(f32)
        grad = pair_rows(core, b, halves)
        sums_ref[0:1, :] += jnp.sum(grad * unit, axis=0, keepdims=True)
        sums_ref[1:2, :] += jnp.sum(grad, axis=0, keepdims=True)
        cot = cot_ref[rows, :].astype(f32)
        sums_ref[2:3, :] += jnp.sum(cot, axis=0, keepdims=True)
        total = cot + norm_back(grad, unit, rstd_ref[rows, 0:1], vec_ref[2:3, :])
        gb_ref[rows, :] = total.astype(bf16)

        @pl.when(b == rank)
        def _():
            grad_ref[...] = total

    copies.start(gb_ref, gb_hbm.at[both, :])
    copies.wait(wo_load)
    lane = lax.broadcasted_iota(jnp.int32, (1, LANE), 1)
    acc = jnp.zeros((length, LANE), f32)
    logits = jnp.zeros((length, LANE), f32)
    for e in range(E):
        mixed = mm(gb_ref[...], wo_ref[e * LANE : (e + 1) * LANE, :], NT)
        acc += mixed * gate_ref[:, DH + E + e : DH + E + e + 1]
        dot = jnp.sum(mixed * att_ref[...], axis=-1, keepdims=True)
        logits = jnp.where(lane == DH + E + e, dot, logits)
    ga_ref[...] = acc.astype(bf16)
    logit_ref[...] = logits
    copies.finish()


def back_kernel(m, rank_ref, side_ref, ga_ref, logit_ref, pos_ref, gate_ref, stat_ref, *refs):
    hbm, refs = refs[:8], refs[8:]
    (sums_ref, dproj_hbm, gpos_ref, bias_ref, keep_hbm, send_hbm), refs = refs[:6], refs[6:]
    held, refs = refs[:8], refs[8:]
    dproj_ref, gk_ref, gv_ref, full_ref, keep_ref, send_ref, sems = refs
    copies = Copies(sems)
    *loads, va_load, wt_load, x_load = [copies.start(src, dst) for src, dst in zip(hbm, held)]
    p_ref, v_ref, k_ref, qc_ref, qp_ref, va_ref, wt_ref, x_ref = held
    length = x_ref.shape[0]
    blocks = length // BLK
    rank = rank_ref[0]
    lane = lax.broadcasted_iota(jnp.int32, (1, LANE), 1)
    sums_ref[...] = jnp.zeros(sums_ref.shape, f32)
    gk_ref[...] = jnp.zeros(gk_ref.shape, f32)
    gv_ref[...] = jnp.zeros(gv_ref.shape, f32)
    gpos_ref[...] = jnp.zeros(gpos_ref.shape, f32)
    row = lax.broadcasted_iota(jnp.int32, (BLK, BLK), 0)
    col = lax.broadcasted_iota(jnp.int32, (BLK, BLK), 1)
    mirror = jnp.where(row + col == BLK - 1, 1.0, 0.0).astype(bf16)
    cont_sum = jnp.zeros((1, LANE), f32)
    posn_sum = jnp.zeros((1, LANE), f32)
    copies.wait(*loads)
    for b in range(blocks):
        rows = slice(b * BLK, (b + 1) * BLK)
        wide = (b + 1) * BLK
        prob = p_ref[rows, 0:wide].astype(f32)
        ga = ga_ref[rows, :]
        grad_prob = mm(ga, v_ref[0:wide, :], NT)
        delta = jnp.sum(prob * grad_prob, axis=-1, keepdims=True)
        grad_score = (prob * (grad_prob - delta)).astype(bf16)
        gv_ref[0:wide, :] += mm(p_ref[rows, 0:wide], ga, TN)
        gk_ref[0:wide, :] += mm(grad_score, qc_ref[rows, :], TN)
        cont = mm(grad_score, k_ref[0:wide, :]) * SCALE
        table = pltpu.roll(mm(mirror, grad_score), 0, 1, stride=1, stride_axis=0)
        table = mm(mirror, table.astype(bf16)).astype(bf16)
        posn = mm(table, pos_ref[length - wide : length, :]) * SCALE
        gpos_ref[length - wide : length, :] += mm(table, qp_ref[rows, :], TN)
        cont_sum += jnp.sum(cont, axis=0, keepdims=True)
        posn_sum += jnp.sum(posn, axis=0, keepdims=True)
        dproj_ref[rows, 0:LANE] = (cont + posn).astype(bf16)
    bias_ref[...] = jnp.zeros(bias_ref.shape, f32)
    bias_ref[0:1, :] = cont_sum
    bias_ref[1:2, :] = posn_sum
    dproj_ref[:, LANE : 2 * LANE] = gk_ref[...].astype(bf16)
    dproj_ref[:, 2 * LANE : 3 * LANE] = jnp.zeros((length, LANE), bf16)
    copies.wait(va_load, wt_load, x_load)
    grad_values = gv_ref[...].astype(bf16).astype(f32)
    logits = logit_ref[...]
    for e in range(E):
        cols = slice((3 + e) * LANE, (4 + e) * LANE)
        dproj_ref[:, cols] = (grad_values * gate_ref[:, DH + e : DH + e + 1]).astype(bf16)
        dot = jnp.sum(grad_values * va_ref[:, e * LANE : (e + 1) * LANE].astype(f32), axis=-1, keepdims=True)
        logits = jnp.where(lane == DH + e, dot, logits)
    gate = gate_ref[...]
    logits = logits * gate * (1.0 - gate)
    dproj_ref[:, 0:LANE] = jnp.where(
        lane < DH, dproj_ref[:, 0:LANE].astype(f32), logits
    ).astype(bf16)
    copies.start(dproj_ref, dproj_hbm.at[m * length : (m + 1) * length, :])
    chunk = 256
    mean, rstd = stat_ref[:, 0:1], stat_ref[:, 1:2]

    @pl.loop(0, D // chunk)
    def _(c):
        cols = pl.ds(pl.multiple_of(c * chunk, chunk), chunk)
        part = mm(dproj_ref[...], wt_ref[:, cols])
        full_ref[:, cols] = part.astype(bf16)
        unit = (x_ref[:, cols].astype(f32) - mean) * rstd
        sums_ref[3:4, cols] = jnp.sum(part * unit, axis=0, keepdims=True)
        sums_ref[4:5, cols] = jnp.sum(part, axis=0, keepdims=True)

    split_blocks(rank, full_ref, keep_ref, send_ref)
    copies.start(send_ref, send_hbm)
    copies.start(keep_ref, keep_hbm)
    copies.finish()


def output_kernel(rank_ref, side_ref, vec_ref, keep_ref, got_ref, far_ref, *refs):
    *refs, y_hbm, done_ref, y_ref, sems = refs
    done_ref[...] = jnp.zeros(done_ref.shape, f32)
    for m in range(y_ref.shape[0]):
        total = refs[m][...] + keep_ref[0, m].astype(f32) + got_ref[0, m].astype(f32)
        y_ref[m, 0] = (total + far_ref[m].astype(f32) + vec_ref[4:5, :]).astype(bf16)
    copies = Copies(sems)
    copies.start(y_ref, y_hbm)
    copies.finish()


def input_kernel(rank_ref, side_ref, x_ref, vec_ref, far_ref, *refs):
    y_ref = refs[-1]
    for m in range(y_ref.shape[0]):
        grad_ref, keep_ref, got_ref = refs[3 * m : 3 * m + 3]
        unit, rstd = norm_stats(x_ref[m].astype(f32))
        back = keep_ref[0].astype(f32) + got_ref[0].astype(f32) + far_ref[m].astype(f32)
        y_ref[m, 0] = grad_ref[...] + norm_back(back, unit, rstd, vec_ref[0:1, :])


def vectors_kernel(
    rank_ref, side_ref, sums0, sums1, norm0, norm1, bias0, bias1, hid0, hid1, y_ref
):
    y_ref[...] = jnp.zeros(y_ref.shape, f32)
    width = D // H
    own = pl.ds(pl.multiple_of(rank_ref[0] * width, width), width)
    y_ref[0, 6:7, :] = norm0[3:4, :] + norm1[3:4, :]
    y_ref[1, 6:7, :] = norm0[4:5, :] + norm1[4:5, :]
    for i in range(3):
        y_ref[i, 7:8, own] = sums0[i : i + 1, own] + sums1[i : i + 1, own]
    for i in range(2):
        cols = pl.ds(pl.multiple_of(rank_ref[0] * width + i * LANE, LANE), LANE)
        y_ref[3, 7:8, cols] = bias0[i : i + 1, :] + bias1[i : i + 1, :]
    for i in range(4):
        cols = slice(i * width, (i + 1) * width)
        y_ref[4 + i, 7:8, own] = hid0[0:1, cols] + hid1[0:1, cols]


def load_ffn_chunk(copies, c, sources, dst):
    grad_o, grad_i = sources
    rows = D // RING
    part = rows // H
    copies.start(grad_o.at[pl.ds(pl.multiple_of(c * rows, rows), rows), :], dst.at[0:rows, :])
    for s in range(H):
        src = pl.ds(pl.multiple_of(s * (D // H) + c * part, part), part)
        copies.start(grad_i.at[src, :], dst.at[rows + s * part : rows + (s + 1) * part, :])


def load_pack_chunk(copies, c, sources, dst):
    grad_p, grad_w = sources
    rows = D // RING
    part = E * LANE // RING
    copies.start(grad_p.at[pl.ds(pl.multiple_of(c * rows, rows), rows), :], dst.at[0:rows, :])
    copies.start(
        grad_w.at[pl.ds(pl.multiple_of(c * part, part), part), :], dst.at[rows : rows + part, :]
    )


def ring_kernel(load, split, t, rank_ref, pos_ref, src0, src1, *refs):
    tail_ref, refs = (refs[0], refs[1:]) if load is load_pack_chunk else (None, refs)
    got_hbm, refs = (refs[:2], refs[2:]) if t else ((), refs)
    outs_hbm, refs = (refs[:2], refs[2:]) if t < 4 else (refs[: 1 + H], refs[1 + H :])
    loaded, held, *more, sems = refs
    got, outs = more[: len(got_hbm)], more[len(got_hbm) :]
    copies = Copies(sems)
    for src, dst in zip(got_hbm, got):
        copies.start(src, dst)
    pos = pos_ref[0]
    total = held.shape[1]
    chunks = [(pos + 4 - t) % RING, (pos + 4 + t) % RING][: 2 if t < 4 else 1]
    for i, c in enumerate(chunks[: 2 if t < 4 else 1]):
        load(copies, c, (src0, src1), loaded.at[i])
    copies.finish()
    held[...] = loaded[...].astype(f32)
    if tail_ref is not None:
        for i, c in enumerate(chunks):
            rows = slice(D // RING - TAIL, D // RING)
            held[i, rows, :] = held[i, rows, :] + tail_ref[c]
    if t == 4:
        held[0] = held[0] + got[0][...].astype(f32) + got[1][...].astype(f32)
        rows = D // RING
        rank = rank_ref[0]
        for r, ref in enumerate(outs[1:]):
            if tail_ref is None:
                size = rows // H
                at = pl.multiple_of(rows + (rank ^ r) * size, size)
                ref[...] = held[0, pl.ds(at, size), :].astype(bf16)
            else:
                size = D // H
                at = pl.multiple_of((rank ^ r) * size, size)
                ref[...] = held[0, 0:rows, pl.ds(at, size)].astype(bf16)
        outs[0][...] = (held[0, 0:rows, :] if tail_ref is None else held[0, rows:total, :]).astype(bf16)
        for ref, dst in zip(outs, outs_hbm):
            copies.start(ref, dst)
        copies.finish()
        return
    for i, ref in enumerate(outs):
        part = slice(0, split) if i == 0 else slice(split, total)
        if t == 0:
            ref[...] = held[i, part, :].astype(bf16)
        elif t == 1:
            ref[...] = held[i].astype(bf16)
            ref[part, :] = (held[i, part, :] + got[i][...].astype(f32)).astype(bf16)
        else:
            ref[...] = (held[i] + got[i][...].astype(f32)).astype(bf16)
        copies.start(ref, outs_hbm[i])
    copies.finish()


def load_ring(copies, pos, split, refs, dst):
    own, fwd, bwd, half_fwd, half_bwd = refs[0], refs[1:4], refs[4:7], refs[7], refs[8]
    copies.start(own, dst.at[pos])
    for i in range(3):
        copies.start(fwd[i], dst.at[(pos + RING - 1 - i) % RING])
        copies.start(bwd[i], dst.at[(pos + 1 + i) % RING])
    last = (pos + 4) % RING
    copies.start(half_fwd, dst.at[last, 0:split, :])
    copies.start(half_bwd, dst.at[last, split : dst.shape[1], :])
    copies.finish()


def ffn_grads_kernel(split, rank_ref, pos_ref, *refs):
    parts, (o_hbm, i_hbm, done_ref, held, o_ref, i_ref, sems) = refs[:9], refs[9:]
    done_ref[...] = jnp.zeros(done_ref.shape, f32)
    copies = Copies(sems)
    load_ring(copies, pos_ref[0], split, parts, held)
    rows = D // RING
    part = rows // H
    for c in range(RING):
        o_rows = slice(c * rows, (c + 1) * rows)
        o_ref[o_rows, :] = held[c, 0:rows, :].astype(f32)
        copies.start(o_ref.at[o_rows, :], o_hbm.at[o_rows, :])
        i_rows = slice(c * part, (c + 1) * part)
        for r in range(H):
            cols = pl.ds(pl.multiple_of((rank_ref[0] ^ r) * D, D), D)
            at = rows + r * part
            i_ref[i_rows, cols] = held[c, at : at + part, :].astype(f32)
        copies.start(i_ref.at[i_rows, :], i_hbm.at[i_rows, :])
    copies.finish()


def pack_grads_kernel(split, rank_ref, pos_ref, *refs):
    parts, refs = refs[:9], refs[9:]
    (q_ref, rv_ref, ro_ref, k_ref, p_ref, v_ref, w_ref), refs = refs[:7], refs[7:]
    (g1, b1, g2, b2, bo, content, posn, bin_ref), refs = refs[:8], refs[8:]
    held, heads, sems = refs
    copies = Copies(sems)
    load_ring(copies, pos_ref[0], split, parts, held)
    width = D // H
    rank = rank_ref[0]
    for r in range(H):
        heads[rank ^ r] = held[:, 0:LANE, r * width : (r + 1) * width].astype(f32)
    for h in range(H):
        rows = slice(h * DH, (h + 1) * DH)
        q_ref[rows, :] = heads[h, 0, 0:DH, :]
        rv_ref[h * E : (h + 1) * E, :] = heads[h, 0, DH : DH + E, :]
        ro_ref[h * E : (h + 1) * E, :] = heads[h, 0, DH + E : DH + 2 * E, :]
        k_ref[rows, :] = heads[h, 1, 0:DH, :]
        p_ref[rows, :] = heads[h, 2, 0:DH, :]
        for e in range(E):
            at = (h * E + e) * DH
            v_ref[at : at + DH, :] = heads[h, 3 + e, 0:DH, :]
    part = E * LANE // RING
    for c in range(RING):
        for e in range(E):
            low, high = max(c * part, e * LANE), min((c + 1) * part, e * LANE + DH)
            if low < high:
                at = low - e * LANE + e * DH
                w_ref[at : at + high - low, :] = held[
                    c, LANE + low - c * part : LANE + high - c * part, :
                ].astype(f32)
    last = slice(LANE - 1, LANE)
    before = slice(LANE - 2, LANE - 1)
    for ref, c in ((g1, 0), (b1, 1)):
        ref[...] = sum(heads[h, c, before, :] for h in range(H)).reshape(ref.shape)
    for c, ref in enumerate((g2, b2, bo)):
        ref[...] = heads[rank, c, last, :].reshape(ref.shape)
    row = heads[rank, 3, last, :]
    content[...] = row[:, 0:DH].reshape(content.shape)
    posn[...] = row[:, LANE : LANE + DH].reshape(posn.shape)
    for i in range(4):
        bin_ref[i * width : (i + 1) * width] = heads[rank, 4 + i, last, :].reshape((width,))


def flip_shard(value, bit):
    return lax.ppermute(value, "shard", [(s, s ^ bit) for s in range(H)])


def flip_dp(value, bit):
    count = lax.axis_size("dp")
    return lax.ppermute(value, "dp", [(d, d ^ bit) for d in range(count)])


def take(value, at, size, axis=0):
    return lax.dynamic_slice_in_dim(value, at, size, axis)


def put(value, part, at, axis=0):
    return lax.dynamic_update_slice_in_dim(value, part, at, axis)


def spread(own):
    across = flip_shard(own, 2)
    return own, flip_shard(own, 1), across, flip_shard(across, 1)


def ring_order():
    return list(range(0, RING, 2)) + list(range(RING - 1, 0, -2))


def pass_on(value, way):
    order, count = ring_order(), lax.axis_size("dp")
    pairs = [
        (base + order[i], base + order[(i + way) % RING])
        for base in range(0, count, RING)
        for i in range(RING)
    ]
    return lax.ppermute(value, "dp", pairs)


def swap_shard(value, rank, size, axis):
    parts = [take(value, (rank ^ r) * size, size, axis) for r in range(H)]
    return [flip_shard(p, r) if r else p for r, p in enumerate(parts)]


def sinusoid(length, feature_count):
    distance = (length - 1 - jnp.arange(length, dtype=jnp.int32)).astype(f32)
    inv_freq = jnp.exp(
        jnp.arange(0, feature_count, 2, dtype=jnp.int32).astype(f32)
        * (-math.log(10000.0) / feature_count)
    )
    angles = distance[:, None] * inv_freq[None, :]
    return jnp.concatenate([jnp.sin(angles), jnp.cos(angles)], axis=1)


def local(
    inputs,
    segments,
    padding,
    routes_value,
    routes_output,
    norm1_gain,
    norm1_bias,
    query_weight,
    key_weight,
    pos_weight,
    content_bias,
    pos_bias,
    value_router,
    output_router,
    value_experts,
    output_experts,
    norm2_gain,
    norm2_bias,
    ffn_in,
    ffn_in_bias,
    ffn_out,
    ffn_out_bias,
    cotangent,
):
    micro = inputs.shape[0]
    own = inputs.shape[2]
    length = own * H
    dp_count = lax.axis_size("dp")
    rank = lax.axis_index("shard")
    me = rank.astype(jnp.int32).reshape(1)
    dp_rank = lax.axis_index("dp")
    side = (dp_rank % RING).astype(jnp.int32).reshape(1)
    place = dp_rank % RING
    place = jnp.where(place % 2 == 0, place // 2, RING - 1 - place // 2)
    place = place.astype(jnp.int32).reshape(1)
    quarter = D // H

    token = [me]

    def after(value, *deps):
        return lax.optimization_barrier((value, *deps))[0]

    def step(fn, first, *rest):
        res = fn(after(first, token[0]), *rest)
        token[0] = jax.tree.leaves(res)[0]
        return res

    def kernel(fn, outs, args, second=side, **kwargs):
        deps = [*kwargs.pop("deps", ()), *([] if token[0] is me else [token[0]])]
        res = call(fn, outs, [me, second, *args], deps=deps, **kwargs)
        token[0] = min(res, key=lambda r: r.size)
        return res

    packs = kernel(
        prep_kernel,
        [out((PACK, quarter), bf16)] * 2
        + [out((PACK, LANE), bf16)] * 2
        + [out((8, LANE), f32), out((1, FF // H), f32)]
        + [out((quarter, FF // H), bf16)]
        + [out((quarter // 2, FF // H), bf16)] * 2
        + [out((own, D), bf16)] * micro,
        [
            Far(a)
            for a in (
                inputs,
                ffn_in,
                query_weight.T,
                key_weight.T,
                pos_weight.T,
                value_router.T,
                output_router.T,
                value_experts.T,
                routes_value[:, 0].transpose(0, 2, 3, 1),
                routes_output[:, 0].transpose(0, 2, 3, 1),
                segments,
                padding,
                norm1_gain,
                norm1_bias,
                norm2_gain,
                norm2_bias,
                ffn_out_bias,
                content_bias,
                pos_bias,
                ffn_in_bias,
            )
        ],
        scratch=[
            pltpu.VMEM(shape, dtype)
            for shape, dtype in [((H * DH, quarter), bf16)] * 3
            + [((H * E, quarter), bf16)] * 2
            + [((H * E * DH, quarter), bf16)]
            + [((micro, H, 2, own), jnp.int32)] * 2
            + [((micro, 1, own), jnp.int32)] * 2
            + [((quarter,), bf16)] * 5
            + [((DH,), bf16)] * 2
            + [((FF // H,), bf16)]
            + [((LANE - DH, quarter), f32), ((PACK, quarter), bf16)]
        ],
        copies=18 + 3 + micro,
        vmem=56,
    )
    sine = sinusoid(length, D).astype(bf16)
    head, b_in, core_in, *sent = packs[H:]
    sent_in, sent_x = sent[:2], sent[2:]
    near = [flip_shard(packs[r], r) for r in (2, 3)]
    w_core = flip_shard(packs[1], 1)
    far = [flip_dp(w, 1) for w in near]
    weights = [packs[0], w_core, *near, *far]
    x_own = inputs[:, 0]
    sent_x[0] = gate(sent_x[0], [*near, sine])
    x_parts = [spread(x) for x in sent_x]
    near_in = [flip_shard(w, r) for w, r in zip(sent_in, (2, 3))]
    w_in_core = flip_shard(core_in, 1)
    cot_parts = spread(cotangent[:, 0])

    def add_chip(keep, send):
        got = flip_shard(send, 1)
        add = lambda k, g: (k.astype(f32) + g.astype(f32)).astype(bf16)
        return step(add, keep, got)

    def finish_halves(chip):
        across = flip_shard(chip, 2)
        return chip, across, flip_shard(chip, 1), flip_shard(across, 1)

    half = out((length // 2, D), bf16)
    wide = out((length, D), bf16)
    saved_shapes = (
        [wide]
        + [out((length, LANE), bf16)] * 4
        + [
            out((length, E * LANE), bf16),
            out((length, LANE), f32),
            out((length, length), bf16),
            out((length, LANE), f32),
            out((length, E * LANE), bf16),
        ]
    )
    vmem_of = lambda shapes: [pltpu.VMEM(o.shape, o.dtype) for o in shapes]
    weight_shapes = [out((PACK, D), bf16), out((E * LANE, D), bf16)]
    joined = out((micro * length, D), bf16)
    saved = []
    residuals = []
    for m in range(micro):
        if m == 0:
            more = [Far(w) for w in weights] + [Far(sine), Far(output_experts)]
            extra = [Far(o) for o in weight_shapes]
            extra += [out((length, LANE), bf16), out((8, D), f32), out((micro, 8, length), f32)]
        else:
            more = [Far(wt), Far(w_out_heads), pos, vec, rows]
            extra = []
        res = kernel(
            functools.partial(attention_kernel, m),
            [Far(wide)]
            + [Far(joined)]
            + [Far(o) for o in saved_shapes[1:-1]]
            + [Far(out((micro * length, E * LANE), bf16))]
            + [out((length, LANE), f32), Far(half), Far(half)]
            + extra,
            [Far(x) for x in (x_own, *x_parts[m][1:])] + [head] + more,
            scratch=vmem_of(
                saved_shapes + weight_shapes + [wide, half, half] + ([wide] if m == 0 else [])
            ),
            copies=40,
            into={1: saved[0][1], 10: saved[0][10]} if m else None,
            deps=[*near_in, residuals[0][0]] if m else [],
            vmem=60,
            flops=2 * length * D * 1700,
        )
        saved.append(res[:12])
        if m == 0:
            near_in = [gate(w, [res[12]]) for w in near_in]
            far_in = [flip_dp(w, 1) for w in near_in]
        send, keep = res[12:14]
        if m == 0:
            wt, w_out_heads, pos, vec, rows = res[14:]
            send = gate(send, [*near_in, *x_parts[1][1:3]][: 4])
        else:
            send = gate(send, [*far_in, cot_parts[2], residuals[0][1]])
        residuals.append(finish_halves(add_chip(keep, send)))
    ffn = []
    gn2 = []
    for m in range(micro):
        res = kernel(
            functools.partial(ffn_kernel, m),
            [Far(joined)] * 4
            + [Far(wide)]
            + [
                out((length, LANE), f32),
                out((own, D), f32),
                out((8, FF // H), f32),
                Far(half),
                Far(half),
            ],
            [Far(a) for a in (saved[m][0], *residuals[m])]
            + [vec, b_in]
            + [Far(w) for w in (ffn_in, w_in_core, *near_in, *far_in, ffn_out, *cot_parts)],
            scratch=vmem_of(
                [wide, out((D, FF // H), bf16), out((FF // H, D), bf16)] + [wide] * 5 + [half] * 6
            ),
            copies=30,
            into={i: ffn[0][i] for i in range(4)} if m else None,
            vmem=60,
            deps=[residuals[1][0] if m == 0 else gn2[0][0]],
            flops=2 * length * D * D * 3,
        )
        ffn.append(res)
        gn2.append(finish_halves(add_chip(res[-1], res[-2])))

    def tn(a, b):
        return mm(a, b, TN).astype(bf16)

    class Ring:
        def __init__(self, load, split, total, sources):
            self.load, self.split, self.total = load, split, total
            self.sources, self.got, self.t = sources, (), 0

        def step(self, deps=()):
            rows = D // RING
            if self.t == 0:
                shapes = [(self.split, D), (self.total - self.split, D)]
            elif self.t < 4:
                shapes = [(self.total, D)] * 2
            elif len(self.sources) == 2:
                shapes = [(rows, D)] + [(rows // H, D)] * H
            else:
                shapes = [(self.total - rows, D)] + [(rows, D // H)] * H
            shapes = [out(shape, bf16) for shape in shapes]
            res = kernel(
                functools.partial(ring_kernel, self.load, self.split, self.t),
                [Far(o) for o in shapes],
                [Far(g) for g in self.sources[:2]]
                + list(self.sources[2:])
                + [Far(g) for g in self.got],
                second=place,
                scratch=[pltpu.VMEM((2, self.total, D), bf16), pltpu.VMEM((2, self.total, D), f32)]
                + vmem_of(self.got)
                + vmem_of(shapes),
                copies=20,
                deps=deps,
                vmem=56,
            )
            self.t += 1
            self.sent = res[0]
            if self.t == 5:
                return [self.across(p) for p in res]
            self.got = (pass_on(res[0], 1), pass_on(res[1], -1))

        def across(self, piece):
            bit = RING
            while bit < dp_count:
                piece = (piece.astype(f32) + flip_dp(piece, bit).astype(f32)).astype(bf16)
                bit *= 2
            return piece

        def gather(self, piece):
            self.parts = [[piece], [piece]]
            self.cuts = []
            self.pass_parts()

        def pass_parts(self):
            for way, parts in zip((1, -1), self.parts):
                value = parts[-1]
                if len(parts) == 4:
                    value = value[: self.split] if way == 1 else value[self.split :]
                    self.cuts.append(value)
                parts.append(pass_on(value, way))

        def result(self):
            fwd, bwd = self.parts
            return [fwd[0], *fwd[1:4], *bwd[1:4], fwd[4], bwd[4]]

    n2, hid, gp, cots = ffn[1][:4]
    grad_o = tn(hid, cots)
    grad_i = tn(n2, gp)
    ffn_ring = Ring(load_ffn_chunk, D // RING, 2 * D // RING, [grad_o, grad_i])
    ffn_ring.step()
    back = []

    branch = []

    def run_branch(m, deps=()):
        gate_m, att, rstd = saved[m][7], saved[m][9], ffn[m][5]
        from_far = [*gn2[m], ffn[1][3], ffn[m][4], w_out_heads]
        branch.append(
            kernel(
                functools.partial(branch_kernel, m),
                [
                    Far(joined),
                    out((8, D), f32),
                    out((own, D), f32),
                    out((length, LANE), bf16),
                    out((length, LANE), f32),
                ],
                [vec, rstd, gate_m, att] + [Far(a) for a in from_far],
                copies=10,
                vmem=56,
                deps=deps,
                scratch=vmem_of([*from_far[:4], wide, *from_far[5:], wide]),
                into={0: branch[0][0]} if m else None,
            )
        )

    def run_back(m, deps=()):
        x, n1, qc, qp, k, v, va, gate_m, prob, att, mix, stat = saved[m]
        from_far = [prob, v, k, qc, qp, va, wt, x]
        back.append(
            kernel(
                functools.partial(back_kernel, m),
                [
                    out((8, D), f32),
                    Far(out((micro * length, PACK), bf16)),
                    out((length, LANE), f32),
                    out((8, LANE), f32),
                    Far(out((2, own, D), bf16)),
                    Far(out((2, own, D), bf16)),
                ],
                [branch[m][3], branch[m][4], pos, gate_m, stat] + [Far(a) for a in from_far],
                copies=12,
                into={1: back[0][1]} if m else None,
                vmem=56,
                deps=deps,
                scratch=vmem_of(from_far)
                + [
                    pltpu.VMEM((length, PACK), bf16),
                    pltpu.VMEM((length, LANE), f32),
                    pltpu.VMEM((length, LANE), f32),
                    pltpu.VMEM((length, D), bf16),
                    pltpu.VMEM((2, own, D), bf16),
                    pltpu.VMEM((2, own, D), bf16),
                ],
            )
        )

    run_branch(0)
    ffn_ring.step()
    run_back(0)
    ffn_ring.step()
    run_branch(1)
    ffn_ring.step()
    grad_w = tn(saved[1][10], branch[1][0])
    run_back(1, deps=[grad_w])
    turned = lambda parts: [flip_shard(p, r) if r else p for r, p in enumerate(parts)]
    piece, *parts = ffn_ring.step()
    ffn_piece = jnp.concatenate([piece, *turned(parts)])
    gpos = (back[0][2] + back[1][2]).astype(bf16)
    grad_p = tn(gate(back[1][1], [piece]), saved[1][1])
    grad_p = lax.dynamic_update_slice(grad_p, tn(gpos, sine), (2 * LANE, 0))
    tails = kernel(
        vectors_kernel,
        [out((RING, TAIL, D), f32)],
        [branch[0][1], branch[1][1], back[0][0], back[1][0], back[0][3], back[1][3]]
        + [ffn[0][7], ffn[1][7]],
    )[0]
    pack_ring = Ring(
        load_pack_chunk, DH, D // RING + E * LANE // RING, [grad_p, grad_w, tails]
    )
    ffn_ring.gather(ffn_piece)
    pack_ring.step()
    add = lambda a, b: (a.astype(f32) + b.astype(f32)).astype(bf16)
    gx_got = [flip_shard(back[m][5], 1) for m in range(micro)]
    gx_far = jnp.stack([add(back[m][4][1], gx_got[m][1]) for m in range(micro)])
    gx_far = flip_shard(gx_far, 2)
    came = lambda i: [p[i] for p in ffn_ring.parts]
    both_ways = ffn_ring.parts
    both_ways[0][1] = gate(both_ways[0][1], [pack_ring.sent, both_ways[1][1]])
    ffn_ring.pass_parts()
    pack_ring.step()
    pack_ring.step(deps=came(2))
    ffn_ring.pass_parts()
    pack_ring.step()
    gx_all = kernel(
        input_kernel,
        [out((micro, 1, own, D), f32)],
        [x_own, vec, gx_far]
        + [a for m in range(micro) for a in (branch[m][2], back[m][4], gx_got[m])],
    )[0]
    ffn_ring.pass_parts()
    piece, *parts = pack_ring.step(deps=ffn_ring.cuts)
    parts[0] = gate(parts[0], came(4))
    pack_piece = jnp.concatenate([jnp.concatenate(turned(parts), axis=1), piece])
    pack_ring.gather(pack_piece)
    ways = pack_ring.parts
    sides = out((2, micro, own, D), bf16)
    keep, send = kernel(
        project_kernel,
        [Far(sides)] * 2,
        [Far(hid), Far(ffn_out)],
        scratch=vmem_of([joined, out((FF // H, D), bf16), joined, sides, sides]),
        copies=4,
        vmem=56,
        deps=[pack_piece],
    )
    ways[0][1] = gate(ways[0][1], [keep, ways[1][1]])
    got = flip_shard(gate(send, [ways[0][1]]), 1)
    far = flip_shard(add(keep[1], got[1]), 2)
    pack_ring.pass_parts()
    g_out, g_in, done = kernel(
        functools.partial(ffn_grads_kernel, ffn_ring.split),
        [Far(out((FF // H, D), f32)), Far(out((quarter, FF), f32)), out((8, LANE), f32)],
        [Far(p) for p in ffn_ring.result()],
        second=place,
        scratch=[
            pltpu.VMEM((RING, ffn_ring.total, D), bf16),
            pltpu.VMEM((FF // H, D), f32),
            pltpu.VMEM((quarter, FF), f32),
        ],
        copies=25,
        vmem=60,
        deps=[ways[0][1]],
    )
    ways[0][2] = gate(ways[0][2], [done, ways[1][2]])
    pack_ring.pass_parts()
    pack_ring.pass_parts()
    y_all = kernel(
        output_kernel,
        [Far(out((micro, 1, own, D), bf16)), out((8, LANE), f32)],
        [vec, keep, got, far] + [ffn[m][6] for m in range(micro)],
        scratch=[pltpu.VMEM((micro, 1, own, D), bf16)],
        copies=1,
    )[0]
    res = kernel(
        functools.partial(pack_grads_kernel, pack_ring.split),
        [
            out((H * DH, quarter), f32),
            out((H * E, quarter), f32),
            out((H * E, quarter), f32),
            out((H * DH, quarter), f32),
            out((H * DH, quarter), f32),
            out((H * E * DH, quarter), f32),
            out((E * DH, D), f32),
        ]
        + [out((quarter,), f32)] * 5
        + [out((DH,), f32)] * 2
        + [out((FF // H,), f32)],
        [Far(p) for p in pack_ring.result()],
        second=place,
        scratch=[
            pltpu.VMEM((RING, pack_ring.total, D), bf16),
            pltpu.VMEM((H, RING, LANE, quarter), f32),
        ],
        copies=9,
        vmem=40,
    )
    g_q, g_rv, g_ro, g_k, g_p, g_v, g_wo, g1, b1, g2, b2, bo, content, posb, bi = res
    return (
        y_all,
        gx_all,
        g1,
        b1,
        g_q.T,
        g_k.T,
        g_p.T,
        content,
        posb,
        g_rv.T,
        g_ro.T,
        g_v.T,
        g_wo,
        g2,
        b2,
        g_in,
        bi,
        g_out,
        bo,
    )


def solution(mesh):
    tokens = P(None, "dp", "shard")
    whole = P(None, "dp", "shard", None)
    routes = P(None, "dp", "shard", None, None)
    vector = P("shard")
    matrix = P("shard", None)
    weights = (
        vector,
        vector,
        matrix,
        matrix,
        matrix,
        vector,
        vector,
        matrix,
        matrix,
        matrix,
        matrix,
        vector,
        vector,
        matrix,
        vector,
        matrix,
        vector,
    )
    return jax.shard_map(
        local,
        mesh=mesh,
        in_specs=(whole, tokens, tokens, routes, routes) + weights + (whole,),
        out_specs=(whole, whole) + weights,
        check_vma=False,
    )
```

```python
import functools
import math

import jax
import jax.numpy as jnp
from jax import lax
from jax.experimental import pallas as pl
from jax.experimental.pallas import tpu as pltpu
from jax.sharding import PartitionSpec as P

D = 1024
H = 4
DH = 112
E = 5
FF = 4096
LANE = 128
PACK = 1024
BLK = 128
RING = 8
TAIL = 8
MASKED = -1e30
SCALE = DH ** (-0.5)
bf16 = jnp.bfloat16
f32 = jnp.float32
NN = (((1,), (0,)), ((), ()))
NT = (((1,), (1,)), ((), ()))
TN = (((0,), (0,)), ((), ()))


def mm(a, b, dims=NN):
    return lax.dot_general(a, b, dims, preferred_element_type=f32)


def call(kernel, outs, args, scratch=(), copies=0, flops=0, vmem=12, smem=2, deps=(), into=None):
    in_specs, arrays = [], []
    args = list(args)
    count = len(args)
    into = into or {}
    deps = [*deps, *into.values()]
    aliases = {count + len(deps) - len(into) + n: i for n, i in enumerate(into)}
    args += [Far(d, pl.ANY) for d in deps]
    body = lambda *refs: kernel(*refs[:count], *refs[count + len(deps) :])
    for i, arg in enumerate(args):
        far = isinstance(arg, Far)
        space = pltpu.SMEM if i < smem else arg.space if far else pltpu.VMEM
        in_specs.append(pl.BlockSpec(memory_space=space))
        arrays.append(arg.value if far else arg)
    out_specs, out_shapes = [], []
    for o in outs:
        far = isinstance(o, Far)
        out_specs.append(pl.BlockSpec(memory_space=o.space if far else pltpu.VMEM))
        out_shapes.append(o.value if far else o)
    moved = sum(math.prod(a.shape) * a.dtype.itemsize for a in arrays + out_shapes)
    scratch = list(scratch)
    if copies:
        scratch.append(pltpu.SemaphoreType.DMA((copies,)))
    return pl.pallas_call(
        body if deps else kernel,
        out_shape=out_shapes,
        in_specs=in_specs,
        out_specs=out_specs,
        scratch_shapes=scratch,
        compiler_params=pltpu.CompilerParams(vmem_limit_bytes=vmem << 20),
        input_output_aliases=aliases,
        cost_estimate=pl.CostEstimate(flops=0, bytes_accessed=0, transcendentals=0),
    )(*arrays)


class Far:
    def __init__(self, value, space=pltpu.HBM):
        self.value, self.space = value, space


class Copies:
    def __init__(self, sems):
        self.sems, self.count, self.left = sems, 0, []

    def start(self, src, dst):
        copy = pltpu.make_async_copy(src, dst, self.sems.at[self.count])
        self.count += 1
        copy.start()
        self.left.append(copy)
        return copy

    def wait(self, *copies):
        for copy in copies:
            copy.wait()
            self.left.remove(copy)

    def finish(self):
        self.wait(*list(self.left))


def gate(value, deps):
    return pl.pallas_call(
        lambda *refs: None,
        out_shape=jax.ShapeDtypeStruct(value.shape, value.dtype),
        in_specs=[pl.BlockSpec(memory_space=pl.ANY)] * (1 + len(deps)),
        out_specs=pl.BlockSpec(memory_space=pl.ANY),
        input_output_aliases={0: 0},
        cost_estimate=pl.CostEstimate(flops=0, bytes_accessed=0, transcendentals=0),
    )(value, *deps)


def out(shape, dtype):
    return jax.ShapeDtypeStruct(shape, dtype)


def prep_kernel(rank_ref, side_ref, *refs):
    count = 18
    (x_hbm, win_hbm), refs = refs[:2], refs[2:]
    ins, outs, scratch = refs[:count], refs[count : count + 6], refs[count + 6 :]
    (core_hbm, near2_hbm, near3_hbm, *x_outs), scratch = scratch[:5], scratch[5:]
    held, (marks_ref, pack_ref, sems) = scratch[:count], scratch[count:]
    copies = Copies(sems)
    loads = [copies.start(src, dst) for src, dst in zip(ins, held)]
    for m, ref in enumerate(x_outs):
        copies.start(x_hbm.at[m, 0], ref)
    width = win_hbm.shape[1] // H
    size = win_hbm.shape[0] // 2
    for r, ref in ((1, core_hbm), (2, near2_hbm), (3, near3_hbm)):
        cols = pl.ds(pl.multiple_of((rank_ref[0] ^ r) * width, width), width)
        rows = pl.ds(pl.multiple_of((side_ref[0] % 2) * size, size), size) if r > 1 else slice(0, 2 * size)
        copies.start(win_hbm.at[rows, cols], ref)
    copies.wait(*loads)
    q_ref, k_ref, p_ref, rv_ref, ro_ref, v_ref, routes_v_ref, routes_o_ref = held[:8]
    seg_ref, pad_ref, g1_ref, b1_ref, g2_ref, b2_ref, bo_ref, cb_ref, pb_ref, bi_ref = held[8:]
    head_ref, bin_ref = outs[4:]
    head_ref[...] = jnp.zeros(head_ref.shape, f32)
    head_ref[0:1, 0:DH] = cb_ref[...].astype(f32).reshape(1, -1)
    head_ref[1:2, 0:DH] = pb_ref[...].astype(f32).reshape(1, -1)
    bin_ref[...] = bi_ref[...].astype(f32).reshape(1, -1)
    micro, own = seg_ref.shape[0], seg_ref.shape[2]
    marks_ref[...] = jnp.zeros(marks_ref.shape, f32)
    copied = [slice(0, own), slice(own, 2 * own)]
    for m in range(micro):
        for cols in copied:
            marks_ref[4 * m + 2 : 4 * m + 3, cols] = seg_ref[m].astype(f32)
            marks_ref[4 * m + 3 : 4 * m + 4, cols] = pad_ref[m].astype(f32)
    for i, ref in enumerate((g1_ref, b1_ref, g2_ref, b2_ref, bo_ref)):
        marks_ref[4 * micro + i : 4 * micro + i + 1, :] = ref[...].astype(f32).reshape(1, -1)
    row = lax.broadcasted_iota(jnp.int32, (16, H * E), 0)
    col = lax.broadcasted_iota(jnp.int32, (16, H * E), 1)
    for r in range(H):
        out_ref = outs[r] if r < 2 else pack_ref
        h = rank_ref[0] ^ r
        rows = pl.ds(pl.multiple_of(h * DH, 16), DH)
        for m in range(micro):
            for i, ref in enumerate((routes_v_ref, routes_o_ref)):
                ones = lax.shift_left(jnp.ones((2, own), jnp.int32), ref[m, h])
                code = jnp.sum(ones.astype(f32), axis=0, keepdims=True)
                for cols in copied:
                    marks_ref[4 * m + i : 4 * m + i + 1, cols] = code
        pick_v = jnp.where((row < E) & (col == h * E + row), 1.0, 0.0).astype(bf16)
        pick_o = jnp.where((row >= E) & (row < 2 * E) & (col == h * E + row - E), 1.0, 0.0)
        routers = mm(pick_v, rv_ref[...]) + mm(pick_o.astype(bf16), ro_ref[...])
        out_ref[0:DH, :] = q_ref[rows, :]
        out_ref[DH:LANE, :] = routers.astype(bf16)
        out_ref[LANE : LANE + DH, :] = k_ref[rows, :]
        out_ref[LANE + DH : 2 * LANE, :] = marks_ref[...].astype(bf16)
        out_ref[2 * LANE : 2 * LANE + DH, :] = p_ref[rows, :]
        out_ref[2 * LANE + DH : 3 * LANE, :] = jnp.zeros((LANE - DH, out_ref.shape[1]), bf16)
        for e in range(E):
            at = (3 + e) * LANE
            expert = pl.ds(pl.multiple_of((h * E + e) * DH, 16), DH)
            out_ref[at : at + DH, :] = v_ref[expert, :]
            out_ref[at + DH : at + LANE, :] = jnp.zeros((LANE - DH, out_ref.shape[1]), bf16)
        if r >= 2:
            half = pl.ds(pl.multiple_of((side_ref[0] % 2) * LANE, LANE), LANE)
            outs[r][...] = pack_ref[:, half]
    copies.finish()


def norm_stats(x):
    mean = jnp.mean(x, axis=-1, keepdims=True)
    centred = x - mean
    var = jnp.mean(centred * centred, axis=-1, keepdims=True)
    rstd = lax.rsqrt(var + 1e-05)
    return centred * rstd, rstd


def norm_back(grad, unit, rstd, gain):
    g = grad * gain
    return rstd * (
        g
        - jnp.mean(g, axis=-1, keepdims=True)
        - unit * jnp.mean(g * unit, axis=-1, keepdims=True)
    )


def x_send_keep(held, x_hbm, send_hbm, keep_hbm):
    return held[0], held[1], x_hbm, send_hbm, keep_hbm


def attention_kernel(m, rank_ref, side_ref, *refs):
    first = m == 0
    (x0, x1, x2, x3), refs = refs[:4], refs[4:]
    head_ref, refs = refs[0], refs[1:]
    if first:
        (w0, w1, near2, near3, far2, far3, sine_hbm, wo_hbm), refs = refs[:8], refs[8:]
    else:
        (wt_hbm, wo_hbm, pos_ref, vec_ref, rows_ref), refs = refs[:5], refs[5:]
    (x_ref, n_hbm, qc_hbm, qp_hbm, k_hbm, v_hbm, va_hbm, gate_hbm, p_hbm, att_hbm), refs = (
        refs[:10],
        refs[10:],
    )
    (mix_hbm, stat_ref), refs = refs[:2], refs[2:]
    (send_ref, keep_ref), refs = refs[:2], refs[2:]
    if first:
        (wt_hbm, wop_hbm, pos_ref, vec_ref, rows_ref), refs = refs[:5], refs[5:]
    n_ref, qc_ref, qp_ref, k_ref, v_ref, va_ref, gate_ref, p_ref, att_ref, mix_ref = refs[:10]
    wt_ref, wo_ref, x_out, send_out, keep_out = x_send_keep(refs[10:15], x_ref, send_ref, keep_ref)
    x_ref, send_ref, keep_ref = refs[12:15]
    sine_ref = refs[15] if first else None
    copies = Copies(refs[-1])
    length = x_ref.shape[0]
    both = slice(m * length, (m + 1) * length)
    blocks = length // BLK
    rank = rank_ref[0]
    quarter = D // H

    def at(r, size):
        return pl.ds(pl.multiple_of((rank ^ r) * size, size), size)

    loads = [copies.start(x0.at[m], x_ref.at[at(0, BLK), :])]
    loads += [copies.start(ref, x_ref.at[at(r, BLK), :]) for r, ref in enumerate((x1, x2, x3), 1)]
    if first:
        side = side_ref[0] % 2
        for r, ref in enumerate((w0, w1)):
            loads.append(copies.start(ref, wt_ref.at[:, at(r, quarter)]))
        for r, place, ref in (
            (2, side, near2),
            (3, side, near3),
            (2, 1 - side, far2),
            (3, 1 - side, far3),
        ):
            cols = pl.ds(pl.multiple_of((rank ^ r) * quarter + place * LANE, LANE), LANE)
            loads.append(copies.start(ref, wt_ref.at[:, cols]))
        sine_load = copies.start(sine_hbm, sine_ref)
        wo_loads = []
        for e in range(E):
            rows = slice(e * LANE, e * LANE + DH)
            wo_loads.append(copies.start(wo_hbm.at[e * DH : (e + 1) * DH, :], wo_ref.at[rows, :]))
            wo_ref[e * LANE + DH : (e + 1) * LANE, :] = jnp.zeros((LANE - DH, D), bf16)
        copies.wait(*loads)
        vec_ref[...] = jnp.zeros(vec_ref.shape, f32)
        rows_ref[...] = jnp.zeros(rows_ref.shape, f32)
        for r in range(H):
            micro = rows_ref.shape[0]
            marks = wt_ref[LANE + DH : 2 * LANE, at(r, quarter)].astype(f32)
            vec_ref[0:5, at(r, quarter)] = marks[4 * micro : 4 * micro + 5, :]
            fresh = pl.ds(pl.multiple_of((rank ^ r) * quarter + side * LANE, LANE), LANE)
            marks = wt_ref[LANE + DH : 2 * LANE, fresh].astype(f32)
            for i in range(micro):
                part = marks[4 * i : 4 * i + 4, :]
                rows_ref[i, 0:1, at(r, BLK)] = part[0:1, :] + 2.0**E * part[1:2, :]
                rows_ref[i, 1:3, at(r, BLK)] = part[2:4, :]
        copies.start(wt_ref, wt_hbm)
    else:
        wt_load = copies.start(wt_hbm, wt_ref)
        wo_loads = [copies.start(wo_hbm, wo_ref)]
        copies.wait(*loads)

    @pl.loop(0, blocks)
    def _(b):
        rows = pl.ds(pl.multiple_of(b * BLK, BLK), BLK)
        x = x_ref[rows, :].astype(f32)
        unit, rstd = norm_stats(x)
        n_ref[rows, :] = (unit * vec_ref[0:1, :] + vec_ref[1:2, :]).astype(bf16)
        first_lane = lax.broadcasted_iota(jnp.int32, (BLK, LANE), 1) == 0
        stat_ref[rows, :] = jnp.where(first_lane, jnp.mean(x, axis=-1, keepdims=True), rstd)

    copies.start(x_ref, x_out)
    copies.start(n_ref, n_hbm.at[both, :])
    if first:
        copies.wait(sine_load)
        pos_ref[...] = mm(sine_ref[...], wt_ref[2 * LANE : 3 * LANE, :], NT).astype(bf16)
    else:
        copies.wait(wt_load)
    lane = lax.broadcasted_iota(jnp.int32, (1, LANE), 1)
    is_head = lane < DH
    raw_keys = mm(n_ref[...], wt_ref[0 : 2 * LANE, :], NT)
    raw = raw_keys[:, 0:LANE]
    columns = rows_ref[m].T
    code = jnp.broadcast_to(columns[:, 0:1].astype(jnp.int32), (length, LANE))
    slot = jnp.where((lane >= DH) & (lane < DH + 2 * E), lane - DH, 31)
    pick = (lax.shift_right_logical(code, jnp.broadcast_to(slot, (length, LANE))) & 1) == 1
    gate = jnp.where(pick, 1.0 / (1.0 + jnp.exp(-raw)), 0.0)
    gate_ref[...] = gate
    copies.start(gate_ref, gate_hbm)
    qc_ref[...] = jnp.where(is_head, (raw + head_ref[0:1, :]) * SCALE, 0.0).astype(bf16)
    qp_ref[...] = jnp.where(is_head, (raw + head_ref[1:2, :]) * SCALE, 0.0).astype(bf16)
    k_ref[...] = jnp.where(is_head, raw_keys[:, LANE : 2 * LANE], 0.0).astype(bf16)
    values = jnp.zeros((length, LANE), f32)
    for e in range(0, E, 2):
        last = min(e + 2, E)
        parts = mm(n_ref[...], wt_ref[(3 + e) * LANE : (3 + last) * LANE, :], NT)
        va_ref[:, e * LANE : last * LANE] = parts.astype(bf16)
        for i in range(e, last):
            part = parts[:, (i - e) * LANE : (i - e + 1) * LANE]
            values += part * gate[:, DH + i : DH + i + 1]
    v_ref[...] = values.astype(bf16)
    for src, dst in ((qc_ref, qc_hbm), (qp_ref, qp_hbm), (k_ref, k_hbm), (v_ref, v_hbm), (va_ref, va_hbm)):
        copies.start(src, dst)
    seg_col = columns[:, 1:2]
    for b in range(blocks):
        rows = slice(b * BLK, (b + 1) * BLK)
        wide = (b + 1) * BLK
        content = mm(qc_ref[rows, :], k_ref[0:wide, :], NT)
        table = mm(qp_ref[rows, :], pos_ref[length - wide : length, :], NT)
        table = pltpu.roll(table, (wide - BLK + 1) % wide, 1, stride=1, stride_axis=0)
        row = lax.broadcasted_iota(jnp.int32, (BLK, wide), 0) + b * BLK
        col = lax.broadcasted_iota(jnp.int32, (BLK, wide), 1)
        same = seg_col[rows, :] == rows_ref[m, 1:2, 0:wide]
        live = ((rows_ref[m, 2:3, 0:wide] > 0.0) & (col < row)) | (col == row)
        scores = jnp.where(same & live, content + table, MASKED)
        top = jnp.max(scores, axis=-1, keepdims=True)
        expo = jnp.exp(scores - top)
        prob = (expo / jnp.sum(expo, axis=-1, keepdims=True)).astype(bf16)
        p_ref[rows, 0:wide] = prob
        att = mm(prob, v_ref[0:wide, :])
        att_ref[rows, :] = att
        for e in range(E):
            share = gate_ref[rows, DH + E + e : DH + E + e + 1]
            mix_ref[rows, e * LANE : (e + 1) * LANE] = (att * share).astype(bf16)
        copies.start(p_ref.at[rows, 0:wide], p_hbm.at[rows, 0:wide])
    copies.start(att_ref, att_hbm)
    copies.start(mix_ref, mix_hbm.at[both, :])
    half = length // 2
    core = rank & 1
    copies.wait(*wo_loads)
    if first:
        copies.start(wo_ref, wop_hbm)
    for place, ref, dst in ((1 - core, send_ref, send_out), (core, keep_ref, keep_out)):
        rows = pl.ds(pl.multiple_of(place * half, half), half)
        ref[...] = mm(mix_ref[rows, :], wo_ref[...]).astype(bf16)
        copies.start(ref, dst)
    copies.finish()


def normal_terms(v):
    bell = jnp.exp(-0.5 * v * v)
    phi = 0.5 * (1.0 + lax.erf(v * (1.0 / math.sqrt(2.0))))
    return phi, bell * (1.0 / math.sqrt(2.0 * math.pi))


def pair_rows(core, b, refs):
    mine, far, mine2, far2 = refs
    own_half = (b // 2) == core
    rows = pl.ds(pl.multiple_of((b % 2) * BLK, BLK), BLK)
    near = mine[rows, :].astype(f32) + far[rows, :].astype(f32)
    away = mine2[rows, :].astype(f32) + far2[rows, :].astype(f32)
    return jnp.where(own_half, near, away)


def ffn_kernel(
    m,
    rank_ref,
    side_ref,
    x_hbm,
    a0,
    a1,
    a2,
    a3,
    vec_ref,
    bin_ref,
    win_hbm,
    win_core,
    *refs,
):
    (near2, near3, far2, far3), refs = refs[:4], refs[4:]
    (wout_hbm, c0, c1, c2, c3), refs = refs[:5], refs[5:]
    (n_hbm, hid_hbm, gp_hbm, cot_hbm, unit_hbm, rstd_ref, resid_ref, sum_ref), refs = (
        refs[:8],
        refs[8:],
    )
    (send_hbm, keep_hbm), refs = refs[:2], refs[2:]
    (unit_ref, win_ref, wout_ref, x_ref, n_ref, hid_ref, gp_ref, cot_ref), refs = refs[:8], refs[8:]
    halves, (send_ref, keep_ref, sems) = refs[:4], refs[4:]
    length = x_ref.shape[0]
    both = slice(m * length, (m + 1) * length)
    rank, place = rank_ref[0], side_ref[0]
    core = rank & 1
    copies = Copies(sems)
    size = D // H
    sum_ref[...] = jnp.zeros(sum_ref.shape, f32)

    def at(r, size):
        return pl.ds(pl.multiple_of((rank ^ r) * size, size), size)

    early = [copies.start(x_hbm, x_ref)]
    early += [copies.start(src, dst) for src, dst in zip((a0, a1, a2, a3), halves)]
    loads = []
    width = win_ref.shape[1]
    own_cols = pl.ds(pl.multiple_of(rank * width, width), width)
    loads.append(copies.start(win_hbm.at[:, own_cols], win_ref.at[at(0, size), :]))
    loads.append(copies.start(win_core, win_ref.at[at(1, size), :]))
    side = place % 2
    for r, half, ref in ((2, side, near2), (3, side, near3), (2, 1 - side, far2), (3, 1 - side, far3)):
        rows = pl.ds(pl.multiple_of((rank ^ r) * size + half * (size // 2), size // 2), size // 2)
        loads.append(copies.start(ref, win_ref.at[rows, :]))
    loads.append(copies.start(wout_hbm, wout_ref))
    for r, ref in enumerate((c0, c1, c2, c3)):
        loads.append(copies.start(ref.at[m], cot_ref.at[at(r, BLK), :]))

    copies.wait(*early)

    @pl.loop(0, length // BLK)
    def _(b):
        rows = pl.ds(pl.multiple_of(b * BLK, BLK), BLK)
        resid = x_ref[rows, :].astype(f32) + pair_rows(core, b, halves)
        unit, rstd = norm_stats(resid)
        unit_ref[rows, :] = unit.astype(bf16)
        rstd_ref[rows, :] = jnp.broadcast_to(rstd, (BLK, LANE))
        n_ref[rows, :] = (unit * vec_ref[2:3, :] + vec_ref[3:4, :]).astype(bf16)

        @pl.when(b == rank)
        def _():
            resid_ref[...] = resid

    copies.wait(*loads)
    for src, dst in (
        (unit_ref, unit_hbm),
        (n_ref, n_hbm.at[both, :]),
        (cot_ref, cot_hbm.at[both, :]),
    ):
        copies.start(src, dst)
    chunk = 1024

    @pl.loop(0, width // chunk)
    def _(c):
        cols = pl.ds(pl.multiple_of(c * chunk, chunk), chunk)
        pre = mm(n_ref[...], win_ref[:, cols]) + bin_ref[0:1, cols]
        back = mm(cot_ref[...], wout_ref[cols, :], NT)
        phi, density = normal_terms(pre)
        hid_ref[:, cols] = (pre * phi).astype(bf16)
        grad = (back * (phi + pre * density)).astype(bf16)
        gp_ref[:, cols] = grad
        sum_ref[0:1, cols] = jnp.sum(grad.astype(f32), axis=0, keepdims=True)

    copies.start(hid_ref, hid_hbm.at[both, :])
    copies.start(gp_ref, gp_hbm.at[both, :])
    half = length // 2
    for place, ref, dst in ((1 - core, send_ref, send_hbm), (core, keep_ref, keep_hbm)):
        rows = pl.ds(pl.multiple_of(place * half, half), half)
        ref[...] = mm(gp_ref[rows, :], win_ref[...], NT).astype(bf16)
        copies.start(ref, dst)
    copies.finish()


def split_blocks(rank, value_ref, keep_ref, send_ref):
    for r in range(H):
        rows = pl.ds(pl.multiple_of((rank ^ r) * BLK, BLK), BLK)
        (send_ref if r % 2 else keep_ref)[r // 2] = value_ref[rows, :]


def project_kernel(rank_ref, side_ref, hid_hbm, wout_hbm, keep_hbm, send_hbm, *refs):
    hid_ref, wout_ref, full_ref, keep_ref, send_ref, sems = refs
    copies = Copies(sems)
    loads = [copies.start(wout_hbm, wout_ref), copies.start(hid_hbm, hid_ref)]
    copies.wait(*loads)
    full_ref[...] = mm(hid_ref[...], wout_ref[...]).astype(bf16)
    micro = keep_ref.shape[1]
    length = full_ref.shape[0] // micro
    for m in range(micro):
        for r in range(H):
            at = pl.multiple_of((rank_ref[0] ^ r) * BLK + m * length, BLK)
            ref = send_ref if r % 2 else keep_ref
            ref[r // 2, m] = full_ref[pl.ds(at, BLK), :]
    copies.start(keep_ref, keep_hbm)
    copies.start(send_ref, send_hbm)
    copies.finish()


def branch_kernel(m, rank_ref, side_ref, vec_ref, rstd_ref, gate_ref, att_ref, *refs):
    hbm, refs = refs[:7], refs[7:]
    (gb_hbm, sums_ref, grad_ref, ga_ref, logit_ref), refs = refs[:5], refs[5:]
    held, (gb_ref, sems) = refs[:7], refs[7:]
    copies = Copies(sems)
    *halves, cot_ref, unit_ref, wo_ref = held
    length = unit_ref.shape[0]
    both = slice(m * length, (m + 1) * length)
    hbm = [*hbm[:4], hbm[4].at[both, :], *hbm[5:]]
    *loads, wo_load = [copies.start(src, dst) for src, dst in zip(hbm, held)]
    rank = rank_ref[0]
    core = rank & 1
    sums_ref[...] = jnp.zeros(sums_ref.shape, f32)
    copies.wait(*loads)

    @pl.loop(0, length // BLK)
    def _(b):
        rows = pl.ds(pl.multiple_of(b * BLK, BLK), BLK)
        unit = unit_ref[rows, :].astype(f32)
        grad = pair_rows(core, b, halves)
        sums_ref[0:1, :] += jnp.sum(grad * unit, axis=0, keepdims=True)
        sums_ref[1:2, :] += jnp.sum(grad, axis=0, keepdims=True)
        cot = cot_ref[rows, :].astype(f32)
        sums_ref[2:3, :] += jnp.sum(cot, axis=0, keepdims=True)
        total = cot + norm_back(grad, unit, rstd_ref[rows, 0:1], vec_ref[2:3, :])
        gb_ref[rows, :] = total.astype(bf16)

        @pl.when(b == rank)
        def _():
            grad_ref[...] = total

    copies.start(gb_ref, gb_hbm.at[both, :])
    copies.wait(wo_load)
    lane = lax.broadcasted_iota(jnp.int32, (1, LANE), 1)
    acc = jnp.zeros((length, LANE), f32)
    logits = jnp.zeros((length, LANE), f32)
    for first in range(0, E, 2):
        last = min(first + 2, E)
        both_mixed = mm(gb_ref[...], wo_ref[first * LANE : last * LANE, :], NT)
        for e in range(first, last):
            mixed = both_mixed[:, (e - first) * LANE : (e - first + 1) * LANE]
            acc += mixed * gate_ref[:, DH + E + e : DH + E + e + 1]
            dot = jnp.sum(mixed * att_ref[...], axis=-1, keepdims=True)
            logits = jnp.where(lane == DH + E + e, dot, logits)
    ga_ref[...] = acc.astype(bf16)
    logit_ref[...] = logits
    copies.finish()


def back_kernel(m, rank_ref, side_ref, ga_ref, logit_ref, pos_ref, gate_ref, stat_ref, *refs):
    hbm, refs = refs[:8], refs[8:]
    (sums_ref, dproj_hbm, gpos_ref, bias_ref, keep_hbm, send_hbm), refs = refs[:6], refs[6:]
    held, refs = refs[:8], refs[8:]
    dproj_ref, gk_ref, gv_ref, full_ref, keep_ref, send_ref, sems = refs
    copies = Copies(sems)
    *loads, va_load, wt_load, x_load = [copies.start(src, dst) for src, dst in zip(hbm, held)]
    p_ref, v_ref, k_ref, qc_ref, qp_ref, va_ref, wt_ref, x_ref = held
    length = x_ref.shape[0]
    blocks = length // BLK
    rank = rank_ref[0]
    lane = lax.broadcasted_iota(jnp.int32, (1, LANE), 1)
    sums_ref[...] = jnp.zeros(sums_ref.shape, f32)
    gk_ref[...] = jnp.zeros(gk_ref.shape, f32)
    gv_ref[...] = jnp.zeros(gv_ref.shape, f32)
    gpos_ref[...] = jnp.zeros(gpos_ref.shape, f32)
    row = lax.broadcasted_iota(jnp.int32, (BLK, BLK), 0)
    col = lax.broadcasted_iota(jnp.int32, (BLK, BLK), 1)
    mirror = jnp.where(row + col == BLK - 1, 1.0, 0.0).astype(bf16)
    cont_sum = jnp.zeros((1, LANE), f32)
    posn_sum = jnp.zeros((1, LANE), f32)
    copies.wait(*loads)
    for b in range(blocks):
        rows = slice(b * BLK, (b + 1) * BLK)
        wide = (b + 1) * BLK
        prob = p_ref[rows, 0:wide].astype(f32)
        ga = ga_ref[rows, :]
        grad_prob = mm(ga, v_ref[0:wide, :], NT)
        delta = jnp.sum(prob * grad_prob, axis=-1, keepdims=True)
        grad_score = (prob * (grad_prob - delta)).astype(bf16)
        gv_ref[0:wide, :] += mm(p_ref[rows, 0:wide], ga, TN)
        gk_ref[0:wide, :] += mm(grad_score, qc_ref[rows, :], TN)
        cont = mm(grad_score, k_ref[0:wide, :]) * SCALE
        table = pltpu.roll(mm(mirror, grad_score), 0, 1, stride=1, stride_axis=0)
        table = mm(mirror, table.astype(bf16)).astype(bf16)
        posn = mm(table, pos_ref[length - wide : length, :]) * SCALE
        gpos_ref[length - wide : length, :] += mm(table, qp_ref[rows, :], TN)
        cont_sum += jnp.sum(cont, axis=0, keepdims=True)
        posn_sum += jnp.sum(posn, axis=0, keepdims=True)
        dproj_ref[rows, 0:LANE] = (cont + posn).astype(bf16)
    bias_ref[...] = jnp.zeros(bias_ref.shape, f32)
    bias_ref[0:1, :] = cont_sum
    bias_ref[1:2, :] = posn_sum
    dproj_ref[:, LANE : 2 * LANE] = gk_ref[...].astype(bf16)
    dproj_ref[:, 2 * LANE : 3 * LANE] = jnp.zeros((length, LANE), bf16)
    copies.wait(va_load, wt_load, x_load)
    grad_values = gv_ref[...].astype(bf16).astype(f32)
    logits = logit_ref[...]
    for e in range(E):
        cols = slice((3 + e) * LANE, (4 + e) * LANE)
        dproj_ref[:, cols] = (grad_values * gate_ref[:, DH + e : DH + e + 1]).astype(bf16)
        dot = jnp.sum(grad_values * va_ref[:, e * LANE : (e + 1) * LANE].astype(f32), axis=-1, keepdims=True)
        logits = jnp.where(lane == DH + e, dot, logits)
    gate = gate_ref[...]
    logits = logits * gate * (1.0 - gate)
    dproj_ref[:, 0:LANE] = jnp.where(
        lane < DH, dproj_ref[:, 0:LANE].astype(f32), logits
    ).astype(bf16)
    copies.start(dproj_ref, dproj_hbm.at[m * length : (m + 1) * length, :])
    chunk = 1024
    mean, rstd = stat_ref[:, 0:1], stat_ref[:, 1:2]

    @pl.loop(0, D // chunk)
    def _(c):
        cols = pl.ds(pl.multiple_of(c * chunk, chunk), chunk)
        part = mm(dproj_ref[...], wt_ref[:, cols])
        full_ref[:, cols] = part.astype(bf16)
        unit = (x_ref[:, cols].astype(f32) - mean) * rstd
        sums_ref[3:4, cols] = jnp.sum(part * unit, axis=0, keepdims=True)
        sums_ref[4:5, cols] = jnp.sum(part, axis=0, keepdims=True)

    split_blocks(rank, full_ref, keep_ref, send_ref)
    copies.start(send_ref, send_hbm)
    copies.start(keep_ref, keep_hbm)
    copies.finish()


def output_kernel(rank_ref, side_ref, vec_ref, keep_ref, got_ref, far_ref, *refs):
    *refs, y_hbm, done_ref, y_ref, sems = refs
    done_ref[...] = jnp.zeros(done_ref.shape, f32)
    for m in range(y_ref.shape[0]):
        total = refs[m][...] + keep_ref[0, m].astype(f32) + got_ref[0, m].astype(f32)
        y_ref[m, 0] = (total + far_ref[m].astype(f32) + vec_ref[4:5, :]).astype(bf16)
    copies = Copies(sems)
    copies.start(y_ref, y_hbm)
    copies.finish()


def input_kernel(rank_ref, side_ref, x_ref, vec_ref, far_ref, *refs):
    y_ref = refs[-1]
    for m in range(y_ref.shape[0]):
        grad_ref, keep_ref, got_ref = refs[3 * m : 3 * m + 3]
        unit, rstd = norm_stats(x_ref[m].astype(f32))
        back = keep_ref[0].astype(f32) + got_ref[0].astype(f32) + far_ref[m].astype(f32)
        y_ref[m, 0] = grad_ref[...] + norm_back(back, unit, rstd, vec_ref[0:1, :])


def vectors_kernel(
    rank_ref, side_ref, sums0, sums1, norm0, norm1, bias0, bias1, hid0, hid1, y_ref
):
    y_ref[...] = jnp.zeros(y_ref.shape, f32)
    width = D // H
    own = pl.ds(pl.multiple_of(rank_ref[0] * width, width), width)
    y_ref[0, 6:7, :] = norm0[3:4, :] + norm1[3:4, :]
    y_ref[1, 6:7, :] = norm0[4:5, :] + norm1[4:5, :]
    for i in range(3):
        y_ref[i, 7:8, own] = sums0[i : i + 1, own] + sums1[i : i + 1, own]
    for i in range(2):
        cols = pl.ds(pl.multiple_of(rank_ref[0] * width + i * LANE, LANE), LANE)
        y_ref[3, 7:8, cols] = bias0[i : i + 1, :] + bias1[i : i + 1, :]
    for i in range(4):
        cols = slice(i * width, (i + 1) * width)
        y_ref[4 + i, 7:8, own] = hid0[0:1, cols] + hid1[0:1, cols]


def load_ffn_chunk(copies, c, sources, dst):
    grad_o, grad_i = sources
    rows = D // RING
    part = rows // H
    copies.start(grad_o.at[pl.ds(pl.multiple_of(c * rows, rows), rows), :], dst.at[0:rows, :])
    for s in range(H):
        src = pl.ds(pl.multiple_of(s * (D // H) + c * part, part), part)
        copies.start(grad_i.at[src, :], dst.at[rows + s * part : rows + (s + 1) * part, :])


def load_pack_chunk(copies, c, sources, dst):
    grad_p, grad_w = sources
    rows = D // RING
    part = E * LANE // RING
    copies.start(grad_p.at[pl.ds(pl.multiple_of(c * rows, rows), rows), :], dst.at[0:rows, :])
    copies.start(
        grad_w.at[pl.ds(pl.multiple_of(c * part, part), part), :], dst.at[rows : rows + part, :]
    )


def ring_kernel(load, split, t, rank_ref, pos_ref, src0, src1, *refs):
    tail_ref, refs = (refs[0], refs[1:]) if load is load_pack_chunk else (None, refs)
    got_hbm, refs = (refs[:2], refs[2:]) if t else ((), refs)
    outs_hbm, refs = (refs[:2], refs[2:]) if t < 4 else (refs[: 1 + H], refs[1 + H :])
    loaded, held, *more, sems = refs
    got, outs = more[: len(got_hbm)], more[len(got_hbm) :]
    copies = Copies(sems)
    for src, dst in zip(got_hbm, got):
        copies.start(src, dst)
    pos = pos_ref[0]
    total = held.shape[1]
    chunks = [(pos + 4 - t) % RING, (pos + 4 + t) % RING][: 2 if t < 4 else 1]
    for i, c in enumerate(chunks[: 2 if t < 4 else 1]):
        load(copies, c, (src0, src1), loaded.at[i])
    copies.finish()
    held[...] = loaded[...].astype(f32)
    if tail_ref is not None:
        for i, c in enumerate(chunks):
            rows = slice(D // RING - TAIL, D // RING)
            held[i, rows, :] = held[i, rows, :] + tail_ref[c]
    if t == 4:
        held[0] = held[0] + got[0][...].astype(f32) + got[1][...].astype(f32)
        rows = D // RING
        rank = rank_ref[0]
        for r, ref in enumerate(outs[1:]):
            if tail_ref is None:
                size = rows // H
                at = pl.multiple_of(rows + (rank ^ r) * size, size)
                ref[...] = held[0, pl.ds(at, size), :].astype(bf16)
            else:
                size = D // H
                at = pl.multiple_of((rank ^ r) * size, size)
                ref[...] = held[0, 0:rows, pl.ds(at, size)].astype(bf16)
        outs[0][...] = (held[0, 0:rows, :] if tail_ref is None else held[0, rows:total, :]).astype(bf16)
        for ref, dst in zip(outs, outs_hbm):
            copies.start(ref, dst)
        copies.finish()
        return
    for i, ref in enumerate(outs):
        part = slice(0, split) if i == 0 else slice(split, total)
        if t == 0:
            ref[...] = held[i, part, :].astype(bf16)
        elif t == 1:
            ref[...] = held[i].astype(bf16)
            ref[part, :] = (held[i, part, :] + got[i][...].astype(f32)).astype(bf16)
        else:
            ref[...] = (held[i] + got[i][...].astype(f32)).astype(bf16)
        copies.start(ref, outs_hbm[i])
    copies.finish()


def load_ring(copies, pos, split, refs, dst):
    own, fwd, bwd, half_fwd, half_bwd = refs[0], refs[1:4], refs[4:7], refs[7], refs[8]
    copies.start(own, dst.at[pos])
    for i in range(3):
        copies.start(fwd[i], dst.at[(pos + RING - 1 - i) % RING])
        copies.start(bwd[i], dst.at[(pos + 1 + i) % RING])
    last = (pos + 4) % RING
    copies.start(half_fwd, dst.at[last, 0:split, :])
    copies.start(half_bwd, dst.at[last, split : dst.shape[1], :])
    copies.finish()


def ffn_grads_kernel(split, rank_ref, pos_ref, *refs):
    parts, (o_hbm, i_hbm, done_ref, held, o_ref, i_ref, sems) = refs[:9], refs[9:]
    done_ref[...] = jnp.zeros(done_ref.shape, f32)
    copies = Copies(sems)
    load_ring(copies, pos_ref[0], split, parts, held)
    rows = D // RING
    part = rows // H
    for c in range(RING):
        o_rows = slice(c * rows, (c + 1) * rows)
        o_ref[o_rows, :] = held[c, 0:rows, :].astype(f32)
        copies.start(o_ref.at[o_rows, :], o_hbm.at[o_rows, :])
        i_rows = slice(c * part, (c + 1) * part)
        for r in range(H):
            cols = pl.ds(pl.multiple_of((rank_ref[0] ^ r) * D, D), D)
            at = rows + r * part
            i_ref[i_rows, cols] = held[c, at : at + part, :].astype(f32)
        copies.start(i_ref.at[i_rows, :], i_hbm.at[i_rows, :])
    copies.finish()


def pack_grads_kernel(split, rank_ref, pos_ref, *refs):
    parts, refs = refs[:9], refs[9:]
    (q_ref, rv_ref, ro_ref, k_ref, p_ref, v_ref, w_ref), refs = refs[:7], refs[7:]
    (g1, b1, g2, b2, bo, content, posn, bin_ref), refs = refs[:8], refs[8:]
    held, heads, sems = refs
    copies = Copies(sems)
    load_ring(copies, pos_ref[0], split, parts, held)
    width = D // H
    rank = rank_ref[0]
    for r in range(H):
        heads[rank ^ r] = held[:, 0:LANE, r * width : (r + 1) * width].astype(f32)
    for h in range(H):
        rows = slice(h * DH, (h + 1) * DH)
        q_ref[rows, :] = heads[h, 0, 0:DH, :]
        rv_ref[h * E : (h + 1) * E, :] = heads[h, 0, DH : DH + E, :]
        ro_ref[h * E : (h + 1) * E, :] = heads[h, 0, DH + E : DH + 2 * E, :]
        k_ref[rows, :] = heads[h, 1, 0:DH, :]
        p_ref[rows, :] = heads[h, 2, 0:DH, :]
        for e in range(E):
            at = (h * E + e) * DH
            v_ref[at : at + DH, :] = heads[h, 3 + e, 0:DH, :]
    part = E * LANE // RING
    for c in range(RING):
        for e in range(E):
            low, high = max(c * part, e * LANE), min((c + 1) * part, e * LANE + DH)
            if low < high:
                at = low - e * LANE + e * DH
                w_ref[at : at + high - low, :] = held[
                    c, LANE + low - c * part : LANE + high - c * part, :
                ].astype(f32)
    last = slice(LANE - 1, LANE)
    before = slice(LANE - 2, LANE - 1)
    for ref, c in ((g1, 0), (b1, 1)):
        ref[...] = sum(heads[h, c, before, :] for h in range(H)).reshape(ref.shape)
    for c, ref in enumerate((g2, b2, bo)):
        ref[...] = heads[rank, c, last, :].reshape(ref.shape)
    row = heads[rank, 3, last, :]
    content[...] = row[:, 0:DH].reshape(content.shape)
    posn[...] = row[:, LANE : LANE + DH].reshape(posn.shape)
    for i in range(4):
        bin_ref[i * width : (i + 1) * width] = heads[rank, 4 + i, last, :].reshape((width,))


def flip_shard(value, bit):
    return lax.ppermute(value, "shard", [(s, s ^ bit) for s in range(H)])


def flip_dp(value, bit):
    count = lax.axis_size("dp")
    return lax.ppermute(value, "dp", [(d, d ^ bit) for d in range(count)])


def take(value, at, size, axis=0):
    return lax.dynamic_slice_in_dim(value, at, size, axis)


def put(value, part, at, axis=0):
    return lax.dynamic_update_slice_in_dim(value, part, at, axis)


def spread(own):
    across = flip_shard(own, 2)
    return own, flip_shard(own, 1), across, flip_shard(across, 1)


def ring_order():
    return list(range(0, RING, 2)) + list(range(RING - 1, 0, -2))


def pass_on(value, way):
    order, count = ring_order(), lax.axis_size("dp")
    pairs = [
        (base + order[i], base + order[(i + way) % RING])
        for base in range(0, count, RING)
        for i in range(RING)
    ]
    return lax.ppermute(value, "dp", pairs)


def swap_shard(value, rank, size, axis):
    parts = [take(value, (rank ^ r) * size, size, axis) for r in range(H)]
    return [flip_shard(p, r) if r else p for r, p in enumerate(parts)]


def sinusoid(length, feature_count):
    distance = (length - 1 - jnp.arange(length, dtype=jnp.int32)).astype(f32)
    inv_freq = jnp.exp(
        jnp.arange(0, feature_count, 2, dtype=jnp.int32).astype(f32)
        * (-math.log(10000.0) / feature_count)
    )
    angles = distance[:, None] * inv_freq[None, :]
    return jnp.concatenate([jnp.sin(angles), jnp.cos(angles)], axis=1)


def local(
    inputs,
    segments,
    padding,
    routes_value,
    routes_output,
    norm1_gain,
    norm1_bias,
    query_weight,
    key_weight,
    pos_weight,
    content_bias,
    pos_bias,
    value_router,
    output_router,
    value_experts,
    output_experts,
    norm2_gain,
    norm2_bias,
    ffn_in,
    ffn_in_bias,
    ffn_out,
    ffn_out_bias,
    cotangent,
):
    micro = inputs.shape[0]
    own = inputs.shape[2]
    length = own * H
    dp_count = lax.axis_size("dp")
    rank = lax.axis_index("shard")
    me = rank.astype(jnp.int32).reshape(1)
    dp_rank = lax.axis_index("dp")
    side = (dp_rank % RING).astype(jnp.int32).reshape(1)
    place = dp_rank % RING
    place = jnp.where(place % 2 == 0, place // 2, RING - 1 - place // 2)
    place = place.astype(jnp.int32).reshape(1)
    quarter = D // H

    token = [me]

    def after(value, *deps):
        return lax.optimization_barrier((value, *deps))[0]

    def step(fn, first, *rest):
        res = fn(after(first, token[0]), *rest)
        token[0] = jax.tree.leaves(res)[0]
        return res

    def kernel(fn, outs, args, second=side, **kwargs):
        deps = [*kwargs.pop("deps", ()), *([] if token[0] is me else [token[0]])]
        res = call(fn, outs, [me, second, *args], deps=deps, **kwargs)
        token[0] = min(res, key=lambda r: r.size)
        return res

    packs = kernel(
        prep_kernel,
        [out((PACK, quarter), bf16)] * 2
        + [out((PACK, LANE), bf16)] * 2
        + [out((8, LANE), f32), out((1, FF // H), f32)]
        + [out((quarter, FF // H), bf16)]
        + [out((quarter // 2, FF // H), bf16)] * 2
        + [out((own, D), bf16)] * micro,
        [
            Far(a)
            for a in (
                inputs,
                ffn_in,
                query_weight.T,
                key_weight.T,
                pos_weight.T,
                value_router.T,
                output_router.T,
                value_experts.T,
                routes_value[:, 0].transpose(0, 2, 3, 1),
                routes_output[:, 0].transpose(0, 2, 3, 1),
                segments,
                padding,
                norm1_gain,
                norm1_bias,
                norm2_gain,
                norm2_bias,
                ffn_out_bias,
                content_bias,
                pos_bias,
                ffn_in_bias,
            )
        ],
        scratch=[
            pltpu.VMEM(shape, dtype)
            for shape, dtype in [((H * DH, quarter), bf16)] * 3
            + [((H * E, quarter), bf16)] * 2
            + [((H * E * DH, quarter), bf16)]
            + [((micro, H, 2, own), jnp.int32)] * 2
            + [((micro, 1, own), jnp.int32)] * 2
            + [((quarter,), bf16)] * 5
            + [((DH,), bf16)] * 2
            + [((FF // H,), bf16)]
            + [((LANE - DH, quarter), f32), ((PACK, quarter), bf16)]
        ],
        copies=18 + 3 + micro,
        vmem=56,
    )
    sine = sinusoid(length, D).astype(bf16)
    head, b_in, core_in, *sent = packs[H:]
    sent_in, sent_x = sent[:2], sent[2:]
    near = [flip_shard(packs[r], r) for r in (2, 3)]
    w_core = flip_shard(packs[1], 1)
    far = [flip_dp(w, 1) for w in near]
    weights = [packs[0], w_core, *near, *far]
    x_own = inputs[:, 0]
    sent_x[0] = gate(sent_x[0], [*near, sine])
    x_parts = [spread(x) for x in sent_x]
    near_in = [flip_shard(w, r) for w, r in zip(sent_in, (2, 3))]
    w_in_core = flip_shard(core_in, 1)
    cot_parts = spread(cotangent[:, 0])

    def add_chip(keep, send):
        got = flip_shard(send, 1)
        add = lambda k, g: (k.astype(f32) + g.astype(f32)).astype(bf16)
        return step(add, keep, got)

    def finish_halves(chip):
        across = flip_shard(chip, 2)
        return chip, across, flip_shard(chip, 1), flip_shard(across, 1)

    half = out((length // 2, D), bf16)
    wide = out((length, D), bf16)
    saved_shapes = (
        [wide]
        + [out((length, LANE), bf16)] * 4
        + [
            out((length, E * LANE), bf16),
            out((length, LANE), f32),
            out((length, length), bf16),
            out((length, LANE), f32),
            out((length, E * LANE), bf16),
        ]
    )
    vmem_of = lambda shapes: [pltpu.VMEM(o.shape, o.dtype) for o in shapes]
    weight_shapes = [out((PACK, D), bf16), out((E * LANE, D), bf16)]
    joined = out((micro * length, D), bf16)
    saved = []
    residuals = []
    for m in range(micro):
        if m == 0:
            more = [Far(w) for w in weights] + [Far(sine), Far(output_experts)]
            extra = [Far(o) for o in weight_shapes]
            extra += [out((length, LANE), bf16), out((8, D), f32), out((micro, 8, length), f32)]
        else:
            more = [Far(wt), Far(w_out_heads), pos, vec, rows]
            extra = []
        res = kernel(
            functools.partial(attention_kernel, m),
            [Far(wide)]
            + [Far(joined)]
            + [Far(o) for o in saved_shapes[1:-1]]
            + [Far(out((micro * length, E * LANE), bf16))]
            + [out((length, LANE), f32), Far(half), Far(half)]
            + extra,
            [Far(x) for x in (x_own, *x_parts[m][1:])] + [head] + more,
            scratch=vmem_of(
                saved_shapes + weight_shapes + [wide, half, half] + ([wide] if m == 0 else [])
            ),
            copies=40,
            into={1: saved[0][1], 10: saved[0][10]} if m else None,
            deps=[*near_in, residuals[0][0]] if m else [],
            vmem=60,
            flops=2 * length * D * 1700,
        )
        saved.append(res[:12])
        if m == 0:
            near_in = [gate(w, [res[12]]) for w in near_in]
            far_in = [flip_dp(w, 1) for w in near_in]
        send, keep = res[12:14]
        if m == 0:
            wt, w_out_heads, pos, vec, rows = res[14:]
            send = gate(send, [*near_in, *x_parts[1][1:3]][: 4])
        else:
            send = gate(send, [*far_in, cot_parts[2], residuals[0][1]])
        residuals.append(finish_halves(add_chip(keep, send)))
    ffn = []
    gn2 = []
    for m in range(micro):
        res = kernel(
            functools.partial(ffn_kernel, m),
            [Far(joined)] * 4
            + [Far(wide)]
            + [
                out((length, LANE), f32),
                out((own, D), f32),
                out((8, FF // H), f32),
                Far(half),
                Far(half),
            ],
            [Far(a) for a in (saved[m][0], *residuals[m])]
            + [vec, b_in]
            + [Far(w) for w in (ffn_in, w_in_core, *near_in, *far_in, ffn_out, *cot_parts)],
            scratch=vmem_of(
                [wide, out((D, FF // H), bf16), out((FF // H, D), bf16)] + [wide] * 5 + [half] * 6
            ),
            copies=30,
            into={i: ffn[0][i] for i in range(4)} if m else None,
            vmem=60,
            deps=[residuals[1][0] if m == 0 else gn2[0][0]],
            flops=2 * length * D * D * 3,
        )
        ffn.append(res)
        gn2.append(finish_halves(add_chip(res[-1], res[-2])))

    def tn(a, b):
        return mm(a, b, TN).astype(bf16)

    class Ring:
        def __init__(self, load, split, total, sources):
            self.load, self.split, self.total = load, split, total
            self.sources, self.got, self.t = sources, (), 0

        def step(self, deps=()):
            rows = D // RING
            if self.t == 0:
                shapes = [(self.split, D), (self.total - self.split, D)]
            elif self.t < 4:
                shapes = [(self.total, D)] * 2
            elif len(self.sources) == 2:
                shapes = [(rows, D)] + [(rows // H, D)] * H
            else:
                shapes = [(self.total - rows, D)] + [(rows, D // H)] * H
            shapes = [out(shape, bf16) for shape in shapes]
            res = kernel(
                functools.partial(ring_kernel, self.load, self.split, self.t),
                [Far(o) for o in shapes],
                [Far(g) for g in self.sources[:2]]
                + list(self.sources[2:])
                + [Far(g) for g in self.got],
                second=place,
                scratch=[pltpu.VMEM((2, self.total, D), bf16), pltpu.VMEM((2, self.total, D), f32)]
                + vmem_of(self.got)
                + vmem_of(shapes),
                copies=20,
                deps=deps,
                vmem=56,
            )
            self.t += 1
            self.sent = res[0]
            if self.t == 5:
                return [self.across(p) for p in res]
            self.got = (pass_on(res[0], 1), pass_on(res[1], -1))

        def across(self, piece):
            bit = RING
            while bit < dp_count:
                piece = (piece.astype(f32) + flip_dp(piece, bit).astype(f32)).astype(bf16)
                bit *= 2
            return piece

        def gather(self, piece):
            self.parts = [[piece], [piece]]
            self.cuts = []
            self.pass_parts()

        def pass_parts(self):
            for way, parts in zip((1, -1), self.parts):
                value = parts[-1]
                if len(parts) == 4:
                    value = value[: self.split] if way == 1 else value[self.split :]
                    self.cuts.append(value)
                parts.append(pass_on(value, way))

        def result(self):
            fwd, bwd = self.parts
            return [fwd[0], *fwd[1:4], *bwd[1:4], fwd[4], bwd[4]]

    n2, hid, gp, cots = ffn[1][:4]
    grad_o = tn(hid, cots)
    grad_i = tn(n2, gp)
    ffn_ring = Ring(load_ffn_chunk, D // RING, 2 * D // RING, [grad_o, grad_i])
    ffn_ring.step()
    back = []

    branch = []

    def run_branch(m, deps=()):
        gate_m, att, rstd = saved[m][7], saved[m][9], ffn[m][5]
        from_far = [*gn2[m], ffn[1][3], ffn[m][4], w_out_heads]
        branch.append(
            kernel(
                functools.partial(branch_kernel, m),
                [
                    Far(joined),
                    out((8, D), f32),
                    out((own, D), f32),
                    out((length, LANE), bf16),
                    out((length, LANE), f32),
                ],
                [vec, rstd, gate_m, att] + [Far(a) for a in from_far],
                copies=10,
                vmem=56,
                deps=deps,
                scratch=vmem_of([*from_far[:4], wide, *from_far[5:], wide]),
                into={0: branch[0][0]} if m else None,
            )
        )

    def run_back(m, deps=()):
        x, n1, qc, qp, k, v, va, gate_m, prob, att, mix, stat = saved[m]
        from_far = [prob, v, k, qc, qp, va, wt, x]
        back.append(
            kernel(
                functools.partial(back_kernel, m),
                [
                    out((8, D), f32),
                    Far(out((micro * length, PACK), bf16)),
                    out((length, LANE), f32),
                    out((8, LANE), f32),
                    Far(out((2, own, D), bf16)),
                    Far(out((2, own, D), bf16)),
                ],
                [branch[m][3], branch[m][4], pos, gate_m, stat] + [Far(a) for a in from_far],
                copies=12,
                into={1: back[0][1]} if m else None,
                vmem=56,
                deps=deps,
                scratch=vmem_of(from_far)
                + [
                    pltpu.VMEM((length, PACK), bf16),
                    pltpu.VMEM((length, LANE), f32),
                    pltpu.VMEM((length, LANE), f32),
                    pltpu.VMEM((length, D), bf16),
                    pltpu.VMEM((2, own, D), bf16),
                    pltpu.VMEM((2, own, D), bf16),
                ],
            )
        )

    run_branch(0)
    ffn_ring.step()
    run_back(0)
    ffn_ring.step()
    run_branch(1)
    ffn_ring.step()
    grad_w = tn(saved[1][10], branch[1][0])
    run_back(1, deps=[grad_w])
    turned = lambda parts: [flip_shard(p, r) if r else p for r, p in enumerate(parts)]
    piece, *parts = ffn_ring.step()
    ffn_piece = jnp.concatenate([piece, *turned(parts)])
    gpos = (back[0][2] + back[1][2]).astype(bf16)
    grad_p = tn(gate(back[1][1], [piece]), saved[1][1])
    grad_p = lax.dynamic_update_slice(grad_p, tn(gpos, sine), (2 * LANE, 0))
    tails = kernel(
        vectors_kernel,
        [out((RING, TAIL, D), f32)],
        [branch[0][1], branch[1][1], back[0][0], back[1][0], back[0][3], back[1][3]]
        + [ffn[0][7], ffn[1][7]],
    )[0]
    pack_ring = Ring(
        load_pack_chunk, DH, D // RING + E * LANE // RING, [grad_p, grad_w, tails]
    )
    ffn_ring.gather(ffn_piece)
    pack_ring.step()
    add = lambda a, b: (a.astype(f32) + b.astype(f32)).astype(bf16)
    gx_got = [flip_shard(back[m][5], 1) for m in range(micro)]
    gx_far = jnp.stack([add(back[m][4][1], gx_got[m][1]) for m in range(micro)])
    gx_far = flip_shard(gx_far, 2)
    came = lambda i: [p[i] for p in ffn_ring.parts]
    both_ways = ffn_ring.parts
    both_ways[0][1] = gate(both_ways[0][1], [pack_ring.sent, both_ways[1][1]])
    ffn_ring.pass_parts()
    pack_ring.step()
    pack_ring.step(deps=came(2))
    ffn_ring.pass_parts()
    pack_ring.step()
    gx_all = kernel(
        input_kernel,
        [out((micro, 1, own, D), f32)],
        [x_own, vec, gx_far]
        + [a for m in range(micro) for a in (branch[m][2], back[m][4], gx_got[m])],
    )[0]
    ffn_ring.pass_parts()
    piece, *parts = pack_ring.step(deps=ffn_ring.cuts)
    parts = turned(parts)
    parts[1] = gate(parts[1], came(4))
    pack_piece = jnp.concatenate([jnp.concatenate(parts, axis=1), piece])
    pack_ring.gather(pack_piece)
    ways = pack_ring.parts
    sides = out((2, micro, own, D), bf16)
    keep, send = kernel(
        project_kernel,
        [Far(sides)] * 2,
        [Far(hid), Far(ffn_out)],
        scratch=vmem_of([joined, out((FF // H, D), bf16), joined, sides, sides]),
        copies=4,
        vmem=56,
        deps=[pack_piece],
    )
    ways[0][1] = gate(ways[0][1], [keep, ways[1][1]])
    got = flip_shard(gate(send, [ways[0][1]]), 1)
    far = flip_shard(add(keep[1], got[1]), 2)
    pack_ring.pass_parts()
    g_out, g_in, done = kernel(
        functools.partial(ffn_grads_kernel, ffn_ring.split),
        [Far(out((FF // H, D), f32)), Far(out((quarter, FF), f32)), out((8, LANE), f32)],
        [Far(p) for p in ffn_ring.result()],
        second=place,
        scratch=[
            pltpu.VMEM((RING, ffn_ring.total, D), bf16),
            pltpu.VMEM((FF // H, D), f32),
            pltpu.VMEM((quarter, FF), f32),
        ],
        copies=25,
        vmem=60,
        deps=[ways[0][1]],
    )
    ways[0][2] = gate(ways[0][2], [done, ways[1][2]])
    pack_ring.pass_parts()
    pack_ring.pass_parts()
    y_all = kernel(
        output_kernel,
        [Far(out((micro, 1, own, D), bf16)), out((8, LANE), f32)],
        [vec, keep, got, far] + [ffn[m][6] for m in range(micro)],
        scratch=[pltpu.VMEM((micro, 1, own, D), bf16)],
        copies=1,
    )[0]
    res = kernel(
        functools.partial(pack_grads_kernel, pack_ring.split),
        [
            out((H * DH, quarter), f32),
            out((H * E, quarter), f32),
            out((H * E, quarter), f32),
            out((H * DH, quarter), f32),
            out((H * DH, quarter), f32),
            out((H * E * DH, quarter), f32),
            out((E * DH, D), f32),
        ]
        + [out((quarter,), f32)] * 5
        + [out((DH,), f32)] * 2
        + [out((FF // H,), f32)],
        [Far(p) for p in pack_ring.result()],
        second=place,
        scratch=[
            pltpu.VMEM((RING, pack_ring.total, D), bf16),
            pltpu.VMEM((H, RING, LANE, quarter), f32),
        ],
        copies=9,
        vmem=40,
    )
    g_q, g_rv, g_ro, g_k, g_p, g_v, g_wo, g1, b1, g2, b2, bo, content, posb, bi = res
    return (
        y_all,
        gx_all,
        g1,
        b1,
        g_q.T,
        g_k.T,
        g_p.T,
        content,
        posb,
        g_rv.T,
        g_ro.T,
        g_v.T,
        g_wo,
        g2,
        b2,
        g_in,
        bi,
        g_out,
        bo,
    )


def solution(mesh):
    tokens = P(None, "dp", "shard")
    whole = P(None, "dp", "shard", None)
    routes = P(None, "dp", "shard", None, None)
    vector = P("shard")
    matrix = P("shard", None)
    weights = (
        vector,
        vector,
        matrix,
        matrix,
        matrix,
        vector,
        vector,
        matrix,
        matrix,
        matrix,
        matrix,
        vector,
        vector,
        matrix,
        vector,
        matrix,
        vector,
    )
    return jax.shard_map(
        local,
        mesh=mesh,
        in_specs=(whole, tokens, tokens, routes, routes) + weights + (whole,),
        out_specs=(whole, whole) + weights,
        check_vma=False,
    )
```

```python
import functools
import math

import jax
import jax.numpy as jnp
from jax import lax
from jax.experimental import pallas as pl
from jax.experimental.pallas import tpu as pltpu
from jax.sharding import PartitionSpec as P

D = 1024
H = 4
DH = 112
E = 5
FF = 4096
LANE = 128
PACK = 1024
BLK = 128
RING = 8
TAIL = 8
MASKED = -1e30
SCALE = DH ** (-0.5)
bf16 = jnp.bfloat16
f32 = jnp.float32
NN = (((1,), (0,)), ((), ()))
NT = (((1,), (1,)), ((), ()))
TN = (((0,), (0,)), ((), ()))


def mm(a, b, dims=NN):
    return lax.dot_general(a, b, dims, preferred_element_type=f32)


def call(kernel, outs, args, scratch=(), copies=0, flops=0, vmem=12, smem=2, deps=(), into=None):
    in_specs, arrays = [], []
    args = list(args)
    count = len(args)
    into = into or {}
    deps = [*deps, *into.values()]
    aliases = {count + len(deps) - len(into) + n: i for n, i in enumerate(into)}
    args += [Far(d, pl.ANY) for d in deps]
    body = lambda *refs: kernel(*refs[:count], *refs[count + len(deps) :])
    for i, arg in enumerate(args):
        far = isinstance(arg, Far)
        space = pltpu.SMEM if i < smem else arg.space if far else pltpu.VMEM
        in_specs.append(pl.BlockSpec(memory_space=space))
        arrays.append(arg.value if far else arg)
    out_specs, out_shapes = [], []
    for o in outs:
        far = isinstance(o, Far)
        out_specs.append(pl.BlockSpec(memory_space=o.space if far else pltpu.VMEM))
        out_shapes.append(o.value if far else o)
    moved = sum(math.prod(a.shape) * a.dtype.itemsize for a in arrays + out_shapes)
    scratch = list(scratch)
    if copies:
        scratch.append(pltpu.SemaphoreType.DMA((copies,)))
    return pl.pallas_call(
        body if deps else kernel,
        out_shape=out_shapes,
        in_specs=in_specs,
        out_specs=out_specs,
        scratch_shapes=scratch,
        compiler_params=pltpu.CompilerParams(vmem_limit_bytes=vmem << 20),
        input_output_aliases=aliases,
        cost_estimate=pl.CostEstimate(flops=0, bytes_accessed=0, transcendentals=0),
    )(*arrays)


class Far:
    def __init__(self, value, space=pltpu.HBM):
        self.value, self.space = value, space


class Copies:
    def __init__(self, sems):
        self.sems, self.count, self.left = sems, 0, []

    def start(self, src, dst):
        copy = pltpu.make_async_copy(src, dst, self.sems.at[self.count])
        self.count += 1
        copy.start()
        self.left.append(copy)
        return copy

    def wait(self, *copies):
        for copy in copies:
            copy.wait()
            self.left.remove(copy)

    def finish(self):
        self.wait(*list(self.left))


def gate(value, deps):
    return pl.pallas_call(
        lambda *refs: None,
        out_shape=jax.ShapeDtypeStruct(value.shape, value.dtype),
        in_specs=[pl.BlockSpec(memory_space=pl.ANY)] * (1 + len(deps)),
        out_specs=pl.BlockSpec(memory_space=pl.ANY),
        input_output_aliases={0: 0},
        cost_estimate=pl.CostEstimate(flops=0, bytes_accessed=0, transcendentals=0),
    )(value, *deps)


def out(shape, dtype):
    return jax.ShapeDtypeStruct(shape, dtype)


def prep_kernel(rank_ref, side_ref, *refs):
    count = 18
    (x_hbm, win_hbm), refs = refs[:2], refs[2:]
    ins, outs, scratch = refs[:count], refs[count : count + 6], refs[count + 6 :]
    (core_hbm, near2_hbm, near3_hbm, *x_outs), scratch = scratch[:5], scratch[5:]
    held, (marks_ref, pack_ref, sems) = scratch[:count], scratch[count:]
    copies = Copies(sems)
    loads = [copies.start(src, dst) for src, dst in zip(ins, held)]
    for m, ref in enumerate(x_outs):
        copies.start(x_hbm.at[m, 0], ref)
    width = win_hbm.shape[1] // H
    size = win_hbm.shape[0] // 2
    for r, ref in ((1, core_hbm), (2, near2_hbm), (3, near3_hbm)):
        cols = pl.ds(pl.multiple_of((rank_ref[0] ^ r) * width, width), width)
        rows = pl.ds(pl.multiple_of((side_ref[0] % 2) * size, size), size) if r > 1 else slice(0, 2 * size)
        copies.start(win_hbm.at[rows, cols], ref)
    copies.wait(*loads)
    q_ref, k_ref, p_ref, rv_ref, ro_ref, v_ref, routes_v_ref, routes_o_ref = held[:8]
    seg_ref, pad_ref, g1_ref, b1_ref, g2_ref, b2_ref, bo_ref, cb_ref, pb_ref, bi_ref = held[8:]
    head_ref, bin_ref = outs[4:]
    head_ref[...] = jnp.zeros(head_ref.shape, f32)
    head_ref[0:1, 0:DH] = cb_ref[...].astype(f32).reshape(1, -1)
    head_ref[1:2, 0:DH] = pb_ref[...].astype(f32).reshape(1, -1)
    bin_ref[...] = bi_ref[...].astype(f32).reshape(1, -1)
    micro, own = seg_ref.shape[0], seg_ref.shape[2]
    marks_ref[...] = jnp.zeros(marks_ref.shape, f32)
    copied = [slice(0, own), slice(own, 2 * own)]
    for m in range(micro):
        for cols in copied:
            marks_ref[4 * m + 2 : 4 * m + 3, cols] = seg_ref[m].astype(f32)
            marks_ref[4 * m + 3 : 4 * m + 4, cols] = pad_ref[m].astype(f32)
    for i, ref in enumerate((g1_ref, b1_ref, g2_ref, b2_ref, bo_ref)):
        marks_ref[4 * micro + i : 4 * micro + i + 1, :] = ref[...].astype(f32).reshape(1, -1)
    row = lax.broadcasted_iota(jnp.int32, (16, H * E), 0)
    col = lax.broadcasted_iota(jnp.int32, (16, H * E), 1)
    for r in range(H):
        out_ref = outs[r] if r < 2 else pack_ref
        h = rank_ref[0] ^ r
        rows = pl.ds(pl.multiple_of(h * DH, 16), DH)
        for m in range(micro):
            for i, ref in enumerate((routes_v_ref, routes_o_ref)):
                ones = lax.shift_left(jnp.ones((2, own), jnp.int32), ref[m, h])
                code = jnp.sum(ones.astype(f32), axis=0, keepdims=True)
                for cols in copied:
                    marks_ref[4 * m + i : 4 * m + i + 1, cols] = code
        pick_v = jnp.where((row < E) & (col == h * E + row), 1.0, 0.0).astype(bf16)
        pick_o = jnp.where((row >= E) & (row < 2 * E) & (col == h * E + row - E), 1.0, 0.0)
        routers = mm(pick_v, rv_ref[...]) + mm(pick_o.astype(bf16), ro_ref[...])
        out_ref[0:DH, :] = q_ref[rows, :]
        out_ref[DH:LANE, :] = routers.astype(bf16)
        out_ref[LANE : LANE + DH, :] = k_ref[rows, :]
        out_ref[LANE + DH : 2 * LANE, :] = marks_ref[...].astype(bf16)
        out_ref[2 * LANE : 2 * LANE + DH, :] = p_ref[rows, :]
        out_ref[2 * LANE + DH : 3 * LANE, :] = jnp.zeros((LANE - DH, out_ref.shape[1]), bf16)
        for e in range(E):
            at = (3 + e) * LANE
            expert = pl.ds(pl.multiple_of((h * E + e) * DH, 16), DH)
            out_ref[at : at + DH, :] = v_ref[expert, :]
            out_ref[at + DH : at + LANE, :] = jnp.zeros((LANE - DH, out_ref.shape[1]), bf16)
        if r >= 2:
            half = pl.ds(pl.multiple_of((side_ref[0] % 2) * LANE, LANE), LANE)
            outs[r][...] = pack_ref[:, half]
    copies.finish()


def norm_stats(x):
    mean = jnp.mean(x, axis=-1, keepdims=True)
    centred = x - mean
    var = jnp.mean(centred * centred, axis=-1, keepdims=True)
    rstd = lax.rsqrt(var + 1e-05)
    return centred * rstd, rstd


def norm_back(grad, unit, rstd, gain):
    g = grad * gain
    return rstd * (
        g
        - jnp.mean(g, axis=-1, keepdims=True)
        - unit * jnp.mean(g * unit, axis=-1, keepdims=True)
    )


def x_send_keep(held, x_hbm, send_hbm, keep_hbm):
    return held[0], held[1], x_hbm, send_hbm, keep_hbm


def attention_kernel(m, rank_ref, side_ref, *refs):
    first = m == 0
    (x0, x1, x2, x3), refs = refs[:4], refs[4:]
    head_ref, refs = refs[0], refs[1:]
    if first:
        (w0, w1, near2, near3, far2, far3, sine_hbm, wo_hbm), refs = refs[:8], refs[8:]
    else:
        (wt_hbm, wo_hbm, pos_ref, vec_ref, rows_ref), refs = refs[:5], refs[5:]
    (x_ref, n_hbm, qc_hbm, qp_hbm, k_hbm, v_hbm, va_hbm, gate_hbm, p_hbm, att_hbm), refs = (
        refs[:10],
        refs[10:],
    )
    (mix_hbm, stat_ref), refs = refs[:2], refs[2:]
    (send_ref, keep_ref), refs = refs[:2], refs[2:]
    if first:
        (wt_hbm, wop_hbm, pos_ref, vec_ref, rows_ref), refs = refs[:5], refs[5:]
    n_ref, qc_ref, qp_ref, k_ref, v_ref, va_ref, gate_ref, p_ref, att_ref, mix_ref = refs[:10]
    wt_ref, wo_ref, x_out, send_out, keep_out = x_send_keep(refs[10:15], x_ref, send_ref, keep_ref)
    x_ref, send_ref, keep_ref = refs[12:15]
    sine_ref = refs[15] if first else None
    copies = Copies(refs[-1])
    length = x_ref.shape[0]
    both = slice(m * length, (m + 1) * length)
    blocks = length // BLK
    rank = rank_ref[0]
    quarter = D // H

    def at(r, size):
        return pl.ds(pl.multiple_of((rank ^ r) * size, size), size)

    loads = [copies.start(x0.at[m], x_ref.at[at(0, BLK), :])]
    loads += [copies.start(ref, x_ref.at[at(r, BLK), :]) for r, ref in enumerate((x1, x2, x3), 1)]
    if first:
        side = side_ref[0] % 2
        for r, ref in enumerate((w0, w1)):
            loads.append(copies.start(ref, wt_ref.at[:, at(r, quarter)]))
        for r, place, ref in (
            (2, side, near2),
            (3, side, near3),
            (2, 1 - side, far2),
            (3, 1 - side, far3),
        ):
            cols = pl.ds(pl.multiple_of((rank ^ r) * quarter + place * LANE, LANE), LANE)
            loads.append(copies.start(ref, wt_ref.at[:, cols]))
        sine_load = copies.start(sine_hbm, sine_ref)
        wo_loads = []
        for e in range(E):
            rows = slice(e * LANE, e * LANE + DH)
            wo_loads.append(copies.start(wo_hbm.at[e * DH : (e + 1) * DH, :], wo_ref.at[rows, :]))
            wo_ref[e * LANE + DH : (e + 1) * LANE, :] = jnp.zeros((LANE - DH, D), bf16)
        copies.wait(*loads)
        vec_ref[...] = jnp.zeros(vec_ref.shape, f32)
        rows_ref[...] = jnp.zeros(rows_ref.shape, f32)
        for r in range(H):
            micro = rows_ref.shape[0]
            marks = wt_ref[LANE + DH : 2 * LANE, at(r, quarter)].astype(f32)
            vec_ref[0:5, at(r, quarter)] = marks[4 * micro : 4 * micro + 5, :]
            fresh = pl.ds(pl.multiple_of((rank ^ r) * quarter + side * LANE, LANE), LANE)
            marks = wt_ref[LANE + DH : 2 * LANE, fresh].astype(f32)
            for i in range(micro):
                part = marks[4 * i : 4 * i + 4, :]
                rows_ref[i, 0:1, at(r, BLK)] = part[0:1, :] + 2.0**E * part[1:2, :]
                rows_ref[i, 1:3, at(r, BLK)] = part[2:4, :]
        copies.start(wt_ref, wt_hbm)
    else:
        wt_load = copies.start(wt_hbm, wt_ref)
        wo_loads = [copies.start(wo_hbm, wo_ref)]
        copies.wait(*loads)

    @pl.loop(0, blocks)
    def _(b):
        rows = pl.ds(pl.multiple_of(b * BLK, BLK), BLK)
        x = x_ref[rows, :].astype(f32)
        unit, rstd = norm_stats(x)
        n_ref[rows, :] = (unit * vec_ref[0:1, :] + vec_ref[1:2, :]).astype(bf16)
        first_lane = lax.broadcasted_iota(jnp.int32, (BLK, LANE), 1) == 0
        stat_ref[rows, :] = jnp.where(first_lane, jnp.mean(x, axis=-1, keepdims=True), rstd)

    copies.start(x_ref, x_out)
    copies.start(n_ref, n_hbm.at[both, :])
    if first:
        copies.wait(sine_load)
        pos_ref[...] = mm(sine_ref[...], wt_ref[2 * LANE : 3 * LANE, :], NT).astype(bf16)
    else:
        copies.wait(wt_load)
    lane = lax.broadcasted_iota(jnp.int32, (1, LANE), 1)
    is_head = lane < DH
    raw_keys = mm(n_ref[...], wt_ref[0 : 2 * LANE, :], NT)
    raw = raw_keys[:, 0:LANE]
    columns = rows_ref[m].T
    code = jnp.broadcast_to(columns[:, 0:1].astype(jnp.int32), (length, LANE))
    slot = jnp.where((lane >= DH) & (lane < DH + 2 * E), lane - DH, 31)
    pick = (lax.shift_right_logical(code, jnp.broadcast_to(slot, (length, LANE))) & 1) == 1
    gate = jnp.where(pick, 1.0 / (1.0 + jnp.exp(-raw)), 0.0)
    gate_ref[...] = gate
    copies.start(gate_ref, gate_hbm)
    qc_ref[...] = jnp.where(is_head, (raw + head_ref[0:1, :]) * SCALE, 0.0).astype(bf16)
    qp_ref[...] = jnp.where(is_head, (raw + head_ref[1:2, :]) * SCALE, 0.0).astype(bf16)
    k_ref[...] = jnp.where(is_head, raw_keys[:, LANE : 2 * LANE], 0.0).astype(bf16)
    values = jnp.zeros((length, LANE), f32)
    for e in range(0, E, 2):
        last = min(e + 2, E)
        parts = mm(n_ref[...], wt_ref[(3 + e) * LANE : (3 + last) * LANE, :], NT)
        va_ref[:, e * LANE : last * LANE] = parts.astype(bf16)
        for i in range(e, last):
            part = parts[:, (i - e) * LANE : (i - e + 1) * LANE]
            values += part * gate[:, DH + i : DH + i + 1]
    v_ref[...] = values.astype(bf16)
    for src, dst in ((qc_ref, qc_hbm), (qp_ref, qp_hbm), (k_ref, k_hbm), (v_ref, v_hbm), (va_ref, va_hbm)):
        copies.start(src, dst)
    seg_col = columns[:, 1:2]
    for b in range(blocks):
        rows = slice(b * BLK, (b + 1) * BLK)
        wide = (b + 1) * BLK
        content = mm(qc_ref[rows, :], k_ref[0:wide, :], NT)
        table = mm(qp_ref[rows, :], pos_ref[length - wide : length, :], NT)
        table = pltpu.roll(table, (wide - BLK + 1) % wide, 1, stride=1, stride_axis=0)
        row = lax.broadcasted_iota(jnp.int32, (BLK, wide), 0) + b * BLK
        col = lax.broadcasted_iota(jnp.int32, (BLK, wide), 1)
        same = seg_col[rows, :] == rows_ref[m, 1:2, 0:wide]
        live = ((rows_ref[m, 2:3, 0:wide] > 0.0) & (col < row)) | (col == row)
        scores = jnp.where(same & live, content + table, MASKED)
        top = jnp.max(scores, axis=-1, keepdims=True)
        expo = jnp.exp(scores - top)
        prob = (expo / jnp.sum(expo, axis=-1, keepdims=True)).astype(bf16)
        p_ref[rows, 0:wide] = prob
        att = mm(prob, v_ref[0:wide, :])
        att_ref[rows, :] = att
        for e in range(E):
            share = gate_ref[rows, DH + E + e : DH + E + e + 1]
            mix_ref[rows, e * LANE : (e + 1) * LANE] = (att * share).astype(bf16)
        copies.start(p_ref.at[rows, 0:wide], p_hbm.at[rows, 0:wide])
    copies.start(att_ref, att_hbm)
    copies.start(mix_ref, mix_hbm.at[both, :])
    half = length // 2
    core = rank & 1
    copies.wait(*wo_loads)
    if first:
        copies.start(wo_ref, wop_hbm)
    for place, ref, dst in ((1 - core, send_ref, send_out), (core, keep_ref, keep_out)):
        rows = pl.ds(pl.multiple_of(place * half, half), half)
        ref[...] = mm(mix_ref[rows, :], wo_ref[...]).astype(bf16)
        copies.start(ref, dst)
    copies.finish()


def normal_terms(v):
    bell = jnp.exp(-0.5 * v * v)
    phi = 0.5 * (1.0 + lax.erf(v * (1.0 / math.sqrt(2.0))))
    return phi, bell * (1.0 / math.sqrt(2.0 * math.pi))


def pair_rows(core, b, refs):
    mine, far, mine2, far2 = refs
    own_half = (b // 2) == core
    rows = pl.ds(pl.multiple_of((b % 2) * BLK, BLK), BLK)
    near = mine[rows, :].astype(f32) + far[rows, :].astype(f32)
    away = mine2[rows, :].astype(f32) + far2[rows, :].astype(f32)
    return jnp.where(own_half, near, away)


def ffn_kernel(
    m,
    rank_ref,
    side_ref,
    x_hbm,
    a0,
    a1,
    a2,
    a3,
    vec_ref,
    bin_ref,
    win_hbm,
    win_core,
    *refs,
):
    (near2, near3, far2, far3), refs = refs[:4], refs[4:]
    (wout_hbm, c0, c1, c2, c3), refs = refs[:5], refs[5:]
    (n_hbm, hid_hbm, gp_hbm, cot_hbm, unit_hbm, rstd_ref, resid_ref, sum_ref), refs = (
        refs[:8],
        refs[8:],
    )
    (send_hbm, keep_hbm), refs = refs[:2], refs[2:]
    (unit_ref, win_ref, wout_ref, x_ref, n_ref, hid_ref, gp_ref, cot_ref), refs = refs[:8], refs[8:]
    halves, (send_ref, keep_ref, sems) = refs[:4], refs[4:]
    length = x_ref.shape[0]
    both = slice(m * length, (m + 1) * length)
    rank, place = rank_ref[0], side_ref[0]
    core = rank & 1
    copies = Copies(sems)
    size = D // H
    sum_ref[...] = jnp.zeros(sum_ref.shape, f32)

    def at(r, size):
        return pl.ds(pl.multiple_of((rank ^ r) * size, size), size)

    early = [copies.start(x_hbm, x_ref)]
    early += [copies.start(src, dst) for src, dst in zip((a0, a1, a2, a3), halves)]
    loads = []
    width = win_ref.shape[1]
    own_cols = pl.ds(pl.multiple_of(rank * width, width), width)
    loads.append(copies.start(win_hbm.at[:, own_cols], win_ref.at[at(0, size), :]))
    loads.append(copies.start(win_core, win_ref.at[at(1, size), :]))
    side = place % 2
    for r, half, ref in ((2, side, near2), (3, side, near3), (2, 1 - side, far2), (3, 1 - side, far3)):
        rows = pl.ds(pl.multiple_of((rank ^ r) * size + half * (size // 2), size // 2), size // 2)
        loads.append(copies.start(ref, win_ref.at[rows, :]))
    loads.append(copies.start(wout_hbm, wout_ref))
    for r, ref in enumerate((c0, c1, c2, c3)):
        loads.append(copies.start(ref.at[m], cot_ref.at[at(r, BLK), :]))

    copies.wait(*early)

    @pl.loop(0, length // BLK)
    def _(b):
        rows = pl.ds(pl.multiple_of(b * BLK, BLK), BLK)
        resid = x_ref[rows, :].astype(f32) + pair_rows(core, b, halves)
        unit, rstd = norm_stats(resid)
        unit_ref[rows, :] = unit.astype(bf16)
        rstd_ref[rows, :] = jnp.broadcast_to(rstd, (BLK, LANE))
        n_ref[rows, :] = (unit * vec_ref[2:3, :] + vec_ref[3:4, :]).astype(bf16)

        @pl.when(b == rank)
        def _():
            resid_ref[...] = resid

    copies.wait(*loads)
    for src, dst in (
        (unit_ref, unit_hbm),
        (n_ref, n_hbm.at[both, :]),
        (cot_ref, cot_hbm.at[both, :]),
    ):
        copies.start(src, dst)
    chunk = 1024

    @pl.loop(0, width // chunk)
    def _(c):
        cols = pl.ds(pl.multiple_of(c * chunk, chunk), chunk)
        pre = mm(n_ref[...], win_ref[:, cols]) + bin_ref[0:1, cols]
        back = mm(cot_ref[...], wout_ref[cols, :], NT)
        phi, density = normal_terms(pre)
        hid_ref[:, cols] = (pre * phi).astype(bf16)
        grad = (back * (phi + pre * density)).astype(bf16)
        gp_ref[:, cols] = grad
        sum_ref[0:1, cols] = jnp.sum(grad.astype(f32), axis=0, keepdims=True)

    copies.start(hid_ref, hid_hbm.at[both, :])
    copies.start(gp_ref, gp_hbm.at[both, :])
    half = length // 2
    for place, ref, dst in ((1 - core, send_ref, send_hbm), (core, keep_ref, keep_hbm)):
        rows = pl.ds(pl.multiple_of(place * half, half), half)
        ref[...] = mm(gp_ref[rows, :], win_ref[...], NT).astype(bf16)
        copies.start(ref, dst)
    copies.finish()


def split_blocks(rank, value_ref, keep_ref, send_ref):
    for r in range(H):
        rows = pl.ds(pl.multiple_of((rank ^ r) * BLK, BLK), BLK)
        (send_ref if r % 2 else keep_ref)[r // 2] = value_ref[rows, :]


def project_kernel(rank_ref, side_ref, hid_hbm, wout_hbm, keep_hbm, send_hbm, *refs):
    hid_ref, wout_ref, full_ref, keep_ref, send_ref, sems = refs
    copies = Copies(sems)
    loads = [copies.start(wout_hbm, wout_ref), copies.start(hid_hbm, hid_ref)]
    copies.wait(*loads)
    full_ref[...] = mm(hid_ref[...], wout_ref[...]).astype(bf16)
    micro = keep_ref.shape[1]
    length = full_ref.shape[0] // micro
    for m in range(micro):
        for r in range(H):
            at = pl.multiple_of((rank_ref[0] ^ r) * BLK + m * length, BLK)
            ref = send_ref if r % 2 else keep_ref
            ref[r // 2, m] = full_ref[pl.ds(at, BLK), :]
    copies.start(keep_ref, keep_hbm)
    copies.start(send_ref, send_hbm)
    copies.finish()


def branch_kernel(m, rank_ref, side_ref, vec_ref, rstd_ref, gate_ref, att_ref, *refs):
    hbm, refs = refs[:7], refs[7:]
    (gb_hbm, sums_ref, grad_ref, ga_ref, logit_ref), refs = refs[:5], refs[5:]
    held, (gb_ref, sems) = refs[:7], refs[7:]
    copies = Copies(sems)
    *halves, cot_ref, unit_ref, wo_ref = held
    length = unit_ref.shape[0]
    both = slice(m * length, (m + 1) * length)
    hbm = [*hbm[:4], hbm[4].at[both, :], *hbm[5:]]
    *loads, wo_load = [copies.start(src, dst) for src, dst in zip(hbm, held)]
    rank = rank_ref[0]
    core = rank & 1
    sums_ref[...] = jnp.zeros(sums_ref.shape, f32)
    copies.wait(*loads)

    @pl.loop(0, length // BLK)
    def _(b):
        rows = pl.ds(pl.multiple_of(b * BLK, BLK), BLK)
        unit = unit_ref[rows, :].astype(f32)
        grad = pair_rows(core, b, halves)
        sums_ref[0:1, :] += jnp.sum(grad * unit, axis=0, keepdims=True)
        sums_ref[1:2, :] += jnp.sum(grad, axis=0, keepdims=True)
        cot = cot_ref[rows, :].astype(f32)
        sums_ref[2:3, :] += jnp.sum(cot, axis=0, keepdims=True)
        total = cot + norm_back(grad, unit, rstd_ref[rows, 0:1], vec_ref[2:3, :])
        gb_ref[rows, :] = total.astype(bf16)

        @pl.when(b == rank)
        def _():
            grad_ref[...] = total

    copies.start(gb_ref, gb_hbm.at[both, :])
    copies.wait(wo_load)
    lane = lax.broadcasted_iota(jnp.int32, (1, LANE), 1)
    acc = jnp.zeros((length, LANE), f32)
    logits = jnp.zeros((length, LANE), f32)
    for first in range(0, E, 2):
        last = min(first + 2, E)
        both_mixed = mm(gb_ref[...], wo_ref[first * LANE : last * LANE, :], NT)
        for e in range(first, last):
            mixed = both_mixed[:, (e - first) * LANE : (e - first + 1) * LANE]
            acc += mixed * gate_ref[:, DH + E + e : DH + E + e + 1]
            dot = jnp.sum(mixed * att_ref[...], axis=-1, keepdims=True)
            logits = jnp.where(lane == DH + E + e, dot, logits)
    ga_ref[...] = acc.astype(bf16)
    logit_ref[...] = logits
    copies.finish()


def back_kernel(m, rank_ref, side_ref, ga_ref, logit_ref, pos_ref, gate_ref, stat_ref, *refs):
    hbm, refs = refs[:8], refs[8:]
    (sums_ref, dproj_hbm, gpos_ref, bias_ref, keep_hbm, send_hbm), refs = refs[:6], refs[6:]
    held, refs = refs[:8], refs[8:]
    dproj_ref, gk_ref, gv_ref, full_ref, keep_ref, send_ref, sems = refs
    copies = Copies(sems)
    *loads, va_load, wt_load, x_load = [copies.start(src, dst) for src, dst in zip(hbm, held)]
    p_ref, v_ref, k_ref, qc_ref, qp_ref, va_ref, wt_ref, x_ref = held
    length = x_ref.shape[0]
    blocks = length // BLK
    rank = rank_ref[0]
    lane = lax.broadcasted_iota(jnp.int32, (1, LANE), 1)
    sums_ref[...] = jnp.zeros(sums_ref.shape, f32)
    gk_ref[...] = jnp.zeros(gk_ref.shape, f32)
    gv_ref[...] = jnp.zeros(gv_ref.shape, f32)
    gpos_ref[...] = jnp.zeros(gpos_ref.shape, f32)
    row = lax.broadcasted_iota(jnp.int32, (BLK, BLK), 0)
    col = lax.broadcasted_iota(jnp.int32, (BLK, BLK), 1)
    mirror = jnp.where(row + col == BLK - 1, 1.0, 0.0).astype(bf16)
    cont_sum = jnp.zeros((1, LANE), f32)
    posn_sum = jnp.zeros((1, LANE), f32)
    copies.wait(*loads)
    for b in range(blocks):
        rows = slice(b * BLK, (b + 1) * BLK)
        wide = (b + 1) * BLK
        prob = p_ref[rows, 0:wide].astype(f32)
        ga = ga_ref[rows, :]
        grad_prob = mm(ga, v_ref[0:wide, :], NT)
        delta = jnp.sum(prob * grad_prob, axis=-1, keepdims=True)
        grad_score = (prob * (grad_prob - delta)).astype(bf16)
        gv_ref[0:wide, :] += mm(p_ref[rows, 0:wide], ga, TN)
        gk_ref[0:wide, :] += mm(grad_score, qc_ref[rows, :], TN)
        cont = mm(grad_score, k_ref[0:wide, :]) * SCALE
        table = pltpu.roll(mm(mirror, grad_score), 0, 1, stride=1, stride_axis=0)
        table = mm(mirror, table.astype(bf16)).astype(bf16)
        posn = mm(table, pos_ref[length - wide : length, :]) * SCALE
        gpos_ref[length - wide : length, :] += mm(table, qp_ref[rows, :], TN)
        cont_sum += jnp.sum(cont, axis=0, keepdims=True)
        posn_sum += jnp.sum(posn, axis=0, keepdims=True)
        dproj_ref[rows, 0:LANE] = (cont + posn).astype(bf16)
    bias_ref[...] = jnp.zeros(bias_ref.shape, f32)
    bias_ref[0:1, :] = cont_sum
    bias_ref[1:2, :] = posn_sum
    dproj_ref[:, LANE : 2 * LANE] = gk_ref[...].astype(bf16)
    dproj_ref[:, 2 * LANE : 3 * LANE] = jnp.zeros((length, LANE), bf16)
    copies.wait(va_load, wt_load, x_load)
    grad_values = gv_ref[...].astype(bf16).astype(f32)
    logits = logit_ref[...]
    for e in range(E):
        cols = slice((3 + e) * LANE, (4 + e) * LANE)
        dproj_ref[:, cols] = (grad_values * gate_ref[:, DH + e : DH + e + 1]).astype(bf16)
        dot = jnp.sum(grad_values * va_ref[:, e * LANE : (e + 1) * LANE].astype(f32), axis=-1, keepdims=True)
        logits = jnp.where(lane == DH + e, dot, logits)
    gate = gate_ref[...]
    logits = logits * gate * (1.0 - gate)
    dproj_ref[:, 0:LANE] = jnp.where(
        lane < DH, dproj_ref[:, 0:LANE].astype(f32), logits
    ).astype(bf16)
    copies.start(dproj_ref, dproj_hbm.at[m * length : (m + 1) * length, :])
    chunk = 1024
    mean, rstd = stat_ref[:, 0:1], stat_ref[:, 1:2]

    @pl.loop(0, D // chunk)
    def _(c):
        cols = pl.ds(pl.multiple_of(c * chunk, chunk), chunk)
        part = mm(dproj_ref[...], wt_ref[:, cols])
        full_ref[:, cols] = part.astype(bf16)
        unit = (x_ref[:, cols].astype(f32) - mean) * rstd
        sums_ref[3:4, cols] = jnp.sum(part * unit, axis=0, keepdims=True)
        sums_ref[4:5, cols] = jnp.sum(part, axis=0, keepdims=True)

    split_blocks(rank, full_ref, keep_ref, send_ref)
    copies.start(send_ref, send_hbm)
    copies.start(keep_ref, keep_hbm)
    copies.finish()


def output_kernel(rank_ref, side_ref, vec_ref, keep_ref, got_ref, far_ref, *refs):
    *refs, y_hbm, done_ref, y_ref, sems = refs
    done_ref[...] = jnp.zeros(done_ref.shape, f32)
    for m in range(y_ref.shape[0]):
        total = refs[m][...] + keep_ref[0, m].astype(f32) + got_ref[0, m].astype(f32)
        y_ref[m, 0] = (total + far_ref[m].astype(f32) + vec_ref[4:5, :]).astype(bf16)
    copies = Copies(sems)
    copies.start(y_ref, y_hbm)
    copies.finish()


def input_kernel(rank_ref, side_ref, x_ref, vec_ref, far_ref, *refs):
    y_ref = refs[-1]
    for m in range(y_ref.shape[0]):
        grad_ref, keep_ref, got_ref = refs[3 * m : 3 * m + 3]
        unit, rstd = norm_stats(x_ref[m].astype(f32))
        back = keep_ref[0].astype(f32) + got_ref[0].astype(f32) + far_ref[m].astype(f32)
        y_ref[m, 0] = grad_ref[...] + norm_back(back, unit, rstd, vec_ref[0:1, :])


def vectors_kernel(
    rank_ref, side_ref, sums0, sums1, norm0, norm1, bias0, bias1, hid0, hid1, y_ref
):
    y_ref[...] = jnp.zeros(y_ref.shape, f32)
    width = D // H
    own = pl.ds(pl.multiple_of(rank_ref[0] * width, width), width)
    y_ref[0, 6:7, :] = norm0[3:4, :] + norm1[3:4, :]
    y_ref[1, 6:7, :] = norm0[4:5, :] + norm1[4:5, :]
    for i in range(3):
        y_ref[i, 7:8, own] = sums0[i : i + 1, own] + sums1[i : i + 1, own]
    for i in range(2):
        cols = pl.ds(pl.multiple_of(rank_ref[0] * width + i * LANE, LANE), LANE)
        y_ref[3, 7:8, cols] = bias0[i : i + 1, :] + bias1[i : i + 1, :]
    for i in range(4):
        cols = slice(i * width, (i + 1) * width)
        y_ref[4 + i, 7:8, own] = hid0[0:1, cols] + hid1[0:1, cols]


def load_ffn_chunk(copies, c, sources, dst):
    grad_o, grad_i = sources
    rows = D // RING
    part = rows // H
    copies.start(grad_o.at[pl.ds(pl.multiple_of(c * rows, rows), rows), :], dst.at[0:rows, :])
    for s in range(H):
        src = pl.ds(pl.multiple_of(s * (D // H) + c * part, part), part)
        copies.start(grad_i.at[src, :], dst.at[rows + s * part : rows + (s + 1) * part, :])


def load_pack_chunk(copies, c, sources, dst):
    grad_p, grad_w = sources
    rows = D // RING
    part = E * LANE // RING
    copies.start(grad_p.at[pl.ds(pl.multiple_of(c * rows, rows), rows), :], dst.at[0:rows, :])
    copies.start(
        grad_w.at[pl.ds(pl.multiple_of(c * part, part), part), :], dst.at[rows : rows + part, :]
    )


def add_rows(total, rows, *terms):
    @pl.loop(0, (rows.stop - rows.start) // 16)
    def _(b):
        at = pl.ds(pl.multiple_of(rows.start + b * 16, 16), 16)
        part = pl.ds(pl.multiple_of(b * 16, 16), 16)
        value = total[at, :].astype(f32)
        for term in terms:
            value = value + term[part, :].astype(f32)
        total[at, :] = value.astype(bf16)


def ring_kernel(load, split, t, rank_ref, pos_ref, src0, src1, *refs):
    tail_ref, refs = (refs[0], refs[1:]) if load is load_pack_chunk else (None, refs)
    got_hbm, refs = (refs[:2], refs[2:]) if t else ((), refs)
    outs, refs = (refs[:2], refs[2:]) if t < 4 else (refs[: 1 + H], refs[1 + H :])
    loaded, *got, sems = refs
    copies = Copies(sems)
    pos, rank = pos_ref[0], rank_ref[0]
    total = loaded.shape[1]
    rows = D // RING
    chunks = [(pos + 4 - t) % RING, (pos + 4 + t) % RING][: 2 if t < 4 else 1]
    loads = []
    for i, c in enumerate(chunks):
        first = len(copies.left)
        load(copies, c, (src0, src1), loaded.at[i])
        if got_hbm:
            copies.start(got_hbm[i], got[i])
        if t == 4:
            copies.start(got_hbm[1], got[1])
        loads.append(copies.left[first:])
    for i, c in enumerate(chunks):
        copies.wait(*loads[i])
        if tail_ref is not None:
            last = slice(rows - TAIL, rows)
            loaded[i, last, :] = (loaded[i, last, :].astype(f32) + tail_ref[c]).astype(bf16)
        part = slice(0, split) if i == 0 else slice(split, total)
        if t == 0:
            copies.start(loaded.at[i, part, :], outs[i])
        elif t < 4:
            add_rows(loaded.at[i], part if t == 1 else slice(0, total), got[i])
            copies.start(loaded.at[i], outs[i])
        else:
            add_rows(loaded.at[i], slice(0, total), got[0], got[1])
            for r, dst in enumerate(outs[1:]):
                if tail_ref is None:
                    size = rows // H
                    at = pl.ds(pl.multiple_of(rows + (rank ^ r) * size, size), size)
                    copies.start(loaded.at[i, at, :], dst)
                else:
                    size = D // H
                    at = pl.ds(pl.multiple_of((rank ^ r) * size, size), size)
                    copies.start(loaded.at[i, 0:rows, at], dst)
            rest = slice(0, rows) if tail_ref is None else slice(rows, total)
            copies.start(loaded.at[i, rest, :], outs[0])
    copies.finish()


def load_ring(copies, pos, split, refs, dst):
    own, fwd, bwd, half_fwd, half_bwd = refs[0], refs[1:4], refs[4:7], refs[7], refs[8]
    copies.start(own, dst.at[pos])
    for i in range(3):
        copies.start(fwd[i], dst.at[(pos + RING - 1 - i) % RING])
        copies.start(bwd[i], dst.at[(pos + 1 + i) % RING])
    last = (pos + 4) % RING
    copies.start(half_fwd, dst.at[last, 0:split, :])
    copies.start(half_bwd, dst.at[last, split : dst.shape[1], :])
    copies.finish()


def ffn_grads_kernel(split, rank_ref, pos_ref, *refs):
    parts, (o_hbm, i_hbm, done_ref, held, o_ref, i_ref, sems) = refs[:9], refs[9:]
    done_ref[...] = jnp.zeros(done_ref.shape, f32)
    copies = Copies(sems)
    load_ring(copies, pos_ref[0], split, parts, held)
    rows = D // RING
    part = rows // H

    @pl.loop(0, RING)
    def _(c):
        o_ref[pl.ds(pl.multiple_of(c * rows, rows), rows), :] = held[c, 0:rows, :].astype(f32)
        i_rows = pl.ds(pl.multiple_of(c * part, part), part)
        for r in range(H):
            cols = pl.ds(pl.multiple_of((rank_ref[0] ^ r) * D, D), D)
            at = rows + r * part
            i_ref[i_rows, cols] = held[c, at : at + part, :].astype(f32)

    copies.start(o_ref, o_hbm)
    copies.start(i_ref, i_hbm)
    copies.finish()


def pack_grads_kernel(split, rank_ref, pos_ref, *refs):
    parts, refs = refs[:9], refs[9:]
    (q_ref, rv_ref, ro_ref, k_ref, p_ref, v_ref, w_ref), refs = refs[:7], refs[7:]
    (g1, b1, g2, b2, bo, content, posn, bin_ref), refs = refs[:8], refs[8:]
    held, heads, sems = refs
    copies = Copies(sems)
    load_ring(copies, pos_ref[0], split, parts, held)
    width = D // H
    rank = rank_ref[0]
    for r in range(H):
        heads[rank ^ r] = held[:, 0:LANE, r * width : (r + 1) * width].astype(f32)
    for h in range(H):
        rows = slice(h * DH, (h + 1) * DH)
        q_ref[rows, :] = heads[h, 0, 0:DH, :]
        rv_ref[h * E : (h + 1) * E, :] = heads[h, 0, DH : DH + E, :]
        ro_ref[h * E : (h + 1) * E, :] = heads[h, 0, DH + E : DH + 2 * E, :]
        k_ref[rows, :] = heads[h, 1, 0:DH, :]
        p_ref[rows, :] = heads[h, 2, 0:DH, :]
        for e in range(E):
            at = (h * E + e) * DH
            v_ref[at : at + DH, :] = heads[h, 3 + e, 0:DH, :]
    part = E * LANE // RING
    for c in range(RING):
        for e in range(E):
            low, high = max(c * part, e * LANE), min((c + 1) * part, e * LANE + DH)
            if low < high:
                at = low - e * LANE + e * DH
                w_ref[at : at + high - low, :] = held[
                    c, LANE + low - c * part : LANE + high - c * part, :
                ].astype(f32)
    last = slice(LANE - 1, LANE)
    before = slice(LANE - 2, LANE - 1)
    for ref, c in ((g1, 0), (b1, 1)):
        ref[...] = sum(heads[h, c, before, :] for h in range(H)).reshape(ref.shape)
    for c, ref in enumerate((g2, b2, bo)):
        ref[...] = heads[rank, c, last, :].reshape(ref.shape)
    row = heads[rank, 3, last, :]
    content[...] = row[:, 0:DH].reshape(content.shape)
    posn[...] = row[:, LANE : LANE + DH].reshape(posn.shape)
    for i in range(4):
        bin_ref[i * width : (i + 1) * width] = heads[rank, 4 + i, last, :].reshape((width,))


def flip_shard(value, bit):
    return lax.ppermute(value, "shard", [(s, s ^ bit) for s in range(H)])


def flip_dp(value, bit):
    count = lax.axis_size("dp")
    return lax.ppermute(value, "dp", [(d, d ^ bit) for d in range(count)])


def take(value, at, size, axis=0):
    return lax.dynamic_slice_in_dim(value, at, size, axis)


def put(value, part, at, axis=0):
    return lax.dynamic_update_slice_in_dim(value, part, at, axis)


def spread(own):
    across = flip_shard(own, 2)
    return own, flip_shard(own, 1), across, flip_shard(across, 1)


def ring_order():
    return list(range(0, RING, 2)) + list(range(RING - 1, 0, -2))


def pass_on(value, way):
    order, count = ring_order(), lax.axis_size("dp")
    pairs = [
        (base + order[i], base + order[(i + way) % RING])
        for base in range(0, count, RING)
        for i in range(RING)
    ]
    return lax.ppermute(value, "dp", pairs)


def swap_shard(value, rank, size, axis):
    parts = [take(value, (rank ^ r) * size, size, axis) for r in range(H)]
    return [flip_shard(p, r) if r else p for r, p in enumerate(parts)]


def sinusoid(length, feature_count):
    distance = (length - 1 - jnp.arange(length, dtype=jnp.int32)).astype(f32)
    inv_freq = jnp.exp(
        jnp.arange(0, feature_count, 2, dtype=jnp.int32).astype(f32)
        * (-math.log(10000.0) / feature_count)
    )
    angles = distance[:, None] * inv_freq[None, :]
    return jnp.concatenate([jnp.sin(angles), jnp.cos(angles)], axis=1)


def local(
    inputs,
    segments,
    padding,
    routes_value,
    routes_output,
    norm1_gain,
    norm1_bias,
    query_weight,
    key_weight,
    pos_weight,
    content_bias,
    pos_bias,
    value_router,
    output_router,
    value_experts,
    output_experts,
    norm2_gain,
    norm2_bias,
    ffn_in,
    ffn_in_bias,
    ffn_out,
    ffn_out_bias,
    cotangent,
):
    micro = inputs.shape[0]
    own = inputs.shape[2]
    length = own * H
    dp_count = lax.axis_size("dp")
    rank = lax.axis_index("shard")
    me = rank.astype(jnp.int32).reshape(1)
    dp_rank = lax.axis_index("dp")
    side = (dp_rank % RING).astype(jnp.int32).reshape(1)
    place = dp_rank % RING
    place = jnp.where(place % 2 == 0, place // 2, RING - 1 - place // 2)
    place = place.astype(jnp.int32).reshape(1)
    quarter = D // H

    token = [me]

    def after(value, *deps):
        return lax.optimization_barrier((value, *deps))[0]

    def step(fn, first, *rest):
        res = fn(after(first, token[0]), *rest)
        token[0] = jax.tree.leaves(res)[0]
        return res

    def kernel(fn, outs, args, second=side, **kwargs):
        deps = [*kwargs.pop("deps", ()), *([] if token[0] is me else [token[0]])]
        res = call(fn, outs, [me, second, *args], deps=deps, **kwargs)
        token[0] = min(res, key=lambda r: r.size)
        return res

    packs = kernel(
        prep_kernel,
        [out((PACK, quarter), bf16)] * 2
        + [out((PACK, LANE), bf16)] * 2
        + [out((8, LANE), f32), out((1, FF // H), f32)]
        + [out((quarter, FF // H), bf16)]
        + [out((quarter // 2, FF // H), bf16)] * 2
        + [out((own, D), bf16)] * micro,
        [
            Far(a)
            for a in (
                inputs,
                ffn_in,
                query_weight.T,
                key_weight.T,
                pos_weight.T,
                value_router.T,
                output_router.T,
                value_experts.T,
                routes_value[:, 0].transpose(0, 2, 3, 1),
                routes_output[:, 0].transpose(0, 2, 3, 1),
                segments,
                padding,
                norm1_gain,
                norm1_bias,
                norm2_gain,
                norm2_bias,
                ffn_out_bias,
                content_bias,
                pos_bias,
                ffn_in_bias,
            )
        ],
        scratch=[
            pltpu.VMEM(shape, dtype)
            for shape, dtype in [((H * DH, quarter), bf16)] * 3
            + [((H * E, quarter), bf16)] * 2
            + [((H * E * DH, quarter), bf16)]
            + [((micro, H, 2, own), jnp.int32)] * 2
            + [((micro, 1, own), jnp.int32)] * 2
            + [((quarter,), bf16)] * 5
            + [((DH,), bf16)] * 2
            + [((FF // H,), bf16)]
            + [((LANE - DH, quarter), f32), ((PACK, quarter), bf16)]
        ],
        copies=18 + 3 + micro,
        vmem=56,
    )
    sine = sinusoid(length, D).astype(bf16)
    head, b_in, core_in, *sent = packs[H:]
    sent_in, sent_x = sent[:2], sent[2:]
    near = [flip_shard(packs[r], r) for r in (2, 3)]
    w_core = flip_shard(packs[1], 1)
    far = [flip_dp(w, 1) for w in near]
    weights = [packs[0], w_core, *near, *far]
    x_own = inputs[:, 0]
    sent_x[0] = gate(sent_x[0], [*near, sine])
    x_parts = [spread(x) for x in sent_x]
    near_in = [flip_shard(w, r) for w, r in zip(sent_in, (2, 3))]
    w_in_core = flip_shard(core_in, 1)
    cot_parts = spread(cotangent[:, 0])

    def add_chip(keep, send):
        got = flip_shard(send, 1)
        add = lambda k, g: (k.astype(f32) + g.astype(f32)).astype(bf16)
        return step(add, keep, got)

    def finish_halves(chip):
        across = flip_shard(chip, 2)
        return chip, across, flip_shard(chip, 1), flip_shard(across, 1)

    half = out((length // 2, D), bf16)
    wide = out((length, D), bf16)
    saved_shapes = (
        [wide]
        + [out((length, LANE), bf16)] * 4
        + [
            out((length, E * LANE), bf16),
            out((length, LANE), f32),
            out((length, length), bf16),
            out((length, LANE), f32),
            out((length, E * LANE), bf16),
        ]
    )
    vmem_of = lambda shapes: [pltpu.VMEM(o.shape, o.dtype) for o in shapes]
    weight_shapes = [out((PACK, D), bf16), out((E * LANE, D), bf16)]
    joined = out((micro * length, D), bf16)
    saved = []
    residuals = []
    for m in range(micro):
        if m == 0:
            more = [Far(w) for w in weights] + [Far(sine), Far(output_experts)]
            extra = [Far(o) for o in weight_shapes]
            extra += [out((length, LANE), bf16), out((8, D), f32), out((micro, 8, length), f32)]
        else:
            more = [Far(wt), Far(w_out_heads), pos, vec, rows]
            extra = []
        res = kernel(
            functools.partial(attention_kernel, m),
            [Far(wide)]
            + [Far(joined)]
            + [Far(o) for o in saved_shapes[1:-1]]
            + [Far(out((micro * length, E * LANE), bf16))]
            + [out((length, LANE), f32), Far(half), Far(half)]
            + extra,
            [Far(x) for x in (x_own, *x_parts[m][1:])] + [head] + more,
            scratch=vmem_of(
                saved_shapes + weight_shapes + [wide, half, half] + ([wide] if m == 0 else [])
            ),
            copies=40,
            into={1: saved[0][1], 10: saved[0][10]} if m else None,
            deps=[*near_in, residuals[0][0]] if m else [],
            vmem=60,
            flops=2 * length * D * 1700,
        )
        saved.append(res[:12])
        if m == 0:
            near_in = [gate(w, [res[12]]) for w in near_in]
            far_in = [flip_dp(w, 1) for w in near_in]
        send, keep = res[12:14]
        if m == 0:
            wt, w_out_heads, pos, vec, rows = res[14:]
            send = gate(send, [*near_in, *x_parts[1][1:3]][: 4])
        else:
            send = gate(send, [*far_in, cot_parts[2], residuals[0][1]])
        residuals.append(finish_halves(add_chip(keep, send)))
    ffn = []
    gn2 = []
    for m in range(micro):
        res = kernel(
            functools.partial(ffn_kernel, m),
            [Far(joined)] * 4
            + [Far(wide)]
            + [
                out((length, LANE), f32),
                out((own, D), f32),
                out((8, FF // H), f32),
                Far(half),
                Far(half),
            ],
            [Far(a) for a in (saved[m][0], *residuals[m])]
            + [vec, b_in]
            + [Far(w) for w in (ffn_in, w_in_core, *near_in, *far_in, ffn_out, *cot_parts)],
            scratch=vmem_of(
                [wide, out((D, FF // H), bf16), out((FF // H, D), bf16)] + [wide] * 5 + [half] * 6
            ),
            copies=30,
            into={i: ffn[0][i] for i in range(4)} if m else None,
            vmem=60,
            deps=[residuals[1][0] if m == 0 else gn2[0][0]],
            flops=2 * length * D * D * 3,
        )
        ffn.append(res)
        gn2.append(finish_halves(add_chip(res[-1], res[-2])))

    def tn(a, b):
        return mm(a, b, TN).astype(bf16)

    class Ring:
        def __init__(self, load, split, total, sources):
            self.load, self.split, self.total = load, split, total
            self.sources, self.got, self.t = sources, (), 0

        def step(self, deps=()):
            rows = D // RING
            if self.t == 0:
                shapes = [(self.split, D), (self.total - self.split, D)]
            elif self.t < 4:
                shapes = [(self.total, D)] * 2
            elif len(self.sources) == 2:
                shapes = [(rows, D)] + [(rows // H, D)] * H
            else:
                shapes = [(self.total - rows, D)] + [(rows, D // H)] * H
            shapes = [out(shape, bf16) for shape in shapes]
            res = kernel(
                functools.partial(ring_kernel, self.load, self.split, self.t),
                [Far(o) for o in shapes],
                [Far(g) for g in self.sources[:2]]
                + list(self.sources[2:])
                + [Far(g) for g in self.got],
                second=place,
                scratch=[pltpu.VMEM((2, self.total, D), bf16)] + vmem_of(self.got),
                copies=20,
                deps=deps,
                vmem=56,
            )
            self.t += 1
            self.sent = res[0]
            if self.t == 5:
                return [self.across(p) for p in res]
            self.got = (pass_on(res[0], 1), pass_on(res[1], -1))

        def across(self, piece):
            bit = RING
            while bit < dp_count:
                piece = (piece.astype(f32) + flip_dp(piece, bit).astype(f32)).astype(bf16)
                bit *= 2
            return piece

        def gather(self, piece):
            self.parts = [[piece], [piece]]
            self.cuts = []
            self.pass_parts()

        def pass_parts(self):
            for way, parts in zip((1, -1), self.parts):
                value = parts[-1]
                if len(parts) == 4:
                    value = value[: self.split] if way == 1 else value[self.split :]
                    self.cuts.append(value)
                parts.append(pass_on(value, way))

        def result(self):
            fwd, bwd = self.parts
            return [fwd[0], *fwd[1:4], *bwd[1:4], fwd[4], bwd[4]]

    n2, hid, gp, cots = ffn[1][:4]
    grad_o = tn(hid, cots)
    grad_i = tn(n2, gp)
    ffn_ring = Ring(load_ffn_chunk, D // RING, 2 * D // RING, [grad_o, grad_i])
    ffn_ring.step()
    back = []

    branch = []

    def run_branch(m, deps=()):
        gate_m, att, rstd = saved[m][7], saved[m][9], ffn[m][5]
        from_far = [*gn2[m], ffn[1][3], ffn[m][4], w_out_heads]
        branch.append(
            kernel(
                functools.partial(branch_kernel, m),
                [
                    Far(joined),
                    out((8, D), f32),
                    out((own, D), f32),
                    out((length, LANE), bf16),
                    out((length, LANE), f32),
                ],
                [vec, rstd, gate_m, att] + [Far(a) for a in from_far],
                copies=10,
                vmem=56,
                deps=deps,
                scratch=vmem_of([*from_far[:4], wide, *from_far[5:], wide]),
                into={0: branch[0][0]} if m else None,
            )
        )

    def run_back(m, deps=()):
        x, n1, qc, qp, k, v, va, gate_m, prob, att, mix, stat = saved[m]
        from_far = [prob, v, k, qc, qp, va, wt, x]
        back.append(
            kernel(
                functools.partial(back_kernel, m),
                [
                    out((8, D), f32),
                    Far(out((micro * length, PACK), bf16)),
                    out((length, LANE), f32),
                    out((8, LANE), f32),
                    Far(out((2, own, D), bf16)),
                    Far(out((2, own, D), bf16)),
                ],
                [branch[m][3], branch[m][4], pos, gate_m, stat] + [Far(a) for a in from_far],
                copies=12,
                into={1: back[0][1]} if m else None,
                vmem=56,
                deps=deps,
                scratch=vmem_of(from_far)
                + [
                    pltpu.VMEM((length, PACK), bf16),
                    pltpu.VMEM((length, LANE), f32),
                    pltpu.VMEM((length, LANE), f32),
                    pltpu.VMEM((length, D), bf16),
                    pltpu.VMEM((2, own, D), bf16),
                    pltpu.VMEM((2, own, D), bf16),
                ],
            )
        )

    run_branch(0)
    ffn_ring.step()
    run_back(0)
    ffn_ring.step()
    run_branch(1)
    ffn_ring.step()
    grad_w = tn(saved[1][10], branch[1][0])
    run_back(1, deps=[grad_w])
    turned = lambda parts: [flip_shard(p, r) if r else p for r, p in enumerate(parts)]
    piece, *parts = ffn_ring.step()
    ffn_piece = jnp.concatenate([piece, *turned(parts)])
    gpos = (back[0][2] + back[1][2]).astype(bf16)
    grad_p = tn(gate(back[1][1], [piece]), saved[1][1])
    grad_p = lax.dynamic_update_slice(grad_p, tn(gpos, sine), (2 * LANE, 0))
    tails = kernel(
        vectors_kernel,
        [out((RING, TAIL, D), f32)],
        [branch[0][1], branch[1][1], back[0][0], back[1][0], back[0][3], back[1][3]]
        + [ffn[0][7], ffn[1][7]],
    )[0]
    pack_ring = Ring(
        load_pack_chunk, DH, D // RING + E * LANE // RING, [grad_p, grad_w, tails]
    )
    ffn_ring.gather(ffn_piece)
    pack_ring.step()
    add = lambda a, b: (a.astype(f32) + b.astype(f32)).astype(bf16)
    gx_got = [flip_shard(back[m][5], 1) for m in range(micro)]
    gx_far = jnp.stack([add(back[m][4][1], gx_got[m][1]) for m in range(micro)])
    gx_far = flip_shard(gx_far, 2)
    came = lambda i: [p[i] for p in ffn_ring.parts]
    both_ways = ffn_ring.parts
    both_ways[0][1] = gate(both_ways[0][1], [pack_ring.sent, both_ways[1][1]])
    ffn_ring.pass_parts()
    pack_ring.step()
    pack_ring.step(deps=came(2))
    ffn_ring.pass_parts()
    pack_ring.step()
    gx_all = kernel(
        input_kernel,
        [out((micro, 1, own, D), f32)],
        [x_own, vec, gx_far]
        + [a for m in range(micro) for a in (branch[m][2], back[m][4], gx_got[m])],
    )[0]
    ffn_ring.pass_parts()
    piece, *parts = pack_ring.step(deps=ffn_ring.cuts)
    parts = turned(parts)
    parts[1] = gate(parts[1], came(4))
    pack_piece = jnp.concatenate([jnp.concatenate(parts, axis=1), piece])
    pack_ring.gather(pack_piece)
    ways = pack_ring.parts
    sides = out((2, micro, own, D), bf16)
    keep, send = kernel(
        project_kernel,
        [Far(sides)] * 2,
        [Far(hid), Far(ffn_out)],
        scratch=vmem_of([joined, out((FF // H, D), bf16), joined, sides, sides]),
        copies=4,
        vmem=56,
        deps=[pack_piece],
    )
    ways[0][1] = gate(ways[0][1], [keep, ways[1][1]])
    got = flip_shard(gate(send, [ways[0][1]]), 1)
    far = flip_shard(add(keep[1], got[1]), 2)
    pack_ring.pass_parts()
    g_out, g_in, done = kernel(
        functools.partial(ffn_grads_kernel, ffn_ring.split),
        [Far(out((FF // H, D), f32)), Far(out((quarter, FF), f32)), out((8, LANE), f32)],
        [Far(p) for p in ffn_ring.result()],
        second=place,
        scratch=[
            pltpu.VMEM((RING, ffn_ring.total, D), bf16),
            pltpu.VMEM((FF // H, D), f32),
            pltpu.VMEM((quarter, FF), f32),
        ],
        copies=25,
        vmem=60,
        deps=[ways[0][1]],
    )
    ways[0][2] = gate(ways[0][2], [done, ways[1][2]])
    pack_ring.pass_parts()
    pack_ring.pass_parts()
    y_all = kernel(
        output_kernel,
        [Far(out((micro, 1, own, D), bf16)), out((8, LANE), f32)],
        [vec, keep, got, far] + [ffn[m][6] for m in range(micro)],
        scratch=[pltpu.VMEM((micro, 1, own, D), bf16)],
        copies=1,
    )[0]
    res = kernel(
        functools.partial(pack_grads_kernel, pack_ring.split),
        [
            out((H * DH, quarter), f32),
            out((H * E, quarter), f32),
            out((H * E, quarter), f32),
            out((H * DH, quarter), f32),
            out((H * DH, quarter), f32),
            out((H * E * DH, quarter), f32),
            out((E * DH, D), f32),
        ]
        + [out((quarter,), f32)] * 5
        + [out((DH,), f32)] * 2
        + [out((FF // H,), f32)],
        [Far(p) for p in pack_ring.result()],
        second=place,
        scratch=[
            pltpu.VMEM((RING, pack_ring.total, D), bf16),
            pltpu.VMEM((H, RING, LANE, quarter), f32),
        ],
        copies=9,
        vmem=40,
    )
    g_q, g_rv, g_ro, g_k, g_p, g_v, g_wo, g1, b1, g2, b2, bo, content, posb, bi = res
    return (
        y_all,
        gx_all,
        g1,
        b1,
        g_q.T,
        g_k.T,
        g_p.T,
        content,
        posb,
        g_rv.T,
        g_ro.T,
        g_v.T,
        g_wo,
        g2,
        b2,
        g_in,
        bi,
        g_out,
        bo,
    )


def solution(mesh):
    tokens = P(None, "dp", "shard")
    whole = P(None, "dp", "shard", None)
    routes = P(None, "dp", "shard", None, None)
    vector = P("shard")
    matrix = P("shard", None)
    weights = (
        vector,
        vector,
        matrix,
        matrix,
        matrix,
        vector,
        vector,
        matrix,
        matrix,
        matrix,
        matrix,
        vector,
        vector,
        matrix,
        vector,
        matrix,
        vector,
    )
    return jax.shard_map(
        local,
        mesh=mesh,
        in_specs=(whole, tokens, tokens, routes, routes) + weights + (whole,),
        out_specs=(whole, whole) + weights,
        check_vma=False,
    )
```
